32 devices in a mesh: dp: 8 (over y, x, core), tensor: 4 (over z).
Axes of the slice: x: 2, y: 2, z: 4, core: 2. Of those that a mesh axis runs over, the one named last changes fastest.
Arguments:
- tokens: bfloat16 [16384, 768], P(('dp', 'tensor')), may hold values from -6 to 6
- page_lengths: int32 [32], P('dp'), may hold values from 64 to 512, as said below
- w_query: bfloat16 [768, 768], P(None, 'tensor'), may hold values from -0.21875 to 0.21875
- b_query: bfloat16 [768], P('tensor'), may hold values from -1.796875 to 1.796875
- w_key: bfloat16 [768, 768], P(None, 'tensor'), may hold values from -0.21875 to 0.21875
- w_value: bfloat16 [768, 768], P(None, 'tensor'), may hold values from -0.21875 to 0.21875
- b_value: bfloat16 [768], P('tensor'), may hold values from -1.796875 to 1.796875
- w_out: bfloat16 [768, 768], P('tensor'), may hold values from -3.5 to 3.5
- b_out: bfloat16 [768], replicated, may hold values from -1.796875 to 1.796875
- ln1_gain: bfloat16 [768], replicated, may hold values from 0.099609375 to 1.8984375
- ln1_bias: bfloat16 [768], replicated, may hold values from -1.796875 to 1.796875
- w_up: bfloat16 [768, 3072], P(None, 'tensor'), may hold values from -0.21875 to 0.21875
- b_up: bfloat16 [3072], P('tensor'), may hold values from -3 to 3
- w_down: bfloat16 [3072, 768], P('tensor'), may hold values from -0.109375 to 0.109375
- b_down: bfloat16 [768], replicated, may hold values from -1.796875 to 1.796875
- ln2_gain: bfloat16 [768], replicated, may hold values from 0.099609375 to 1.8984375
- ln2_bias: bfloat16 [768], replicated, may hold values from -1.796875 to 1.796875
- cotangent: bfloat16 [16384, 768], P(('dp', 'tensor')), may hold values from -6 to 6
Outputs:
- output: bfloat16 [16384, 768], P(('dp', 'tensor'))
- grad_tokens: bfloat16 [16384, 768], P(('dp', 'tensor'))
- grad_w_query: float32 [768, 768], P(None, 'tensor')
- grad_b_query: float32 [768], P('tensor')
- grad_w_key: float32 [768, 768], P(None, 'tensor')
- grad_w_value: float32 [768, 768], P(None, 'tensor')
- grad_b_value: float32 [768], P('tensor')
- grad_w_out: float32 [768, 768], P('tensor')
- grad_b_out: float32 [768], replicated
- grad_ln1_gain: float32 [768], replicated
- grad_ln1_bias: float32 [768], replicated
- grad_w_up: float32 [768, 3072], P(None, 'tensor')
- grad_b_up: float32 [3072], P('tensor')
- grad_w_down: float32 [3072, 768], P('tensor')
- grad_b_down: float32 [768], replicated
- grad_ln2_gain: float32 [768], replicated
- grad_ln2_bias: float32 [768], replicated
The draws below stay inside these ranges and needn't reach their ends.
Inputs may be any that keep to these rules, and one draw needn't show every extreme that they name: `page_lengths`: the number of real tokens of page p; the keys of a page at positions from its length on are padding.
All inputs are finite; a program needn't handle non-finite values.
Results may differ from the reference program's by a relative error of at most 0.023.
Values may be sent and summed in bfloat16 or wider, within the bound.
No kernel may reach another device: no remote copies, remote signals or barrier semaphores. Data moves between devices by JAX's collectives and lax.ppermute only.
A program may use at most 128 MiB of HBM per device.

```python
import jax
import jax.numpy as jnp
from jax import lax

D = 768
HEADS = 12
HD = 64
FF = 3072
SEQ = 512
PAGES = 32
TOKENS = 16384


def draw_page_lengths(key, part):
    ticket = jax.random.randint(key, (PAGES,), 0, 1000)
    ladder = jnp.clip(ticket - 200, 0, 600)
    cubed_level = ladder * ladder * ladder // 1000
    shortfall = cubed_level * (SEQ - SEQ // 8) // 216000
    return (SEQ - shortfall).astype(jnp.int32)


def level_of(stream_key, shape, shards, smallest, largest):
    factor_of = 1.0
    for dim, shards_of in shards:
        steps = jax.random.uniform(jax.random.fold_in(jax.random.fold_in(stream_key, 6), dim), (shards_of,), jnp.float32, smallest / len(shards), largest / len(shards))
        factor_of = factor_of * jnp.repeat(jnp.exp(steps), shape[dim] // shards_of).reshape((-1,) + (1,) * (len(shape) - 1 - dim))
    return factor_of


def normal_values(key, extent, deviation, bound, split=(), dtype=jnp.bfloat16):
    drawn = jax.random.normal(key, extent, jnp.float32) * deviation
    if len(split) > 0:
        drawn = level_of(key, extent, split, -0.22, 0.18) * drawn
    return jnp.clip(drawn, min=-bound, max=bound).astype(dtype)


def setup_inputs(seed: int = 0) -> dict:
    arg_keys = jax.random.split(jax.random.key(seed), 19)
    return {
        "tokens": normal_values(arg_keys[0], (TOKENS, D), 1.0, 6.0, ((0, 32),)),
        "page_lengths": draw_page_lengths(jax.random.fold_in(arg_keys[18], 71), 0),
        "w_query": normal_values(arg_keys[2], (D, D), D ** -0.5, 0.21875, ((1, 4),)),
        "b_query": normal_values(arg_keys[3], (D,), 0.3, 1.796875, ((0, 4),)),
        "w_key": normal_values(arg_keys[4], (D, D), D ** -0.5, 0.21875, ((1, 4),)),
        "w_value": normal_values(arg_keys[5], (D, D), D ** -0.5, 0.21875, ((1, 4),)),
        "b_value": normal_values(arg_keys[6], (D,), 0.3, 1.796875, ((0, 4),)),
        "w_out": normal_values(arg_keys[7], (D, D), (max(D // 256, 1)) ** -0.5, 3.5, ((0, 4),)),
        "b_out": normal_values(arg_keys[8], (D,), 0.3, 1.796875),
        "ln1_gain": jnp.clip(1.0 + 0.18 * jax.random.normal(arg_keys[9], (D,), jnp.float32), 0.099609375, 1.8984375).astype(jnp.bfloat16),
        "ln1_bias": normal_values(arg_keys[10], (D,), 0.3, 1.796875),
        "w_up": normal_values(arg_keys[11], (D, FF), D ** -0.5, 0.21875, ((1, 4),)),
        "b_up": normal_values(arg_keys[12], (FF,), 0.5, 3.0, ((0, 4),)),
        "w_down": normal_values(arg_keys[13], (FF, D), FF ** -0.5, 0.109375, ((0, 4),)),
        "b_down": normal_values(arg_keys[14], (D,), 0.3, 1.796875),
        "ln2_gain": jnp.clip(1.0 + 0.18 * jax.random.normal(arg_keys[15], (D,), jnp.float32), 0.099609375, 1.8984375).astype(jnp.bfloat16),
        "ln2_bias": normal_values(arg_keys[16], (D,), 0.3, 1.796875),
        "cotangent": normal_values(arg_keys[17], (TOKENS, D), 1.0, 6.0, ((0, 32),)),
    }


epsilon = 1e-12
masked_score = -1000000000.0

@jax.custom_vjp
def low(v):
    return lax.optimization_barrier(v.astype(jnp.bfloat16)).astype(jnp.float32)

@jax.custom_vjp
def low_back(v):
    return v

def low_keep(v):
    return (low(v), None)

def low_pass(kept, grad):
    return (grad,)

def back_keep(v):
    return (v, None)

def back_low(kept, grad):
    return (low(grad),)
low.defvjp(low_keep, low_pass)
low_back.defvjp(back_keep, back_low)

def matmul(matrix_a, matrix_b):
    return jnp.dot(matrix_a, matrix_b, precision=lax.Precision.HIGHEST, preferred_element_type=jnp.float32)

def layer_norm(values, gain, shift):
    centred = values - lax.optimization_barrier(jnp.mean(values, axis=-1, keepdims=True))
    variance = lax.optimization_barrier(jnp.mean(centred * centred, axis=-1, keepdims=True))
    return centred * lax.rsqrt(variance + epsilon) * gain + shift

def encoder_layer(tokens, lengths, weights):
    w_query, b_query, w_key, w_value, b_value, w_out, b_out, ln1_gain, ln1_bias, w_up, b_up, w_down, b_down, ln2_gain, ln2_bias = weights
    page_count = lengths.shape[0]
    queries = low(low_back(matmul(tokens, w_query) + b_query))
    key_rows = low(low_back(matmul(tokens, w_key)))
    values = low(low_back(matmul(tokens, w_value) + b_value))
    head_split = (page_count, SEQ, HEADS, HD)
    scores = jnp.einsum('bqhd,bkhd->bhqk', queries.reshape(head_split), key_rows.reshape(head_split), precision=lax.Precision.HIGHEST) * HD ** (-0.5)
    scores = low_back(scores)
    key_mask = jnp.arange(SEQ)[None, :] < lengths[:, None]
    scores = jnp.where(key_mask[:, None, None, :], scores, masked_score)
    attn_probs = jax.nn.softmax(scores, axis=-1)
    context = jnp.einsum('bhqk,bkhd->bqhd', low(attn_probs), values.reshape(head_split), precision=lax.Precision.HIGHEST).reshape(tokens.shape)
    context = low(low_back(context))
    attended = low_back(matmul(context, w_out))
    normed = layer_norm(tokens + attended + b_out, ln1_gain, ln1_bias)
    preact = low_back(matmul(low(normed), w_up) + b_up)
    activated = low(jax.nn.gelu(preact, approximate=False))
    branch = low_back(matmul(activated, w_down))
    return layer_norm(normed + branch + b_down, ln2_gain, ln2_bias)

def reference(tokens, page_lengths, w_query, b_query, w_key, w_value, b_value, w_out, b_out, ln1_gain, ln1_bias, w_up, b_up, w_down, b_down, ln2_gain, ln2_bias, cotangent):
    params = tuple((array_in.astype(jnp.float32) for array_in in (w_query, b_query, w_key, w_value, b_value, w_out, b_out, ln1_gain, ln1_bias, w_up, b_up, w_down, b_down, ln2_gain, ln2_bias)))
    block_pages = 8
    blocks = PAGES // block_pages
    block_rows = block_pages * SEQ
    token_blocks = tokens.astype(jnp.float32).reshape(blocks, block_rows, D)
    length_blocks = page_lengths.reshape(blocks, block_pages)
    cot_blocks = cotangent.astype(jnp.float32).reshape(blocks, block_rows, D)

    def one_block(totals, block_item):
        block_tokens, block_lengths, block_cot = block_item

        def forward(inputs, weights):
            return encoder_layer(inputs, block_lengths, weights)
        result, backward = jax.vjp(forward, block_tokens, params)
        grad_in, grad_params = backward(block_cot)
        totals = jax.tree.map(lambda first_term, second_term: first_term + second_term, totals, grad_params)
        return (totals, (result, grad_in))
    zeros = jax.tree.map(jnp.zeros_like, params)
    totals, (results, grads_in) = lax.scan(one_block, zeros, (token_blocks, length_blocks, cot_blocks))
    output = results.reshape(TOKENS, D).astype(jnp.bfloat16)
    grad_tokens = grads_in.reshape(TOKENS, D).astype(jnp.bfloat16)
    return (output, grad_tokens, totals[0], totals[1], totals[2], totals[3], totals[4], totals[5], totals[6], totals[7], totals[8], totals[9], totals[10], totals[11], totals[12], totals[13], totals[14])
```

```python
from functools import partial

import jax
import jax.numpy as jnp
from jax import lax
from jax.sharding import PartitionSpec as P

HD = 64
SEQ = 512
GROUP = 8


epsilon = 1e-12
masked_score = -1000000000.0
low = jnp.bfloat16
wide = jnp.float32


def dot_of(spec, left, right):
    return jnp.einsum(spec, left, right, preferred_element_type=jnp.float32)


def norm_forward(values, gain, shift):
    centred = values - jnp.mean(values, axis=-1, keepdims=True)
    variance = jnp.mean(centred * centred, axis=-1, keepdims=True)
    inverse = lax.rsqrt(variance + epsilon)
    normal = centred * inverse
    return (normal * gain + shift, normal, inverse)


def norm_backward(grad_out, gain, normal, inverse):
    scaled = grad_out * gain
    return inverse * (
        scaled
        - jnp.mean(scaled, axis=-1, keepdims=True)
        - normal * jnp.mean(scaled * normal, axis=-1, keepdims=True)
    )


def swap(array, bit, size):
    return lax.ppermute(array, "dp", [(i, i ^ bit) for i in range(size)])


def shift(array, step, size):
    return lax.ppermute(array, "tensor", [(i, (i + step) % size) for i in range(size)])


def in_order(bit, mine, other, axis):
    return jnp.where(
        bit == 0,
        jnp.stack([mine, other], axis=axis),
        jnp.stack([other, mine], axis=axis),
    )


def gather_weights(own, extra, dp_size, parts):
    place = lax.axis_index("dp") % GROUP
    rows = own.shape[0] // GROUP
    piece = lax.dynamic_slice_in_dim(own, place * rows, rows, 0)
    if extra is not None:
        piece = jnp.concatenate([piece, extra], axis=0)
    arrived = jnp.stack([shift(piece, k, parts) for k in range(1, parts)])
    others = arrived[:, rows:]
    arrived = arrived[:, :rows]
    core, xbit, ybit = place & 1, (place >> 1) & 1, (place >> 2) & 1
    over_x = swap(arrived, 2, dp_size)
    over_y = swap(arrived, 4, dp_size)
    over_xy = swap(arrived, 6, dp_size)
    low_pair = in_order(xbit, arrived, over_x, 1)
    high_pair = in_order(xbit, over_y, over_xy, 1)
    plane = in_order(ybit, low_pair, high_pair, 1)
    mate = swap(plane, 1, dp_size)
    whole = in_order(core, plane, mate, 3)
    whole = whole.reshape(parts - 1, GROUP * rows, own.shape[1])
    return jnp.concatenate([own[None], whole], axis=0), others


def take(array, index, axis):
    return lax.dynamic_index_in_dim(array, index, axis, keepdims=False)


def reduce_shares(shares, dp_size, parts):
    place = lax.axis_index("dp") % GROUP
    core, xbit, ybit = place & 1, (place >> 1) & 1, (place >> 2) & 1
    rows, cols = shares.shape[1] // GROUP, shares.shape[2]
    split = shares.reshape(parts, 2, 2, 2, rows, cols)
    recv = swap(take(split, 1 - core, 3).astype(low), 1, dp_size)
    held = (take(split, core, 3).astype(wide) + recv.astype(wide)).astype(low)
    half = parts // 2
    first, second = held[:half], held[half:]
    recv_a = swap(take(first, 1 - xbit, 2), 2, dp_size)
    recv_b = swap(take(second, 1 - ybit, 1), 4, dp_size)
    first = (take(first, xbit, 2).astype(wide) + recv_a.astype(wide)).astype(low)
    second = (take(second, ybit, 1).astype(wide) + recv_b.astype(wide)).astype(low)
    recv_a = swap(take(first, 1 - ybit, 1), 4, dp_size)
    recv_b = swap(take(second, 1 - xbit, 1), 2, dp_size)
    first = (take(first, ybit, 1).astype(wide) + recv_a.astype(wide)).astype(low)
    second = (take(second, xbit, 1).astype(wide) + recv_b.astype(wide)).astype(low)
    held = [first[k] for k in range(half)] + [second[k] for k in range(parts - half)]
    total = held[0].astype(wide)
    for k in range(1, parts):
        total = total + shift(held[k], -k, parts).astype(wide)
    bit = GROUP
    while bit < dp_size:
        total = total + swap(total, bit, dp_size)
        bit *= 2
    total = total.astype(low)
    over_x = swap(total, 2, dp_size)
    over_y = swap(total, 4, dp_size)
    over_xy = swap(total, 6, dp_size)
    low_pair = in_order(xbit, total, over_x, 0)
    high_pair = in_order(xbit, over_y, over_xy, 0)
    plane = in_order(ybit, low_pair, high_pair, 0)
    mate = swap(plane, 1, dp_size)
    whole = in_order(core, plane, mate, 2)
    return whole.reshape(GROUP * rows, cols).astype(wide)


def sum_everywhere(array, dp_size, parts):
    bit = 1
    while bit < dp_size:
        array = array + swap(array, bit, dp_size)
        bit *= 2
    bit = 1
    while bit < parts:
        array = array + lax.ppermute(array, "tensor", [(i, i ^ bit) for i in range(parts)])
        bit *= 2
    return array


def per_device(
    dp_size,
    parts,
    tokens,
    page_lengths,
    w_query,
    b_query,
    w_key,
    w_value,
    b_value,
    w_out,
    b_out,
    ln1_gain,
    ln1_bias,
    w_up,
    b_up,
    w_down,
    b_down,
    ln2_gain,
    ln2_bias,
    cotangent,
):
    me = lax.axis_index("tensor")
    width = tokens.shape[1]
    local = w_query.shape[1]
    heads = local // HD
    pages = tokens.shape[0] // SEQ
    length = lax.dynamic_slice_in_dim(page_lengths, me * pages, pages, 0)
    biases = jnp.concatenate([b_query, b_value, b_up]).reshape(-1, local)
    biases = jnp.pad(biases.reshape(-1), (0, 16 * width - biases.size)).reshape(16, width)
    attn_own = jnp.concatenate([w_query.T, w_key.T, w_value.T, w_out], axis=0)
    attn_w, others = gather_weights(attn_own, biases, dp_size, parts)
    up_w, _ = gather_weights(w_up, None, dp_size, parts)
    down_w, _ = gather_weights(w_down, None, dp_size, parts)
    biases = jnp.concatenate([biases[None], others], axis=0).reshape(parts, -1)
    bias_q = biases[:, :local].astype(wide)
    bias_v = biases[:, local : 2 * local].astype(wide)
    bias_up = biases[:, 2 * local : 2 * local + width].astype(wide)

    joint_w = attn_w[:, : 3 * local]
    out_w = attn_w[:, 3 * local :]
    projected = dot_of("md,kfd->kmf", tokens, joint_w)
    head_split = (parts, pages, SEQ, heads, HD)
    queries = (projected[:, :, :local] + bias_q[:, None]).astype(low).reshape(head_split)
    key_rows = projected[:, :, local : 2 * local].astype(low).reshape(head_split)
    values = (projected[:, :, 2 * local :] + bias_v[:, None]).astype(low).reshape(head_split)
    key_mask = jnp.arange(SEQ)[None, :] < length[:, None]
    scores = dot_of("kpqhd,kpshd->kphqs", queries, key_rows) * HD ** (-0.5)
    scores = jnp.where(key_mask[None, :, None, None, :], scores, masked_score)
    row_top = jnp.max(scores, axis=-1, keepdims=True)
    log_norm = row_top + jnp.log(jnp.sum(jnp.exp(scores - row_top), axis=-1, keepdims=True))
    probs = jnp.exp(scores - log_norm)
    context = dot_of("kphqs,kpshd->kpqhd", probs.astype(low), values).astype(low)
    context = context.reshape(parts, pages * SEQ, local)
    attended = dot_of("kmf,kfd->md", context, out_w)
    gain_one = ln1_gain.astype(wide)
    normed, normal_one, inverse_one = norm_forward(
        tokens.astype(wide) + attended + b_out.astype(wide), gain_one, ln1_bias.astype(wide)
    )
    normed_low = normed.astype(low)
    preact = dot_of("md,kdf->kmf", normed_low, up_w) + bias_up[:, None]
    gelu_value, gelu_back = jax.vjp(partial(jax.nn.gelu, approximate=False), preact)
    activated = gelu_value.astype(low)
    branch = dot_of("kmf,kfd->md", activated, down_w)
    gain_two = ln2_gain.astype(wide)
    output_value, normal_two, inverse_two = norm_forward(
        normed + branch + b_down.astype(wide), gain_two, ln2_bias.astype(wide)
    )
    grad_out = cotangent.astype(wide)
    grad_gain_two = jnp.sum(grad_out * normal_two, axis=0)
    grad_bias_two = jnp.sum(grad_out, axis=0)
    grad_branch = norm_backward(grad_out, gain_two, normal_two, inverse_two)
    grad_b_down = jnp.sum(grad_branch, axis=0)
    branch_low = grad_branch.astype(low)
    grad_w_down = dot_of("kmf,md->kfd", activated, branch_low).astype(low)
    grad_act = dot_of("md,kfd->kmf", branch_low, down_w)
    grad_preact = gelu_back(grad_act)[0].astype(low)
    grad_w_up = dot_of("md,kmf->kdf", normed_low, grad_preact).astype(low)
    grad_b_up = jnp.sum(grad_preact.astype(wide), axis=1)
    grad_normed = grad_branch + dot_of("kmf,kdf->md", grad_preact, up_w)
    ffn = jnp.concatenate([grad_w_down, grad_w_up], axis=2)
    ffn_sum = reduce_shares(ffn, dp_size, parts)
    grad_gain_one = jnp.sum(grad_normed * normal_one, axis=0)
    grad_bias_one = jnp.sum(grad_normed, axis=0)
    grad_residual = norm_backward(grad_normed, gain_one, normal_one, inverse_one)
    grad_b_out = jnp.sum(grad_residual, axis=0)
    residual_low = grad_residual.astype(low)
    grad_w_out = dot_of("kmf,md->kfd", context, residual_low)
    grad_context = dot_of("md,kfd->kmf", residual_low, out_w).astype(low).reshape(head_split)

    grad_values = dot_of("kphqs,kpqhd->kpshd", probs.astype(low), grad_context).astype(low)
    grad_probs = dot_of("kpqhd,kpshd->kphqs", grad_context, values)
    grad_scores = (
        probs * (grad_probs - jnp.sum(probs * grad_probs, axis=-1, keepdims=True))
    ).astype(low)
    scale = HD ** (-0.5)
    grad_queries = (dot_of("kphqs,kpshd->kpqhd", grad_scores, key_rows) * scale).astype(low)
    grad_keys = (dot_of("kphqs,kpqhd->kpshd", grad_scores, queries) * scale).astype(low)
    flat = (parts, pages * SEQ, local)
    grad_queries, grad_keys, grad_values = (
        array.reshape(flat) for array in (grad_queries, grad_keys, grad_values)
    )
    grad_joint = jnp.concatenate([grad_queries, grad_keys, grad_values], axis=2)
    grad_w_joint = dot_of("kmf,md->kfd", grad_joint, tokens)
    attn = jnp.concatenate([grad_w_joint, grad_w_out], axis=1).astype(low)
    attn_sum = reduce_shares(attn, dp_size, parts)
    grad_tokens = (grad_residual + dot_of("kmf,kfd->md", grad_joint, joint_w)).astype(low)

    def absolute(array):
        return jnp.take(array, (me - jnp.arange(parts)) % parts, axis=0).reshape(-1)

    small = [
        grad_b_out,
        grad_gain_one,
        grad_bias_one,
        grad_b_down,
        grad_gain_two,
        grad_bias_two,
        absolute(jnp.sum(grad_queries.astype(wide), axis=1)),
        absolute(jnp.sum(grad_values.astype(wide), axis=1)),
        absolute(grad_b_up),
    ]
    sizes = [piece.shape[0] for piece in small]
    packed = jnp.concatenate(small).reshape(-1, width)
    packed = sum_everywhere(packed, dp_size, parts).reshape(-1)
    pieces = []
    start = 0
    for size in sizes:
        pieces.append(packed[start : start + size])
        start += size

    def own_part(array):
        return take(array.reshape(parts, -1), me, 0)

    return (
        output_value.astype(low),
        grad_tokens,
        attn_sum[:local].T,
        own_part(pieces[6]),
        attn_sum[local : 2 * local].T,
        attn_sum[2 * local : 3 * local].T,
        own_part(pieces[7]),
        attn_sum[3 * local :],
        pieces[0],
        pieces[1],
        pieces[2],
        ffn_sum[:, width:],
        own_part(pieces[8]),
        ffn_sum[:, :width],
        pieces[3],
        pieces[4],
        pieces[5],
    )


def solution(mesh):
    columns, rows, both = P(None, "tensor"), P("tensor", None), P(("dp", "tensor"), None)
    share = P("tensor")
    return jax.shard_map(
        partial(per_device, mesh.shape["dp"], mesh.shape["tensor"]),
        mesh=mesh,
        in_specs=(
            both,
            P("dp"),
            columns,
            share,
            columns,
            columns,
            share,
            rows,
            P(),
            P(),
            P(),
            columns,
            share,
            rows,
            P(),
            P(),
            P(),
            both,
        ),
        out_specs=(
            both,
            both,
            columns,
            share,
            columns,
            columns,
            share,
            rows,
            P(),
            P(),
            P(),
            columns,
            share,
            rows,
            P(),
            P(),
            P(),
        ),
        check_vma=False,
    )
```

```python
from functools import partial

import jax
import jax.numpy as jnp
from jax import lax
from jax.experimental import pallas as pl
from jax.experimental.pallas import tpu as pltpu
from jax.sharding import PartitionSpec as P

HD = 64
SEQ = 512
GROUP = 8
LOG2E = 1.4426950408889634
TAIL_P = 0.39
TAIL = (
    0.23532521908406087,
    0.09138841455460205,
    0.6495593986198918,
    -0.6354002786931026,
    0.8866643698688825,
    -0.22753712513305413,
)

epsilon = 1e-12
masked_score = -1000000000.0
low = jnp.bfloat16
wide = jnp.float32
PEAK = 1.1e15


def mm(left, right, left_dim, right_dim):
    return lax.dot_general(
        left, right, (((left_dim,), (right_dim,)), ((), ())), preferred_element_type=wide
    )


def vmem():
    return pl.BlockSpec(memory_space=pltpu.VMEM)


def smem():
    return pl.BlockSpec(memory_space=pltpu.SMEM)


def hbm():
    return pl.BlockSpec(memory_space=pl.ANY)


def cost(microseconds):
    return pl.CostEstimate(
        flops=int(microseconds * 1e-6 * PEAK), bytes_accessed=1 << 20, transcendentals=0
    )


def params(mebibytes):
    return pltpu.CompilerParams(vmem_limit_bytes=mebibytes << 20)


def block(shape, index):
    return pl.BlockSpec(shape, lambda i: index)


def shaped(shape, dtype):
    return jax.ShapeDtypeStruct(shape, dtype)


def masked_pad(length, seq):
    row = lax.broadcasted_iota(jnp.int32, (16, seq), 0)
    key = lax.broadcasted_iota(jnp.int32, (16, seq), 1)
    bias = jnp.where((row == 0) & (key >= length), masked_score, 0.0).astype(low)
    ones = jnp.where(row == 0, 1.0, 0.0).astype(low)
    return bias, ones


def as_column(row, ones):
    first = lax.broadcasted_iota(jnp.int32, (16, row.shape[1]), 0) == 0
    return mm(jnp.where(first, row, 0.0).astype(low), ones, 0, 0)


def group_forward(tokens, weights, bias, length, qkv_ref, ctx_ref, lse_ref):
    local = weights.shape[0] // 4
    seq = tokens.shape[0]
    scale = HD**-0.5 * LOG2E
    key_pad, ones = masked_pad(length, seq)
    joint = mm(weights[: 3 * local], tokens, 1, 1)
    query = (joint[:local] + as_column(bias[:, :local], ones)).astype(low)
    key = joint[local : 2 * local].astype(low)
    value = (joint[2 * local :] + as_column(bias[:, local : 2 * local], ones)).astype(low)
    qkv_ref[:local] = query
    qkv_ref[local : 2 * local] = key
    qkv_ref[2 * local :] = value
    for h in range(local // HD):
        part = slice(h * HD, (h + 1) * HD)
        scores = mm(
            jnp.concatenate([key[part], key_pad], 0), jnp.concatenate([query[part], ones], 0), 0, 0
        )
        top = jnp.max(scores, axis=0, keepdims=True)
        probs = jnp.exp2((scores - top) * scale)
        total = jnp.sum(probs, axis=0, keepdims=True)
        context = mm(value[part], probs.astype(low), 1, 0)
        ctx_ref[part] = (context * (1.0 / total)).astype(low)
        lse_ref[h : h + 1] = top * scale + jnp.log2(total)


def gelu_parts(x):
    t = 1.0 / (1.0 + (TAIL_P * 0.5**0.5) * jnp.abs(x))
    poly = TAIL[-1]
    for factor in TAIL[-2::-1]:
        poly = poly * t + factor
    bell = jnp.exp2(x * x * (-0.5 * LOG2E))
    half = 0.5 * poly * t * bell
    cdf = jnp.where(x >= 0, 1.0 - half, half)
    return x * cdf, cdf + x * bell * (0.5 / jnp.pi) ** 0.5


def norm_parts(values):
    centred = values - jnp.mean(values, axis=1, keepdims=True)
    inverse = lax.rsqrt(jnp.mean(centred * centred, axis=1, keepdims=True) + epsilon)
    return centred * inverse, inverse


def norm_back(scaled, normal, inverse):
    return inverse * (
        scaled
        - jnp.mean(scaled, axis=1, keepdims=True)
        - normal * jnp.mean(scaled * normal, axis=1, keepdims=True)
    )


def piece_copies(info, refs, target, sems):
    copies = []
    for s in range(2):
        first, second, third = refs[3 * s : 3 * s + 3]
        holder = info[1] ^ s
        order = (1 + holder, 2 - holder, 3)
        views = (first, second, third.at[0], third.at[1])
        for view, move in zip(views, (0,) + order):
            rows = view.shape[1]
            start = pl.multiple_of((holder * 4 + (info[2] ^ move)) * rows, rows)
            for entry, k in enumerate(order):
                copies.append(
                    pltpu.make_async_copy(
                        view.at[entry],
                        target.at[k, pl.ds(start, rows), :],
                        sems.at[len(copies)],
                    )
                )
    return copies


def place_pieces(info, value, keep_ref, send_ref, entry):
    rows = value.shape[0] // GROUP
    for p in range(GROUP):
        half, move = p >> 2, (p & 3) ^ info[2]
        a, b = (move >> 1, move & 1) if half else (move & 1, move >> 1)
        piece = value[p * rows : (p + 1) * rows].astype(low)

        @pl.when(info[1] == half)
        def _():
            keep_ref[(a, b) + entry] = piece

        @pl.when(info[1] != half)
        def _():
            send_ref[(a, b) + entry] = piece


def start_all(copies):
    for copy in copies:
        copy.start()


def wait_all(copies):
    for copy in copies:
        copy.wait()


def attn_own_kernel(info, tokens, weights, bias, qkv, ctx, lse):
    group_forward(tokens[...], weights[...], bias[0], info[0], qkv.at[0], ctx.at[0], lse.at[0])


def attn_own(info, tokens, weights, bias):
    local, seq = weights.shape[0] // 4, tokens.shape[0]
    return pl.pallas_call(
        attn_own_kernel,
        in_specs=[smem()] + [vmem()] * 3,
        out_specs=[vmem()] * 3,
        out_shape=[
            shaped((1, 3 * local, seq), low),
            shaped((1, local, seq), low),
            shaped((1, 8, seq), wide),
        ],
        compiler_params=params(24),
        cost_estimate=cost(4),
        name="attn_own",
    )(info, tokens, weights, bias)


def attn_rest_kernel(info, tokens, bias, *refs):
    qkv, ctx, lse, whole, weights, sems, keep_sem = refs[6:]
    parts = weights.shape[0]
    copies = piece_copies(info, refs[:6], weights, sems)
    start_all(copies)
    wait_all(copies)
    keep = pltpu.make_async_copy(weights.at[pl.ds(1, parts - 1)], whole, keep_sem.at[0])
    keep.start()

    def group(k, _):
        out = k - 1
        group_forward(
            tokens[...], weights[k], bias[k], info[0], qkv.at[out], ctx.at[out], lse.at[out]
        )
        return 0

    lax.fori_loop(1, parts, group, 0)
    keep.wait()


def attn_rest(info, tokens, bias, pieces):
    others, rows, cols = pieces[0].shape
    size, seq = rows * GROUP, tokens.shape[0]
    local = size // 4
    return pl.pallas_call(
        attn_rest_kernel,
        in_specs=[smem()] + [vmem()] * 2 + [hbm()] * 6,
        out_specs=[vmem()] * 3 + [hbm()],
        out_shape=[
            shaped((others, 3 * local, seq), low),
            shaped((others, local, seq), low),
            shaped((others, 8, seq), wide),
            shaped((others, size, cols), low),
        ],
        scratch_shapes=[
            pltpu.VMEM((others + 1, size, cols), low),
            pltpu.SemaphoreType.DMA((GROUP * others,)),
            pltpu.SemaphoreType.DMA((1,)),
        ],
        compiler_params=params(32),
        cost_estimate=cost(11),
        name="attn_rest",
    )(info, tokens, bias, *pieces)


def ffn_up_kernel(info, tokens, ctx_own, ctx_rest, bias, vec, out_own, out_rest, up_own, *refs):
    act, slope, skip, normed_ref, hat_ref, inv_ref, whole, out_w, up, sems, own_sems = refs[6:]
    parts, size = up.shape[0], up.shape[1]
    local = size // 4
    tail = pl.ds(3 * local, local)
    out_copies = [pltpu.make_async_copy(out_own.at[tail], out_w.at[0], own_sems.at[1])]
    for k in range(1, parts):
        out_copies.append(
            pltpu.make_async_copy(out_rest.at[k - 1, tail], out_w.at[k], own_sems.at[1 + k])
        )
    start_all(out_copies)
    copies = piece_copies(info, refs[:6], up, sems)
    copies.append(pltpu.make_async_copy(up_own, up.at[0], own_sems.at[0]))
    start_all(copies)
    rows = vec[...]
    b_out, gain_one, bias_one, b_down = (rows[i : i + 1] for i in range(4))
    wait_all(out_copies)
    attended = mm(ctx_own[0], out_w[0], 0, 0)
    for k in range(1, parts):
        attended = attended + mm(ctx_rest[k - 1], out_w[k], 0, 0)
    hat, inv = norm_parts(tokens[...].astype(wide) + attended + b_out)
    hat_ref[...] = hat
    inv_ref[...] = jnp.broadcast_to(inv, inv_ref.shape)
    normed = hat * gain_one + bias_one
    normed_ref[...] = normed.astype(low)
    skip[...] = normed + b_down
    wait_all(copies)
    keep = pltpu.make_async_copy(up, whole, own_sems.at[0])
    keep.start()

    def forward(k, _):
        preact = mm(normed_ref[...], up[k], 1, 0) + bias[k][:, 2 * local :].astype(wide)
        value, derivative = gelu_parts(preact)
        act[k] = value.astype(low)
        slope[k] = derivative.astype(low)
        return 0

    lax.fori_loop(0, parts, forward, 0)
    keep.wait()


def ffn_up(info, tokens, ctx_own, ctx_rest, bias, vec, out_own, out_rest, up_own, pieces):
    seq, width = tokens.shape
    parts, size = ctx_rest.shape[0] + 1, up_own.shape[1]
    return pl.pallas_call(
        ffn_up_kernel,
        in_specs=[smem()] + [vmem()] * 5 + [hbm()] * (3 + 6),
        out_specs=[vmem()] * 6 + [hbm()],
        out_shape=[
            shaped((parts, seq, size), low),
            shaped((parts, seq, size), low),
            shaped((seq, width), wide),
            shaped((seq, width), low),
            shaped((seq, width), wide),
            shaped((seq, 128), wide),
            shaped((parts, width, size), low),
        ],
        scratch_shapes=[
            pltpu.VMEM((parts, ctx_own.shape[1], width), low),
            pltpu.VMEM((parts, width, size), low),
            pltpu.SemaphoreType.DMA((GROUP * (parts - 1),)),
            pltpu.SemaphoreType.DMA((1 + parts,)),
        ],
        compiler_params=params(40),
        cost_estimate=cost(15),
        name="ffn_up",
    )(info, tokens, ctx_own, ctx_rest, bias, vec, out_own, out_rest, up_own, *pieces)


def ffn_down_kernel(info, act, skip, vec, cot, down_own, *refs):
    out, grad_ref, branch_ref, keep, send, small, whole, down, sems, own_sems = refs[6:]
    parts = down.shape[0]
    copies = piece_copies(info, refs[:6], down, sems)
    copies.append(pltpu.make_async_copy(down_own, down.at[0], own_sems.at[0]))
    start_all(copies)
    wait_all(copies)
    hold = pltpu.make_async_copy(down, whole, own_sems.at[0])
    hold.start()
    total = skip[...]
    for k in range(parts):
        total = total + mm(act[k], down[k], 1, 0)
    gain_two, bias_two = vec[4:5], vec[5:6]
    hat_two, inv_two = norm_parts(total)
    out[...] = (hat_two * gain_two + bias_two).astype(low)
    grad = cot[...].astype(wide)
    grad_branch = norm_back(grad * gain_two, hat_two, inv_two)
    grad_ref[...] = grad_branch
    branch_low = grad_branch.astype(low)
    branch_ref[...] = branch_low

    def weight(k, _):
        place_pieces(info, mm(act[k], branch_low, 0, 0), keep, send, (k >> 1, k & 1))
        return 0

    lax.fori_loop(0, parts, weight, 0)
    small[...] = jnp.zeros(small.shape, wide)
    small[3:4] = jnp.sum(grad_branch, axis=0, keepdims=True)
    small[4:5] = jnp.sum(grad * hat_two, axis=0, keepdims=True)
    small[5:6] = jnp.sum(grad, axis=0, keepdims=True)
    hold.wait()


def halves_of(parts, rows, cols):
    return shaped((2, 2, 2, parts // 2, rows // GROUP, cols), low)


def ffn_down(info, act, skip, vec, cot, down_own, pieces):
    parts, seq, size = act.shape
    width = skip.shape[1]
    return pl.pallas_call(
        ffn_down_kernel,
        in_specs=[smem()] + [vmem()] * 4 + [hbm()] * (1 + 6),
        out_specs=[vmem()] * 6 + [hbm()],
        out_shape=[
            shaped((seq, width), low),
            shaped((seq, width), wide),
            shaped((seq, width), low),
            halves_of(parts, size, width),
            halves_of(parts, size, width),
            shaped((16, width), wide),
            shaped((parts, size, width), low),
        ],
        scratch_shapes=[
            pltpu.VMEM((parts, size, width), low),
            pltpu.SemaphoreType.DMA((GROUP * (parts - 1),)),
            pltpu.SemaphoreType.DMA((1,)),
        ],
        compiler_params=params(40),
        cost_estimate=cost(12),
        name="ffn_down",
    )(info, act, skip, vec, cot, down_own, *pieces)


def ffn_back_kernel(
    info, branch_low, grad_branch, slope, normed_low, hat_ref, inv_ref, vec, small_in, up, down,
    keep, send, grad_ref, residual_ref, small, turned, total,
):
    parts = up.shape[0]
    index = lax.broadcasted_iota(jnp.int32, small.shape, 0)

    def put(row, value):
        small[...] = jnp.where(index == row, value, small[...])

    small[...] = small_in[...]
    total[...] = grad_branch[...]
    turned[...] = normed_low[...].T

    def backward(k, _):
        grad_pre = (mm(branch_low[...], down[k], 1, 1) * slope[k].astype(wide)).astype(low)
        put(6 + (info[3] ^ k), jnp.sum(grad_pre.astype(wide), axis=0, keepdims=True))
        place_pieces(info, mm(turned[...], grad_pre, 1, 0), keep, send, (k >> 1, k & 1))
        total[...] += mm(grad_pre, up[k], 1, 1)
        return 0

    lax.fori_loop(0, parts, backward, 0)
    grad_normed = total[...]
    hat = hat_ref[...]
    grad_residual = norm_back(grad_normed * vec[1:2], hat, inv_ref[:, :1])
    grad_ref[...] = grad_residual
    residual_ref[...] = grad_residual.astype(low)
    small[0:1] = jnp.sum(grad_residual, axis=0, keepdims=True)
    small[1:2] = jnp.sum(grad_normed * hat, axis=0, keepdims=True)
    small[2:3] = jnp.sum(grad_normed, axis=0, keepdims=True)


def ffn_back(info, branch_low, grad_branch, slope, normed_low, hat, inv, vec, small, up, down):
    parts, width, size = up.shape
    seq = hat.shape[0]
    return pl.pallas_call(
        ffn_back_kernel,
        in_specs=[smem()] + [vmem()] * 10,
        out_specs=[vmem()] * 5,
        out_shape=[
            halves_of(parts, width, size),
            halves_of(parts, width, size),
            shaped((seq, width), wide),
            shaped((seq, width), low),
            shaped((16, width), wide),
        ],
        scratch_shapes=[pltpu.VMEM((width, seq), low), pltpu.VMEM((seq, width), wide)],
        compiler_params=params(48),
        cost_estimate=cost(15),
        name="ffn_back",
    )(info, branch_low, grad_branch, slope, normed_low, hat, inv, vec, small, up, down)


def attn_back_kernel(first, info, tokens, residual_low, small_in, *refs):
    groups = (refs[:4], refs[4:8])
    keep, send, small, joint = refs[8:]
    local = groups[0][2].shape[1]
    seq, width = tokens.shape
    scale = HD**-0.5
    index = lax.broadcasted_iota(jnp.int32, small.shape, 0)
    small[...] = small_in[...]
    key_pad, query_pad = masked_pad(info[0], seq)
    ones = jnp.ones((8, seq), low)
    for i, (weights, qkv, ctx, lse) in enumerate(groups):
        grad_ctx = mm(weights[0, 3 * local :], residual_low[...], 1, 1).astype(low)
        for h in range(local // HD):
            lo, hi = h * HD, (h + 1) * HD
            query = qkv[0, lo:hi]
            key = qkv[0, local + lo : local + hi]
            value = qkv[0, 2 * local + lo : 2 * local + hi]
            grad_head = grad_ctx[lo:hi]
            scores = mm(
                jnp.concatenate([key, key_pad], 0), jnp.concatenate([query, query_pad], 0), 0, 0
            )
            probs = jnp.exp2(scores * (scale * LOG2E) - lse[0, h : h + 1])
            grad_probs = mm(value, grad_head, 0, 0)
            product = probs * grad_probs
            grad_scores = (product - probs * jnp.sum(product, axis=0, keepdims=True)).astype(low)
            joint[i, lo:hi] = (mm(key, grad_scores, 1, 0) * scale).astype(low)
            joint[i, local + lo : local + hi] = (mm(query, grad_scores, 1, 1) * scale).astype(low)
            joint[i, 2 * local + lo : 2 * local + hi] = mm(
                grad_head, probs.astype(low), 1, 1
            ).astype(low)
        grads = joint[i]
        sums = mm(ones, grads, 1, 1)[:1]
        gap = jnp.zeros((1, 256 - local), wide)
        rest = jnp.zeros((1, width - 512), wide)
        sums = jnp.concatenate([sums[:, :local], gap, sums[:, 2 * local :], gap, rest], 1)
        small[...] = jnp.where(index == 10 + (info[3] ^ (first + i)), sums, small[...])
        shares = jnp.concatenate(
            [mm(grads, tokens[...], 1, 0), mm(ctx[0], residual_low[...], 1, 0)], 0
        )
        place_pieces(info, shares, keep, send, (i,))


def attn_back(first, info, tokens, residual_low, small, own_w, own, rest):
    seq, width = tokens.shape
    size = own_w.shape[1]
    local = size // 4
    specs, arrays = [], []
    for k in (first, first + 1):
        source = (own_w,) + tuple(own) if k == 0 else (rest[3],) + tuple(rest[:3])
        index = (max(k - 1, 0), 0, 0)
        specs += [block((1,) + array.shape[1:], index) for array in source]
        arrays += source
    half = shaped((2, 2, 2, size // GROUP, width), low)
    whole = block((seq, width), (0, 0))
    return pl.pallas_call(
        partial(attn_back_kernel, first),
        grid=(1,),
        in_specs=[smem(), whole, whole, block((16, width), (0, 0))] + specs,
        out_specs=[
            block(half.shape, (0,) * 5),
            block(half.shape, (0,) * 5),
            block((16, width), (0, 0)),
            block((2, 3 * local, seq), (0, 0, 0)),
        ],
        out_shape=[half, half, shaped((16, width), wide), shaped((2, 3 * local, seq), low)],
        compiler_params=params(40),
        cost_estimate=cost(14),
        name="attn_back",
    )(info, tokens, residual_low, small, *arrays)


def grad_tokens_kernel(grad, joint_a, joint_b, own_w, rest_w, out):
    rows = joint_a.shape[1]
    total = grad[...]
    for k in range(4):
        joint = joint_a[k] if k < 2 else joint_b[k - 2]
        weights = own_w[0, :rows] if k == 0 else rest_w[k - 1, :rows]
        total = total + mm(joint, weights, 0, 0)
    out[...] = total.astype(low)


def grad_tokens_of(grad, joint_a, joint_b, own_w, rest_w):
    return pl.pallas_call(
        grad_tokens_kernel,
        in_specs=[vmem()] * 5,
        out_specs=vmem(),
        out_shape=shaped(grad.shape, low),
        compiler_params=params(32),
        cost_estimate=cost(5),
        name="grad_tokens",
    )(grad, joint_a, joint_b, own_w, rest_w)


def gather_rows(info, refs, target):
    for s in range(2):
        first, second, third = refs[3 * s : 3 * s + 3]
        holder = info[1] ^ s
        rows = first.shape[0]
        moves = (0, 1 + holder, 2 - holder, 3)
        for move, view in zip(moves, (first, second, third.at[0], third.at[1])):
            start = pl.multiple_of((holder * 4 + (info[2] ^ move)) * rows, rows)
            target[pl.ds(start, rows), :] = view[...].astype(wide)


def finish_ffn_kernel(info, *refs):
    gather_rows(info, refs[:6], refs[6])


def finish_ffn(info, pieces):
    rows, cols = pieces[0].shape
    return pl.pallas_call(
        finish_ffn_kernel,
        in_specs=[smem()] + [vmem()] * 6,
        out_specs=vmem(),
        out_shape=shaped((GROUP * rows, cols), wide),
        compiler_params=params(16),
        cost_estimate=cost(2),
        name="finish_ffn",
    )(info, *pieces)


def finish_attn_kernel(info, *refs):
    query, key, value, out, whole = refs[6:]
    gather_rows(info, refs[:6], whole)
    local = whole.shape[0] // 4
    query[...] = whole[:local].T
    key[...] = whole[local : 2 * local].T
    value[...] = whole[2 * local : 3 * local].T
    out[...] = whole[3 * local :]


def finish_attn(info, pieces):
    rows, cols = pieces[0].shape
    size = GROUP * rows
    local = size // 4
    return pl.pallas_call(
        finish_attn_kernel,
        in_specs=[smem()] + [vmem()] * 6,
        out_specs=[vmem()] * 4,
        out_shape=[shaped((cols, local), wide)] * 3 + [shaped((local, cols), wide)],
        scratch_shapes=[pltpu.VMEM((size, cols), wide)],
        compiler_params=params(24),
        cost_estimate=cost(2),
        name="finish_attn",
    )(info, *pieces)


class Links:
    def __init__(self, dp_size, parts):
        self.dp_size, self.parts = dp_size, parts

    def move(self, array, partner):
        pairs = []
        for d in range(self.dp_size):
            for t in range(self.parts):
                to_d, to_t = partner(d, t)
                pairs.append((d * self.parts + t, to_d * self.parts + to_t))
        return lax.ppermute(array, ("dp", "tensor"), pairs)

    def bit(self, array, bit):
        return self.move(array, lambda d, t: (d ^ bit, t))

    def core(self, array):
        return self.bit(array, 1)

    def plane(self, array, step):
        return self.move(array, lambda d, t: (d ^ (2 if (d & 1) == step else 4), t))

    def line(self, array, step):
        return self.move(array, lambda d, t: (d, t ^ (1 if (d & 1) == step else 2)))


def add(left, right):
    return (left.astype(wide) + right.astype(wide)).astype(low)


def after(*values):
    return lax.optimization_barrier(values)


class Sum:
    def __init__(self, links, is_odd):
        self.links, self.is_odd = links, is_odd

    def split(self, both):
        return jnp.where(self.is_odd, both[:, 1], both[1]), jnp.where(self.is_odd, both[:, 0], both[0])


def per_device(
    dp_size,
    parts,
    tokens,
    page_lengths,
    w_query,
    b_query,
    w_key,
    w_value,
    b_value,
    w_out,
    b_out,
    ln1_gain,
    ln1_bias,
    w_up,
    b_up,
    w_down,
    b_down,
    ln2_gain,
    ln2_bias,
    cotangent,
):
    links = Links(dp_size, parts)
    me = lax.axis_index("tensor")
    place = lax.axis_index("dp") % GROUP
    core, quarter = place & 1, place >> 1
    is_odd = core == 1
    width = tokens.shape[1]
    local = w_query.shape[1]
    rows = width // GROUP
    length = lax.dynamic_slice_in_dim(page_lengths, me, 1, 0)
    info = jnp.concatenate([length, jnp.stack([core, quarter, me]).astype(jnp.int32)])
    attn_w = jnp.concatenate([w_query.T, w_key.T, w_value.T, w_out], axis=0)
    cut = partial(
        lax.dynamic_slice_in_dim, start_index=(core * 4 + quarter) * rows, slice_size=rows, axis=0
    )
    bias_own = jnp.concatenate([b_query, b_value, b_up])
    bias_rows = jnp.pad(bias_own, (0, 16 * width - bias_own.size)).reshape(16, width)
    vec = jnp.stack([b_out, ln1_gain, ln1_bias, b_down, ln2_gain, ln2_bias, b_down, b_down])
    vec = vec.astype(wide)
    attn_w3 = attn_w[None]

    a0 = jnp.concatenate([cut(attn_w), bias_rows], axis=0)
    u0, d0 = cut(w_up), cut(w_down)
    a1 = links.line(a0, 0)
    a1, u0, tokens_in = after(a1, u0, tokens)
    a2 = links.line(jnp.stack([a0, a1]), 1)
    u1 = links.line(u0, 0)
    own = attn_own(info, tokens_in, attn_w, bias_own.astype(wide)[None, None])
    a2, u1, d0 = after(a2, u1, d0)
    a3 = jnp.concatenate([a1[None], a2])
    bias_rest = a3[:, rows:].reshape(parts - 1, 16 * width)[:, : bias_own.size]
    near, far = bias_rest[0], bias_rest[1]
    bias = jnp.stack(
        [bias_own, jnp.where(is_odd, far, near), jnp.where(is_odd, near, far), bias_rest[2]]
    )
    bias = bias.astype(wide)[:, None]
    a3 = a3[:, :rows]
    a4 = links.plane(a3, 0)
    u2 = links.line(jnp.stack([u0, u1]), 1)
    d1 = links.line(d0, 0)
    a4, u2, d1 = after(a4, u2, d1)
    u3 = jnp.concatenate([u1[None], u2])
    a5 = links.plane(jnp.stack([a3, a4]), 1)
    u4 = links.plane(u3, 0)
    d2 = links.line(jnp.stack([d0, d1]), 1)
    a5, u4, d2 = after(a5, u4, d2)
    d3 = jnp.concatenate([d1[None], d2])
    pieces_a = [a3, a4, a5] + [links.core(array) for array in (a3, a4, a5)]
    u5 = links.plane(jnp.stack([u3, u4]), 1)
    d4 = links.plane(d3, 0)
    rest = attn_rest(info, tokens, bias, pieces_a)
    u5, d4, *rest = after(u5, d4, *rest)
    pieces_u = [u3, u4, u5] + [links.core(array) for array in (u3, u4, u5)]
    d5 = links.plane(jnp.stack([d3, d4]), 1)
    act, slope, skip, normed_low, hat, inv, up = ffn_up(
        info, tokens, own[1], rest[1], bias, vec, attn_w, rest[3], w_up, pieces_u
    )
    d5, act = after(d5, act)
    pieces_d = [d3, d4, d5] + [links.core(array) for array in (d3, d4, d5)]
    output, grad_branch, branch_low, keep_d, send_d, small, down = ffn_down(
        info, act, skip, vec, cotangent, w_down, pieces_d
    )

    line_split = Sum(links, is_odd).split

    def plane_a(keep, got):
        return links.plane(add(keep[1], got[1]), 0), add(keep[0], got[0])

    def plane_b(kept, got):
        return links.plane(add(kept[1], got[1]), 1), add(kept[0], got[0])

    def line_a(kept, got):
        sent, held = line_split(add(kept, got))
        return links.line(sent, 1), held

    def line_b(kept, got):
        both = add(kept, got)
        return links.line(both[1], 0), both[0]

    def settle(kept, got):
        total = kept.astype(wide) + got.astype(wide)
        bit = GROUP
        while bit < dp_size:
            total = total + links.bit(total, bit)
            bit *= 2
        return total.astype(low)

    got_d = links.core(send_d)
    got_d, branch_low = after(got_d, branch_low)
    near_d, kept_d = plane_a(keep_d, got_d)
    keep_u, send_u, grad_residual, residual_low, small = ffn_back(
        info, branch_low, grad_branch, slope, normed_low, hat, inv, vec, small, up, down
    )
    near_d, send_u = after(near_d, send_u)
    got_u = links.core(send_u)
    far_d, kept_d = plane_b(kept_d, near_d)
    far_d, got_u, residual_low = after(far_d, got_u, residual_low)
    near_u, kept_u = plane_a(keep_u, got_u)
    line_d, kept_d = line_a(kept_d, far_d)
    keep_a, send_a, small, joint_a = attn_back(
        0, info, tokens, residual_low, small, attn_w3, own, rest
    )
    near_u, line_d, send_a, small = after(near_u, line_d, send_a, small)
    far_u, kept_u = plane_b(kept_u, near_u)
    last_d, kept_d = line_b(kept_d, line_d)
    got_a = links.core(send_a)
    keep_b, send_b, small, joint_b = attn_back(
        2, info, tokens, residual_low, small, attn_w3, own, rest
    )
    far_u, last_d, got_a, send_b = after(far_u, last_d, got_a, send_b)
    got_b = links.core(send_b)
    line_u, kept_u = line_a(kept_u, far_u)
    sum_d = settle(kept_d, last_d)
    g1 = links.plane(sum_d, 0)
    got_b, line_u, g1, joint_b = after(got_b, line_u, g1, joint_b)
    keep = jnp.stack([keep_a, keep_b], axis=2)
    got = jnp.stack([got_a, got_b], axis=2)
    near_a, kept_a = plane_a(keep, got)
    last_u, kept_u = line_b(kept_u, line_u)
    g2 = links.plane(jnp.stack([sum_d, g1]), 1)
    grad_tokens = grad_tokens_of(grad_residual, joint_a, joint_b, attn_w3, rest[3])
    near_a, last_u, g2, grad_tokens, small = after(near_a, last_u, g2, grad_tokens, small)
    far_a, kept_a = plane_b(kept_a, near_a)
    sum_u = settle(kept_u, last_u)
    h1 = links.plane(sum_u, 0)
    held = [sum_d, g1, g2]
    pieces = held + [links.core(array) for array in held]
    small = small + links.core(small)
    small_got = links.plane(small, 0)
    far_a, h1, small_got, *pieces = after(far_a, h1, small_got, *pieces)
    line, kept_a = line_a(kept_a, far_a)
    h2 = links.plane(jnp.stack([sum_u, h1]), 1)
    small = small + small_got
    small_got = links.plane(small, 1)
    grad_w_down = finish_ffn(info, pieces)
    line, h2, small_got = after(line, h2, small_got)
    last_a, kept_a = line_b(kept_a, line)
    held = [sum_u, h1, h2]
    pieces = held + [links.core(array) for array in held]
    small = small + small_got
    small_got = links.line(small, 0)
    last_a, small_got, *pieces = after(last_a, small_got, *pieces)
    sum_a = settle(kept_a, last_a)
    i1 = links.plane(sum_a, 0)
    small = small + small_got
    small_got = links.line(small, 1)
    grad_w_up = finish_ffn(info, pieces)
    i1, small_got, grad_w_up = after(i1, small_got, grad_w_up)
    small = small + small_got
    bit = GROUP
    while bit < dp_size:
        small = small + links.bit(small, bit)
        bit *= 2
    i2 = links.plane(jnp.stack([sum_a, i1]), 1)
    held = [sum_a, i1, i2]
    pieces = held + [links.core(array) for array in held]
    grad_w_query, grad_w_key, grad_w_value, grad_w_out = finish_attn(info, pieces)
    pair = lax.dynamic_index_in_dim(small, 10 + me, 0, keepdims=False)
    grad_b_up = lax.dynamic_index_in_dim(small, 6 + me, 0, keepdims=False)
    return (
        output,
        grad_tokens,
        grad_w_query,
        pair[:local],
        grad_w_key,
        grad_w_value,
        pair[256 : 256 + local],
        grad_w_out,
        small[0],
        small[1],
        small[2],
        grad_w_up,
        grad_b_up,
        grad_w_down,
        small[3],
        small[4],
        small[5],
    )


def solution(mesh):
    columns, rows, both = P(None, "tensor"), P("tensor", None), P(("dp", "tensor"), None)
    share = P("tensor")
    return jax.shard_map(
        partial(per_device, mesh.shape["dp"], mesh.shape["tensor"]),
        mesh=mesh,
        in_specs=(
            both,
            P("dp"),
            columns,
            share,
            columns,
            columns,
            share,
            rows,
            P(),
            P(),
            P(),
            columns,
            share,
            rows,
            P(),
            P(),
            P(),
            both,
        ),
        out_specs=(
            both,
            both,
            columns,
            share,
            columns,
            columns,
            share,
            rows,
            P(),
            P(),
            P(),
            columns,
            share,
            rows,
            P(),
            P(),
            P(),
        ),
        check_vma=False,
    )
```

```python
from functools import partial

import jax
import jax.numpy as jnp
from jax import lax
from jax.experimental import pallas as pl
from jax.experimental.pallas import tpu as pltpu
from jax.sharding import PartitionSpec as P

HD = 64
SEQ = 512
GROUP = 8
LOG2E = 1.4426950408889634
TAIL_P = 0.39
TAIL = (
    0.23532521908406087,
    0.09138841455460205,
    0.6495593986198918,
    -0.6354002786931026,
    0.8866643698688825,
    -0.22753712513305413,
)

epsilon = 1e-12
masked_score = -1000000000.0
low = jnp.bfloat16
wide = jnp.float32
PEAK = 1.1e15
LIMIT = 12


def mm(left, right, left_dim, right_dim):
    return lax.dot_general(
        left, right, (((left_dim,), (right_dim,)), ((), ())), preferred_element_type=wide
    )


def vmem():
    return pl.BlockSpec(memory_space=pltpu.VMEM)


def smem():
    return pl.BlockSpec(memory_space=pltpu.SMEM)


def hbm():
    return pl.BlockSpec(memory_space=pl.ANY)


def cost(microseconds):
    return pl.CostEstimate(
        flops=int(microseconds * 1e-6 * PEAK), bytes_accessed=1 << 20, transcendentals=0
    )


def params(mebibytes=LIMIT):
    return pltpu.CompilerParams(vmem_limit_bytes=mebibytes << 20)


def shaped(shape, dtype):
    return jax.ShapeDtypeStruct(shape, dtype)


def masked_pad(length, seq):
    row = lax.broadcasted_iota(jnp.int32, (16, seq), 0)
    key = lax.broadcasted_iota(jnp.int32, (16, seq), 1)
    bias = jnp.where((row == 0) & (key >= length), masked_score, 0.0).astype(low)
    ones = jnp.where(row == 0, 1.0, 0.0).astype(low)
    return bias, ones


def as_column(row, ones):
    first = lax.broadcasted_iota(jnp.int32, (16, row.shape[1]), 0) == 0
    return mm(jnp.where(first, row, 0.0).astype(low), ones, 0, 0)


def group_forward(tokens, weights, bias, length, qkv_ref, ctx_ref, lse_ref):
    local = weights[0].shape[0]
    seq = tokens.shape[0]
    scale = HD**-0.5 * LOG2E
    key_pad, ones = masked_pad(length, seq)
    query = (mm(weights[0], tokens, 1, 1) + as_column(bias[:, :local], ones)).astype(low)
    key = mm(weights[1], tokens, 1, 1).astype(low)
    value = mm(weights[2], tokens, 1, 1) + as_column(bias[:, local : 2 * local], ones)
    value = value.astype(low)
    qkv_ref[:local] = query
    qkv_ref[local : 2 * local] = key
    qkv_ref[2 * local :] = value
    for h in range(local // HD):
        part = slice(h * HD, (h + 1) * HD)
        scores = mm(
            jnp.concatenate([key[part], key_pad], 0), jnp.concatenate([query[part], ones], 0), 0, 0
        )
        top = jnp.max(scores, axis=0, keepdims=True)
        probs = jnp.exp2((scores - top) * scale)
        total = jnp.sum(probs, axis=0, keepdims=True)
        context = mm(value[part], probs.astype(low), 1, 0)
        ctx_ref[part] = (context * (1.0 / total)).astype(low)
        lse_ref[h : h + 1] = top * scale + jnp.log2(total)


def gelu_parts(x):
    t = 1.0 / (1.0 + (TAIL_P * 0.5**0.5) * jnp.abs(x))
    poly = TAIL[-1]
    for factor in TAIL[-2::-1]:
        poly = poly * t + factor
    bell = jnp.exp2(x * x * (-0.5 * LOG2E))
    half = 0.5 * poly * t * bell
    cdf = jnp.where(x >= 0, 1.0 - half, half)
    return x * cdf, cdf + x * bell * (0.5 / jnp.pi) ** 0.5


def norm_parts(values):
    centred = values - jnp.mean(values, axis=1, keepdims=True)
    inverse = lax.rsqrt(jnp.mean(centred * centred, axis=1, keepdims=True) + epsilon)
    return centred * inverse, inverse


def norm_back(scaled, normal, inverse):
    return inverse * (
        scaled
        - jnp.mean(scaled, axis=1, keepdims=True)
        - normal * jnp.mean(scaled * normal, axis=1, keepdims=True)
    )


def assemble(info, refs, target):
    for s in range(2):
        first, second, third = refs[3 * s : 3 * s + 3]
        holder = info[1] ^ s
        order = (1 + holder, 2 - holder, 3)
        views = (first, second, third.at[0], third.at[1])
        for view, move in zip(views, (0,) + order):
            rows = view.shape[1]
            start = pl.multiple_of((holder * 4 + (info[2] ^ move)) * rows, rows)
            for entry, k in enumerate(order):
                target[k - 1, pl.ds(start, rows), :] = view[entry]


def place_pieces(info, scratch, keep_ref, send_ref, entry):
    rows = scratch.shape[0] // GROUP
    for s, target in enumerate((keep_ref, send_ref)):
        half = info[1] ^ s
        for q in range(4):
            move = info[2] ^ q
            x_bit, y_bit = move & 1, move >> 1
            a = jnp.where(half == 0, x_bit, y_bit)
            start = pl.multiple_of((half * 4 + q) * rows, rows)
            target[a, x_bit + y_bit - a, entry] = scratch[pl.ds(start, rows), :]


def attn_own_kernel(info, tokens, w_query, w_key, w_value, bias, qkv, ctx, lse):
    weights = (w_query[...], w_key[...], w_value[...])
    group_forward(tokens[...], weights, bias[0], info[0], qkv.at[0], ctx.at[0], lse.at[0])


def attn_own(info, tokens, weights, bias):
    local, seq = weights[0].shape[0], tokens.shape[0]
    return pl.pallas_call(
        attn_own_kernel,
        in_specs=[smem()] + [vmem()] * 5,
        out_specs=[vmem()] * 3,
        out_shape=[
            shaped((1, 3 * local, seq), low),
            shaped((1, local, seq), low),
            shaped((1, 8, seq), wide),
        ],
        compiler_params=params(),
        cost_estimate=cost(4),
        name="attn_own",
    )(info, tokens, *weights, bias)


def attn_rest_kernel(info, tokens, bias, *refs):
    qkv_out, whole, ctx, lse, out_w, weights, qkv, sems = refs[6:]
    others, local = ctx.shape[:2]
    assemble(info, refs[:6], weights)
    sent = [pltpu.make_async_copy(weights, whole, sems.at[others])]
    sent[0].start()
    out_w[...] = weights[:, 3 * local :]
    for k in range(others):
        joint = tuple(weights[k, i * local : (i + 1) * local] for i in range(3))
        group_forward(
            tokens[...], joint, bias[k + 1], info[0], qkv.at[k], ctx.at[k], lse.at[k]
        )
        sent.append(pltpu.make_async_copy(qkv.at[k], qkv_out.at[k], sems.at[k]))
        sent[-1].start()
    for copy in sent:
        copy.wait()


def attn_rest(info, tokens, bias, pieces):
    others, rows, cols = pieces[0].shape
    size, seq = rows * GROUP, tokens.shape[0]
    local = size // 4
    joint, whole = (others, 3 * local, seq), (others, size, cols)
    return pl.pallas_call(
        attn_rest_kernel,
        in_specs=[smem()] + [vmem()] * 8,
        out_specs=[pl.BlockSpec(memory_space=pltpu.HBM)] * 2 + [vmem()] * 3,
        out_shape=[
            shaped(joint, low),
            shaped(whole, low),
            shaped((others, local, seq), low),
            shaped((others, 8, seq), wide),
            shaped((others, local, cols), low),
        ],
        scratch_shapes=[
            pltpu.VMEM(whole, low),
            pltpu.VMEM(joint, low),
            pltpu.SemaphoreType.DMA((others + 1,)),
        ],
        compiler_params=params(),
        cost_estimate=cost(8),
        name="attn_rest",
    )(info, tokens, bias, *pieces)


def ffn_in_kernel(tokens, ctx_own, ctx_rest, vec, out_own, out_rest, skip, normed_ref, hat_ref, inv_ref):
    others = ctx_rest.shape[0]
    rows = vec[...]
    b_out, gain_one, bias_one, b_down = (rows[i : i + 1] for i in range(4))
    attended = mm(ctx_own[0], out_own[...], 0, 0)
    for k in range(others):
        attended = attended + mm(ctx_rest[k], out_rest[k], 0, 0)
    hat, inv = norm_parts(tokens[...].astype(wide) + attended + b_out)
    hat_ref[...] = hat
    inv_ref[...] = jnp.broadcast_to(inv, inv_ref.shape)
    normed = hat * gain_one + bias_one
    normed_ref[...] = normed.astype(low)
    skip[...] = normed + b_down


def ffn_in(tokens, ctx_own, ctx_rest, vec, out_own, out_rest):
    seq, width = tokens.shape
    others, local = ctx_rest.shape[:2]
    return pl.pallas_call(
        ffn_in_kernel,
        in_specs=[vmem()] * 6,
        out_specs=[vmem()] * 4,
        out_shape=[
            shaped((seq, width), wide),
            shaped((seq, width), low),
            shaped((seq, width), wide),
            shaped((seq, 128), wide),
        ],
        compiler_params=params(),
        cost_estimate=cost(5),
        name="ffn_in",
    )(tokens, ctx_own, ctx_rest, vec, out_own, out_rest)


def ffn_up_kernel(info, normed, bias, up_own, *refs):
    _, act, slope, up, mark = refs[6:]
    size = up.shape[2]
    first = bias.shape[2] - size
    mark[...] = jnp.zeros(mark.shape, wide)
    assemble(info, refs[:6], up)
    for k in range(act.shape[0]):
        weights = up_own[...] if k == 0 else up[k - 1]
        preact = mm(normed[...], weights, 1, 0) + bias[k][:, first:].astype(wide)
        value, derivative = gelu_parts(preact)
        act[k] = value.astype(low)
        slope[k] = derivative.astype(low)


def ffn_up(info, normed, bias, up_own, pieces, mark):
    seq, width = normed.shape
    others, size = pieces[0].shape[0], up_own.shape[1]
    return pl.pallas_call(
        ffn_up_kernel,
        in_specs=[smem()] + [vmem()] * (3 + 6) + [hbm()],
        out_specs=[vmem()] * 4,
        out_shape=[
            shaped((others + 1, seq, size), low),
            shaped((others + 1, seq, size), low),
            shaped((others, width, size), low),
            shaped((8, 128), wide),
        ],
        compiler_params=params(),
        cost_estimate=cost(11),
        name="ffn_up",
    )(info, normed, bias, up_own, *pieces, mark)


def ffn_down_kernel(info, skip, vec, cot, act, down_own, *refs):
    _, out, grad_ref, branch_ref, small, keep, send, down, scratch = refs[6:]
    parts = act.shape[0]
    total = skip[...] + mm(act[0], down_own[...], 1, 0)
    assemble(info, refs[:6], down)
    for k in range(1, parts):
        total = total + mm(act[k], down[k - 1], 1, 0)
    gain_two, bias_two = vec[4:5], vec[5:6]
    hat_two, inv_two = norm_parts(total)
    out[...] = (hat_two * gain_two + bias_two).astype(low)
    grad = cot[...].astype(wide)
    grad_branch = norm_back(grad * gain_two, hat_two, inv_two)
    grad_ref[...] = grad_branch
    branch_low = grad_branch.astype(low)
    branch_ref[...] = branch_low
    small[...] = jnp.zeros(small.shape, wide)
    small[3:4] = jnp.sum(grad_branch, axis=0, keepdims=True)
    small[4:5] = jnp.sum(grad * hat_two, axis=0, keepdims=True)
    small[5:6] = jnp.sum(grad, axis=0, keepdims=True)
    for k in range(parts):
        scratch[...] = mm(act[k], branch_ref[...], 0, 0).astype(low)
        place_pieces(info, scratch, keep, send, k)


def halves_shape(entries, rows, cols):
    return (2, 2, entries, rows // GROUP, cols)


def ffn_down(info, act, skip, vec, cot, down_own, pieces, mark):
    parts, seq, size = act.shape
    width = skip.shape[1]
    half = halves_shape(parts, size, width)
    return pl.pallas_call(
        ffn_down_kernel,
        in_specs=[smem()] + [vmem()] * (5 + 6) + [hbm()],
        out_specs=[vmem()] * 7,
        out_shape=[
            shaped((seq, width), low),
            shaped((seq, width), wide),
            shaped((seq, width), low),
            shaped((16, width), wide),
            shaped(half, low),
            shaped(half, low),
            shaped((parts - 1, size, width), low),
        ],
        scratch_shapes=[pltpu.VMEM((size, width), low)],
        compiler_params=params(),
        cost_estimate=cost(12),
        name="ffn_down",
    )(info, skip, vec, cot, act, down_own, *pieces, mark)


def ffn_back_kernel(
    info, branch_low, grad_branch, normed_low, hat_ref, inv_ref, vec, small_in, slope, up_own, down_own, up, down,
    grad_ref, residual_ref, small, keep, send, turned, total, scratch,
):
    parts = slope.shape[0]
    index = lax.broadcasted_iota(jnp.int32, small.shape, 0)
    small[...] = small_in[...]
    total[...] = grad_branch[...]
    turned[...] = normed_low[...].T
    for k in range(parts):
        down_w = down_own[...] if k == 0 else down[k - 1]
        up_w = up_own[...] if k == 0 else up[k - 1]
        grad_pre = mm(branch_low[...], down_w, 1, 1) * slope[k].astype(wide)
        grad_pre = grad_pre.astype(low)
        sums = jnp.sum(grad_pre.astype(wide), axis=0, keepdims=True)
        small[...] = jnp.where(index == 6 + (info[3] ^ k), sums, small[...])
        scratch[...] = mm(turned[...], grad_pre, 1, 0).astype(low)
        place_pieces(info, scratch, keep, send, k)
        total[...] += mm(grad_pre, up_w, 1, 1)
    grad_normed = total[...]
    hat = hat_ref[...]
    grad_residual = norm_back(grad_normed * vec[1:2], hat, inv_ref[:, :1])
    grad_ref[...] = grad_residual
    residual_ref[...] = grad_residual.astype(low)
    small[0:1] = jnp.sum(grad_residual, axis=0, keepdims=True)
    small[1:2] = jnp.sum(grad_normed * hat, axis=0, keepdims=True)
    small[2:3] = jnp.sum(grad_normed, axis=0, keepdims=True)


def ffn_back(info, branch_low, grad_branch, slope, normed_low, hat, inv, vec, small, own, up, down):
    _, width, size = up.shape
    parts, seq = slope.shape[:2]
    half = halves_shape(parts, width, size)
    return pl.pallas_call(
        ffn_back_kernel,
        in_specs=[smem()] + [vmem()] * 12,
        out_specs=[vmem()] * 5,
        out_shape=[
            shaped((seq, width), wide),
            shaped((seq, width), low),
            shaped((16, width), wide),
            shaped(half, low),
            shaped(half, low),
        ],
        scratch_shapes=[
            pltpu.VMEM((width, seq), low),
            pltpu.VMEM((seq, width), wide),
            pltpu.VMEM((width, size), low),
        ],
        compiler_params=params(),
        cost_estimate=cost(11),
        name="ffn_back",
    )(info, branch_low, grad_branch, normed_low, hat, inv, vec, small, slope, *own, up, down)


def attn_back_kernel(first, info, tokens, residual_low, small_in, *refs):
    groups = (refs[:4], refs[4:8])
    small, joint, keep, send, scratch = refs[8:]
    local = groups[0][2].shape[1]
    seq, width = tokens.shape
    scale = HD**-0.5
    index = lax.broadcasted_iota(jnp.int32, small.shape, 0)
    small[...] = small_in[...]
    key_pad, query_pad = masked_pad(info[0], seq)
    ones = jnp.ones((8, seq), low)
    for i, (out_w, qkv_ref, ctx_ref, lse_ref) in enumerate(groups):
        k = first + i
        out_rows = out_w[...] if k == 0 else out_w[k - 1]
        qkv, ctx, lse = (ref.at[max(k - 1, 0)] for ref in (qkv_ref, ctx_ref, lse_ref))
        grad_ctx = mm(out_rows, residual_low[...], 1, 1).astype(low)
        for h in range(local // HD):
            lo, hi = h * HD, (h + 1) * HD
            query = qkv[lo:hi]
            key = qkv[local + lo : local + hi]
            value = qkv[2 * local + lo : 2 * local + hi]
            grad_head = grad_ctx[lo:hi]
            scores = mm(
                jnp.concatenate([key, key_pad], 0), jnp.concatenate([query, query_pad], 0), 0, 0
            )
            probs = jnp.exp2(scores * (scale * LOG2E) - lse[h : h + 1])
            grad_probs = mm(value, grad_head, 0, 0)
            product = probs * grad_probs
            grad_scores = (product - probs * jnp.sum(product, axis=0, keepdims=True)).astype(low)
            joint[i, lo:hi] = (mm(key, grad_scores, 1, 0) * scale).astype(low)
            joint[i, local + lo : local + hi] = (mm(query, grad_scores, 1, 1) * scale).astype(low)
            joint[i, 2 * local + lo : 2 * local + hi] = mm(
                grad_head, probs.astype(low), 1, 1
            ).astype(low)
        grads = joint[i]
        sums = mm(ones, grads, 1, 1)[:1]
        gap = jnp.zeros((1, 256 - local), wide)
        rest = jnp.zeros((1, width - 512), wide)
        sums = jnp.concatenate([sums[:, :local], gap, sums[:, 2 * local :], gap, rest], 1)
        small[...] = jnp.where(index == 10 + (info[3] ^ (first + i)), sums, small[...])
        scratch[: 3 * local] = mm(grads, tokens[...], 1, 0).astype(low)
        scratch[3 * local :] = mm(ctx[...], residual_low[...], 1, 0).astype(low)
        place_pieces(info, scratch, keep, send, i)


def attn_back(first, info, tokens, residual_low, small, out_own, own, out_rest, rest):
    seq, width = tokens.shape
    local = out_own.shape[0]
    arrays = []
    for k in (first, first + 1):
        arrays += (out_own,) + tuple(own) if k == 0 else (out_rest,) + tuple(rest)
    half = halves_shape(2, 4 * local, width)
    return pl.pallas_call(
        partial(attn_back_kernel, first),
        in_specs=[smem()] + [vmem()] * 11,
        out_specs=[vmem()] * 4,
        out_shape=[
            shaped((16, width), wide),
            shaped((2, 3 * local, seq), low),
            shaped(half, low),
            shaped(half, low),
        ],
        scratch_shapes=[pltpu.VMEM((4 * local, width), low)],
        compiler_params=params(),
        cost_estimate=cost(9),
        name="attn_back",
    )(info, tokens, residual_low, small, *arrays)


def grad_tokens_kernel(grad, joint_a, joint_b, w_query, w_key, w_value, rest_w, out):
    local, rows = w_query.shape[0], joint_a.shape[1]
    total = grad[...]
    for i, weights in enumerate((w_query, w_key, w_value)):
        total = total + mm(joint_a[0, i * local : (i + 1) * local], weights[...], 0, 0)
    for k in range(1, 4):
        joint = joint_a[k] if k < 2 else joint_b[k - 2]
        total = total + mm(joint, rest_w[k - 1, :rows], 0, 0)
    out[...] = total.astype(low)


def grad_tokens_of(grad, joint_a, joint_b, weights, rest_w):
    return pl.pallas_call(
        grad_tokens_kernel,
        in_specs=[vmem()] * 7,
        out_specs=vmem(),
        out_shape=shaped(grad.shape, low),
        compiler_params=params(),
        cost_estimate=cost(4),
        name="grad_tokens",
    )(grad, joint_a, joint_b, *weights, rest_w)


def gather_rows(info, refs, target):
    for s in range(2):
        first, second, third = refs[3 * s : 3 * s + 3]
        holder = info[1] ^ s
        rows = first.shape[0]
        moves = (0, 1 + holder, 2 - holder, 3)
        for move, view in zip(moves, (first, second, third.at[0], third.at[1])):
            start = pl.multiple_of((holder * 4 + (info[2] ^ move)) * rows, rows)
            target[pl.ds(start, rows), :] = view[...].astype(wide)


def finish_ffn_kernel(info, *refs):
    gather_rows(info, refs[:6], refs[6])


def finish_ffn(info, pieces):
    rows, cols = pieces[0].shape
    return pl.pallas_call(
        finish_ffn_kernel,
        in_specs=[smem()] + [vmem()] * 6,
        out_specs=vmem(),
        out_shape=shaped((GROUP * rows, cols), wide),
        compiler_params=params(),
        cost_estimate=cost(2),
        name="finish_ffn",
    )(info, *pieces)


def finish_attn_kernel(info, *refs):
    query, key, value, out, whole = refs[6:]
    gather_rows(info, refs[:6], whole)
    local = whole.shape[0] // 4
    query[...] = whole[:local]
    key[...] = whole[local : 2 * local]
    value[...] = whole[2 * local : 3 * local]
    out[...] = whole[3 * local :]


def finish_attn(info, pieces):
    rows, cols = pieces[0].shape
    size = GROUP * rows
    local = size // 4
    return pl.pallas_call(
        finish_attn_kernel,
        in_specs=[smem()] + [vmem()] * 6,
        out_specs=[vmem()] * 4,
        out_shape=[shaped((local, cols), wide)] * 4,
        scratch_shapes=[pltpu.VMEM((size, cols), wide)],
        compiler_params=params(),
        cost_estimate=cost(2),
        name="finish_attn",
    )(info, *pieces)


class Links:
    def __init__(self, dp_size, parts):
        self.dp_size, self.parts = dp_size, parts

    def move(self, array, partner):
        pairs = []
        for d in range(self.dp_size):
            for t in range(self.parts):
                to_d, to_t = partner(d, t)
                pairs.append((d * self.parts + t, to_d * self.parts + to_t))
        return lax.ppermute(array, ("dp", "tensor"), pairs)

    def bit(self, array, bit):
        return self.move(array, lambda d, t: (d ^ bit, t))

    def core(self, array):
        return self.bit(array, 1)

    def plane(self, array, step):
        return self.move(array, lambda d, t: (d ^ (2 if (d & 1) == step else 4), t))

    def line(self, array, step):
        return self.move(array, lambda d, t: (d, t ^ (1 if (d & 1) == step else 2)))


def add(left, right):
    return (left.astype(wide) + right.astype(wide)).astype(low)


def after(*values):
    return lax.optimization_barrier(values)


def per_device(
    dp_size,
    parts,
    tokens,
    page_lengths,
    w_query,
    b_query,
    w_key,
    w_value,
    b_value,
    w_out,
    b_out,
    ln1_gain,
    ln1_bias,
    w_up,
    b_up,
    w_down,
    b_down,
    ln2_gain,
    ln2_bias,
    cotangent,
):
    links = Links(dp_size, parts)
    me = lax.axis_index("tensor")
    place = lax.axis_index("dp") % GROUP
    core, quarter = place & 1, place >> 1
    is_odd = core == 1
    width = tokens.shape[1]
    local = w_query.shape[1]
    rows = width // GROUP
    length = lax.dynamic_slice_in_dim(page_lengths, me, 1, 0)
    info = jnp.concatenate([length, jnp.stack([core, quarter, me]).astype(jnp.int32)])
    attn_w = (w_query.T, w_key.T, w_value.T, w_out)
    piece = core * 4 + quarter

    def cut(array, index):
        return lax.dynamic_slice_in_dim(array, index * rows, rows, 0)

    a0 = lax.select_n(piece >> 1, *(cut(array, piece & 1) for array in attn_w))
    bias_own = jnp.concatenate([b_query, b_value, b_up])
    bias_rows = jnp.pad(bias_own, (0, 16 * width - bias_own.size)).reshape(16, width)
    u0, d0 = jnp.concatenate([cut(w_up, piece), bias_rows], axis=0), cut(w_down, piece)
    vec = jnp.stack([b_out, ln1_gain, ln1_bias, b_down, ln2_gain, ln2_bias, b_down, b_down])
    vec = vec.astype(wide)
    a1 = links.line(a0, 0)
    a1, u0, d0, tokens_in = after(a1, u0, d0, tokens)
    a2 = links.line(jnp.stack([a0, a1]), 1)
    u1 = links.line(u0, 0)
    own = list(attn_own(info, tokens_in, attn_w[:3], bias_own.astype(wide)[None, None]))
    a2, u1, own[2] = after(a2, u1, own[2])
    a3 = jnp.concatenate([a1[None], a2])
    a4 = links.plane(a3, 0)
    u2 = links.line(jnp.stack([u0, u1]), 1)
    a4, u2, d0 = after(a4, u2, d0)
    u3 = jnp.concatenate([u1[None], u2])
    bias_rest = u3[:, rows:].reshape(parts - 1, 16 * width)[:, : bias_own.size]
    near, far = bias_rest[0], bias_rest[1]
    bias = jnp.stack(
        [bias_own, jnp.where(is_odd, far, near), jnp.where(is_odd, near, far), bias_rest[2]]
    )
    bias = bias.astype(wide)[:, None]
    u3 = u3[:, :rows]
    a5 = links.plane(jnp.stack([a3, a4]), 1)
    u4 = links.plane(u3, 0)
    d1 = links.line(d0, 0)
    a5, u4, d1, bias = after(a5, u4, d1, bias)
    pieces_a = [a3, a4, a5] + [links.core(array) for array in (a3, a4, a5)]
    u5 = links.plane(jnp.stack([u3, u4]), 1)
    d2 = links.line(jnp.stack([d0, d1]), 1)
    qkv, attn_rest_w, ctx, lse, out_rest = attn_rest(info, tokens, bias, pieces_a)
    u5, d2, lse = after(u5, d2, lse)
    d3 = jnp.concatenate([d1[None], d2])
    pieces_u = [u3, u4, u5] + [links.core(array) for array in (u3, u4, u5)]
    d4 = links.plane(d3, 0)
    skip, normed_low, hat, inv = ffn_in(tokens, own[1], ctx, vec, w_out, out_rest)
    d4, inv, *pieces_u = after(d4, inv, *pieces_u)
    d5 = links.plane(jnp.stack([d3, d4]), 1)
    act, slope, up, mark = ffn_up(info, normed_low, bias, w_up, pieces_u, inv)
    d5, mark = after(d5, mark)
    pieces_d = [d3, d4, d5] + [links.core(array) for array in (d3, d4, d5)]
    output, grad_branch, branch_low, small, keep_d, send_d, down = ffn_down(
        info, act, skip, vec, cotangent, w_down, pieces_d, mark
    )
    rest = (qkv, ctx, lse)

    def plane_a(keep, got):
        return links.plane(add(keep[1], got[1]), 0), add(keep[0], got[0])

    def plane_b(kept, got):
        return links.plane(add(kept[1], got[1]), 1), add(kept[0], got[0])

    def line_a(kept, got):
        both = add(kept, got).reshape(2, parts // 2, rows, width)
        sent = jnp.where(is_odd, both[:, 1], both[1])
        return links.line(sent, 1), jnp.where(is_odd, both[:, 0], both[0])

    def line_b(kept, got):
        both = add(kept, got)
        return links.line(both[1], 0), both[0]

    def settle(kept, got):
        total = kept.astype(wide) + got.astype(wide)
        bit = GROUP
        while bit < dp_size:
            total = total + links.bit(total, bit)
            bit *= 2
        return total.astype(low)

    got_d = links.core(send_d)
    got_d, small = after(got_d, small)
    near_d, kept_d = plane_a(keep_d, got_d)
    grad_residual, residual_low, small, keep_u, send_u = ffn_back(
        info, branch_low, grad_branch, slope, normed_low, hat, inv, vec, small, (w_up, w_down), up, down
    )
    near_d, send_u, small = after(near_d, send_u, small)
    got_u = links.core(send_u)
    far_d, kept_d = plane_b(kept_d, near_d)
    small, joint_a, keep_a, send_a = attn_back(
        0, info, tokens, residual_low, small, w_out, own, out_rest, rest
    )
    got_u, far_d, send_a, small = after(got_u, far_d, send_a, small)
    near_u, kept_u = plane_a(keep_u, got_u)
    got_a = links.core(send_a)
    small, joint_b, keep_b, send_b = attn_back(
        2, info, tokens, residual_low, small, w_out, own, out_rest, rest
    )
    near_u, got_a, far_d, send_b, small, grad_residual = after(
        near_u, got_a, far_d, send_b, small, grad_residual
    )
    got_b = links.core(send_b)
    far_u, kept_u = plane_b(kept_u, near_u)
    line_d, kept_d = line_a(kept_d, far_d)
    grad_tokens = grad_tokens_of(grad_residual, joint_a, joint_b, attn_w[:3], attn_rest_w)
    got_b, far_u, line_d, grad_tokens, small = after(got_b, far_u, line_d, grad_tokens, small)
    keep_ab, got_ab = jnp.stack([keep_a, keep_b], axis=2), jnp.stack([got_a, got_b], axis=2)
    near_a, kept_a = plane_a(keep_ab, got_ab)
    line_u, kept_u = line_a(kept_u, far_u)
    last_d, kept_d = line_b(kept_d, line_d)
    near_a, line_u, last_d, small = after(near_a, line_u, last_d, small)
    far_a, kept_a = plane_b(kept_a, near_a)
    last_u, kept_u = line_b(kept_u, line_u)
    sum_d = settle(kept_d, last_d)
    d1 = links.plane(sum_d, 0)
    small = small + links.core(small)
    small_got = links.plane(small, 0)
    far_a, last_u, d1, small_got = after(far_a, last_u, d1, small_got)
    line, kept_a = line_a(kept_a.reshape(parts, rows, width), far_a.reshape(parts, rows, width))
    sum_u = settle(kept_u, last_u)
    u1 = links.plane(sum_u, 0)
    d2 = links.plane(jnp.stack([sum_d, d1]), 1)
    small = small + small_got
    small_got = links.plane(small, 1)
    line, u1, d2, small_got = after(line, u1, d2, small_got)
    last, kept_a = line_b(kept_a, line)
    u2 = links.plane(jnp.stack([sum_u, u1]), 1)
    held = [sum_d, d1, d2]
    pieces = held + [links.core(array) for array in held]
    small = small + small_got
    small_got = links.line(small, 0)
    last, u2, small_got, *pieces = after(last, u2, small_got, *pieces)
    sum_a = settle(kept_a, last)
    a1 = links.plane(sum_a, 0)
    grad_w_down = finish_ffn(info, pieces)
    held = [sum_u, u1, u2]
    pieces = held + [links.core(array) for array in held]
    small = small + small_got
    small_got = links.line(small, 1)
    a1, small_got, grad_w_down, *pieces = after(a1, small_got, grad_w_down, *pieces)
    a2 = links.plane(jnp.stack([sum_a, a1]), 1)
    small = small + small_got
    bit = GROUP
    while bit < dp_size:
        small = small + links.bit(small, bit)
        bit *= 2
    grad_w_up = finish_ffn(info, pieces)
    a2, grad_w_up = after(a2, grad_w_up)
    held = [sum_a, a1, a2]
    pieces = held + [links.core(array) for array in held]
    grad_w_query, grad_w_key, grad_w_value, grad_w_out = finish_attn(info, pieces)
    grad_w_query, grad_w_key, grad_w_value = grad_w_query.T, grad_w_key.T, grad_w_value.T
    pair = lax.dynamic_index_in_dim(small, 10 + me, 0, keepdims=False)
    grad_b_up = lax.dynamic_index_in_dim(small, 6 + me, 0, keepdims=False)
    return (
        output,
        grad_tokens,
        grad_w_query,
        pair[:local],
        grad_w_key,
        grad_w_value,
        pair[256 : 256 + local],
        grad_w_out,
        small[0],
        small[1],
        small[2],
        grad_w_up,
        grad_b_up,
        grad_w_down,
        small[3],
        small[4],
        small[5],
    )


def solution(mesh):
    columns, rows, both = P(None, "tensor"), P("tensor", None), P(("dp", "tensor"), None)
    share = P("tensor")
    return jax.shard_map(
        partial(per_device, mesh.shape["dp"], mesh.shape["tensor"]),
        mesh=mesh,
        in_specs=(
            both,
            P("dp"),
            columns,
            share,
            columns,
            columns,
            share,
            rows,
            P(),
            P(),
            P(),
            columns,
            share,
            rows,
            P(),
            P(),
            P(),
            both,
        ),
        out_specs=(
            both,
            both,
            columns,
            share,
            columns,
            columns,
            share,
            rows,
            P(),
            P(),
            P(),
            columns,
            share,
            rows,
            P(),
            P(),
            P(),
        ),
        check_vma=False,
    )
```

```python
from functools import partial

import jax
import jax.numpy as jnp
from jax import lax
from jax.experimental import pallas as pl
from jax.experimental.pallas import tpu as pltpu
from jax.sharding import PartitionSpec as P

HD = 64
SEQ = 512
GROUP = 8
LOG2E = 1.4426950408889634
TAIL_P = 0.39
TAIL = (
    0.23532521908406087,
    0.09138841455460205,
    0.6495593986198918,
    -0.6354002786931026,
    0.8866643698688825,
    -0.22753712513305413,
)

epsilon = 1e-12
masked_score = -1000000000.0
low = jnp.bfloat16
wide = jnp.float32
PEAK = 1.1e15
LIMIT = 12


def mm(left, right, left_dim, right_dim):
    return lax.dot_general(
        left, right, (((left_dim,), (right_dim,)), ((), ())), preferred_element_type=wide
    )


def vmem():
    return pl.BlockSpec(memory_space=pltpu.VMEM)


def smem():
    return pl.BlockSpec(memory_space=pltpu.SMEM)


def hbm():
    return pl.BlockSpec(memory_space=pl.ANY)


def cost(microseconds):
    return pl.CostEstimate(
        flops=int(microseconds * 1e-6 * PEAK), bytes_accessed=1 << 20, transcendentals=0
    )


def params(mebibytes=LIMIT):
    return pltpu.CompilerParams(vmem_limit_bytes=mebibytes << 20)


def shaped(shape, dtype):
    return jax.ShapeDtypeStruct(shape, dtype)


def masked_pad(length, seq):
    row = lax.broadcasted_iota(jnp.int32, (16, seq), 0)
    key = lax.broadcasted_iota(jnp.int32, (16, seq), 1)
    bias = jnp.where((row == 0) & (key >= length), masked_score, 0.0).astype(low)
    ones = jnp.where(row == 0, 1.0, 0.0).astype(low)
    return bias, ones


def as_column(row, ones):
    first = lax.broadcasted_iota(jnp.int32, (16, row.shape[1]), 0) == 0
    return mm(jnp.where(first, row, 0.0).astype(low), ones, 0, 0)


def group_forward(tokens, weights, bias, length, qkv_ref, ctx_ref, lse_ref):
    local = weights[0].shape[0]
    seq = tokens.shape[0]
    scale = HD**-0.5 * LOG2E
    key_pad, ones = masked_pad(length, seq)
    query = (mm(weights[0], tokens, 1, 1) + as_column(bias[:, :local], ones)).astype(low)
    key = mm(weights[1], tokens, 1, 1).astype(low)
    value = mm(weights[2], tokens, 1, 1) + as_column(bias[:, local : 2 * local], ones)
    value = value.astype(low)
    qkv_ref[:local] = query
    qkv_ref[local : 2 * local] = key
    qkv_ref[2 * local :] = value
    for h in range(local // HD):
        part = slice(h * HD, (h + 1) * HD)
        scores = mm(
            jnp.concatenate([key[part], key_pad], 0), jnp.concatenate([query[part], ones], 0), 0, 0
        )
        top = jnp.max(scores, axis=0, keepdims=True)
        probs = jnp.exp2((scores - top) * scale)
        total = jnp.sum(probs, axis=0, keepdims=True)
        context = mm(value[part], probs.astype(low), 1, 0)
        ctx_ref[part] = (context * (1.0 / total)).astype(low)
        lse_ref[h : h + 1] = top * scale + jnp.log2(total)


def gelu_parts(x):
    t = 1.0 / (1.0 + (TAIL_P * 0.5**0.5) * jnp.abs(x))
    poly = TAIL[-1]
    for factor in TAIL[-2::-1]:
        poly = poly * t + factor
    bell = jnp.exp2(x * x * (-0.5 * LOG2E))
    half = 0.5 * poly * t * bell
    cdf = jnp.where(x >= 0, 1.0 - half, half)
    return x * cdf, cdf + x * bell * (0.5 / jnp.pi) ** 0.5


def norm_parts(values):
    centred = values - jnp.mean(values, axis=1, keepdims=True)
    inverse = lax.rsqrt(jnp.mean(centred * centred, axis=1, keepdims=True) + epsilon)
    return centred * inverse, inverse


def norm_back(scaled, normal, inverse):
    return inverse * (
        scaled
        - jnp.mean(scaled, axis=1, keepdims=True)
        - normal * jnp.mean(scaled * normal, axis=1, keepdims=True)
    )


def assemble(info, refs, target, own=None):
    if own is not None:
        target[0] = own[...]
    skip = 1 if own is None else 0
    for s in range(2):
        first, second, third = refs[3 * s : 3 * s + 3]
        holder = info[1] ^ s
        order = (1 + holder, 2 - holder, 3)
        views = (first, second, third.at[0], third.at[1])
        for view, move in zip(views, (0,) + order):
            rows = view.shape[1]
            start = pl.multiple_of((holder * 4 + (info[2] ^ move)) * rows, rows)
            for entry, k in enumerate(order):
                target[k - skip, pl.ds(start, rows), :] = view[entry]


def place_pieces(info, scratch, keep_ref, send_ref, entry):
    rows = scratch.shape[0] // GROUP
    for s, target in enumerate((keep_ref, send_ref)):
        half = info[1] ^ s
        for q in range(4):
            move = info[2] ^ q
            x_bit, y_bit = move & 1, move >> 1
            a = jnp.where(half == 0, x_bit, y_bit)
            start = pl.multiple_of((half * 4 + q) * rows, rows)
            target[a, x_bit + y_bit - a, entry] = scratch[pl.ds(start, rows), :]


def attn_own_kernel(info, tokens, w_query, w_key, w_value, bias, qkv, ctx, lse):
    weights = (w_query[...], w_key[...], w_value[...])
    group_forward(tokens[...], weights, bias[0], info[0], qkv.at[0], ctx.at[0], lse.at[0])


def attn_own(info, tokens, weights, bias):
    local, seq = weights[0].shape[0], tokens.shape[0]
    return pl.pallas_call(
        attn_own_kernel,
        in_specs=[smem()] + [vmem()] * 5,
        out_specs=[vmem()] * 3,
        out_shape=[
            shaped((1, 3 * local, seq), low),
            shaped((1, local, seq), low),
            shaped((1, 8, seq), wide),
        ],
        compiler_params=params(),
        cost_estimate=cost(4),
        name="attn_own",
    )(info, tokens, *weights, bias)


def attn_rest_kernel(info, tokens, bias, *refs):
    qkv_out, whole, ctx, lse, out_w, weights, qkv, sems = refs[6:]
    others, local = ctx.shape[:2]
    assemble(info, refs[:6], weights)
    sent = [pltpu.make_async_copy(weights, whole, sems.at[others])]
    sent[0].start()
    out_w[...] = weights[:, 3 * local :]

    def group(k, _):
        joint = tuple(weights[k, i * local : (i + 1) * local] for i in range(3))
        group_forward(
            tokens[...], joint, bias[k + 1], info[0], qkv.at[k], ctx.at[k], lse.at[k]
        )
        pltpu.make_async_copy(qkv.at[k], qkv_out.at[k], sems.at[k]).start()
        return 0

    lax.fori_loop(0, others, group, 0)
    sent += [pltpu.make_async_copy(qkv.at[k], qkv_out.at[k], sems.at[k]) for k in range(others)]
    for copy in sent:
        copy.wait()


def attn_rest(info, tokens, bias, pieces):
    others, rows, cols = pieces[0].shape
    size, seq = rows * GROUP, tokens.shape[0]
    local = size // 4
    joint, whole = (others, 3 * local, seq), (others, size, cols)
    return pl.pallas_call(
        attn_rest_kernel,
        in_specs=[smem()] + [vmem()] * 8,
        out_specs=[pl.BlockSpec(memory_space=pltpu.HBM)] * 2 + [vmem()] * 3,
        out_shape=[
            shaped(joint, low),
            shaped(whole, low),
            shaped((others, local, seq), low),
            shaped((others, 8, seq), wide),
            shaped((others, local, cols), low),
        ],
        scratch_shapes=[
            pltpu.VMEM(whole, low),
            pltpu.VMEM(joint, low),
            pltpu.SemaphoreType.DMA((others + 1,)),
        ],
        compiler_params=params(),
        cost_estimate=cost(8),
        name="attn_rest",
    )(info, tokens, bias, *pieces)


def ffn_in_kernel(tokens, ctx_own, ctx_rest, vec, out_own, out_rest, skip, normed_ref, hat_ref, inv_ref):
    others = ctx_rest.shape[0]
    rows = vec[...]
    b_out, gain_one, bias_one, b_down = (rows[i : i + 1] for i in range(4))
    attended = mm(ctx_own[0], out_own[...], 0, 0)
    for k in range(others):
        attended = attended + mm(ctx_rest[k], out_rest[k], 0, 0)
    hat, inv = norm_parts(tokens[...].astype(wide) + attended + b_out)
    hat_ref[...] = hat
    inv_ref[...] = jnp.broadcast_to(inv, inv_ref.shape)
    normed = hat * gain_one + bias_one
    normed_ref[...] = normed.astype(low)
    skip[...] = normed + b_down


def ffn_in(tokens, ctx_own, ctx_rest, vec, out_own, out_rest):
    seq, width = tokens.shape
    others, local = ctx_rest.shape[:2]
    return pl.pallas_call(
        ffn_in_kernel,
        in_specs=[vmem()] * 6,
        out_specs=[vmem()] * 4,
        out_shape=[
            shaped((seq, width), wide),
            shaped((seq, width), low),
            shaped((seq, width), wide),
            shaped((seq, 128), wide),
        ],
        compiler_params=params(),
        cost_estimate=cost(5),
        name="ffn_in",
    )(tokens, ctx_own, ctx_rest, vec, out_own, out_rest)


def ffn_up_kernel(info, normed, bias, up_own, *refs):
    _, act, slope, up, mark = refs[6:]
    size = up.shape[2]
    first = bias.shape[2] - size
    mark[...] = jnp.zeros(mark.shape, wide)
    assemble(info, refs[:6], up, up_own)

    def forward(k, _):
        preact = mm(normed[...], up[k], 1, 0) + bias[k][:, first:].astype(wide)
        value, derivative = gelu_parts(preact)
        act[k] = value.astype(low)
        slope[k] = derivative.astype(low)
        return 0

    lax.fori_loop(0, act.shape[0], forward, 0)


def ffn_up(info, normed, bias, up_own, pieces, mark):
    seq, width = normed.shape
    others, size = pieces[0].shape[0], up_own.shape[1]
    return pl.pallas_call(
        ffn_up_kernel,
        in_specs=[smem()] + [vmem()] * (3 + 6) + [hbm()],
        out_specs=[vmem()] * 4,
        out_shape=[
            shaped((others + 1, seq, size), low),
            shaped((others + 1, seq, size), low),
            shaped((others + 1, width, size), low),
            shaped((8, 128), wide),
        ],
        compiler_params=params(),
        cost_estimate=cost(11),
        name="ffn_up",
    )(info, normed, bias, up_own, *pieces, mark)


def ffn_down_kernel(info, skip, vec, cot, act, down_own, *refs):
    _, out, grad_ref, branch_ref, small, keep, send, down, scratch = refs[6:]
    parts = act.shape[0]
    assemble(info, refs[:6], down, down_own)
    grad_ref[...] = skip[...]

    def branch(k, _):
        grad_ref[...] += mm(act[k], down[k], 1, 0)
        return 0

    lax.fori_loop(0, parts, branch, 0)
    total = grad_ref[...]
    gain_two, bias_two = vec[4:5], vec[5:6]
    hat_two, inv_two = norm_parts(total)
    out[...] = (hat_two * gain_two + bias_two).astype(low)
    grad = cot[...].astype(wide)
    grad_branch = norm_back(grad * gain_two, hat_two, inv_two)
    grad_ref[...] = grad_branch
    branch_low = grad_branch.astype(low)
    branch_ref[...] = branch_low
    small[...] = jnp.zeros(small.shape, wide)
    small[3:4] = jnp.sum(grad_branch, axis=0, keepdims=True)
    small[4:5] = jnp.sum(grad * hat_two, axis=0, keepdims=True)
    small[5:6] = jnp.sum(grad, axis=0, keepdims=True)

    def weight(k, _):
        scratch[...] = mm(act[k], branch_ref[...], 0, 0).astype(low)
        place_pieces(info, scratch, keep, send, k)
        return 0

    lax.fori_loop(0, parts, weight, 0)


def halves_shape(entries, rows, cols):
    return (2, 2, entries, rows // GROUP, cols)


def ffn_down(info, act, skip, vec, cot, down_own, pieces, mark):
    parts, seq, size = act.shape
    width = skip.shape[1]
    half = halves_shape(parts, size, width)
    return pl.pallas_call(
        ffn_down_kernel,
        in_specs=[smem()] + [vmem()] * (5 + 6) + [hbm()],
        out_specs=[vmem()] * 7,
        out_shape=[
            shaped((seq, width), low),
            shaped((seq, width), wide),
            shaped((seq, width), low),
            shaped((16, width), wide),
            shaped(half, low),
            shaped(half, low),
            shaped((parts, size, width), low),
        ],
        scratch_shapes=[pltpu.VMEM((size, width), low)],
        compiler_params=params(),
        cost_estimate=cost(12),
        name="ffn_down",
    )(info, skip, vec, cot, act, down_own, *pieces, mark)


def ffn_back_kernel(
    info, branch_low, grad_branch, normed_low, hat_ref, inv_ref, vec, small_in, slope, up, down,
    grad_ref, residual_ref, small, keep, send, turned, total, scratch,
):
    parts = slope.shape[0]
    index = lax.broadcasted_iota(jnp.int32, small.shape, 0)
    small[...] = small_in[...]
    total[...] = grad_branch[...]
    turned[...] = normed_low[...].T

    def backward(k, _):
        grad_pre = mm(branch_low[...], down[k], 1, 1) * slope[k].astype(wide)
        grad_pre = grad_pre.astype(low)
        sums = jnp.sum(grad_pre.astype(wide), axis=0, keepdims=True)
        small[...] = jnp.where(index == 6 + (info[3] ^ k), sums, small[...])
        scratch[...] = mm(turned[...], grad_pre, 1, 0).astype(low)
        place_pieces(info, scratch, keep, send, k)
        total[...] += mm(grad_pre, up[k], 1, 1)
        return 0

    lax.fori_loop(0, parts, backward, 0)
    grad_normed = total[...]
    hat = hat_ref[...]
    grad_residual = norm_back(grad_normed * vec[1:2], hat, inv_ref[:, :1])
    grad_ref[...] = grad_residual
    residual_ref[...] = grad_residual.astype(low)
    small[0:1] = jnp.sum(grad_residual, axis=0, keepdims=True)
    small[1:2] = jnp.sum(grad_normed * hat, axis=0, keepdims=True)
    small[2:3] = jnp.sum(grad_normed, axis=0, keepdims=True)


def ffn_back(info, branch_low, grad_branch, slope, normed_low, hat, inv, vec, small, up, down):
    _, width, size = up.shape
    parts, seq = slope.shape[:2]
    half = halves_shape(parts, width, size)
    return pl.pallas_call(
        ffn_back_kernel,
        in_specs=[smem()] + [vmem()] * 10,
        out_specs=[vmem()] * 5,
        out_shape=[
            shaped((seq, width), wide),
            shaped((seq, width), low),
            shaped((16, width), wide),
            shaped(half, low),
            shaped(half, low),
        ],
        scratch_shapes=[
            pltpu.VMEM((width, seq), low),
            pltpu.VMEM((seq, width), wide),
            pltpu.VMEM((width, size), low),
        ],
        compiler_params=params(),
        cost_estimate=cost(11),
        name="ffn_back",
    )(info, branch_low, grad_branch, normed_low, hat, inv, vec, small, slope, up, down)


def attn_back_kernel(first, info, tokens, residual_low, small_in, *refs):
    groups = (refs[:4], refs[4:8])
    small, joint, keep, send, scratch = refs[8:]
    local = groups[0][2].shape[1]
    seq, width = tokens.shape
    scale = HD**-0.5
    index = lax.broadcasted_iota(jnp.int32, small.shape, 0)
    small[...] = small_in[...]
    key_pad, query_pad = masked_pad(info[0], seq)
    ones = jnp.ones((8, seq), low)
    for i, (out_w, qkv_ref, ctx_ref, lse_ref) in enumerate(groups):
        k = first + i
        out_rows = out_w[...] if k == 0 else out_w[k - 1]
        qkv, ctx, lse = (ref.at[max(k - 1, 0)] for ref in (qkv_ref, ctx_ref, lse_ref))
        grad_ctx = mm(out_rows, residual_low[...], 1, 1).astype(low)
        for h in range(local // HD):
            lo, hi = h * HD, (h + 1) * HD
            query = qkv[lo:hi]
            key = qkv[local + lo : local + hi]
            value = qkv[2 * local + lo : 2 * local + hi]
            grad_head = grad_ctx[lo:hi]
            scores = mm(
                jnp.concatenate([key, key_pad], 0), jnp.concatenate([query, query_pad], 0), 0, 0
            )
            probs = jnp.exp2(scores * (scale * LOG2E) - lse[h : h + 1])
            grad_probs = mm(value, grad_head, 0, 0)
            product = probs * grad_probs
            grad_scores = (product - probs * jnp.sum(product, axis=0, keepdims=True)).astype(low)
            joint[i, lo:hi] = (mm(key, grad_scores, 1, 0) * scale).astype(low)
            joint[i, local + lo : local + hi] = (mm(query, grad_scores, 1, 1) * scale).astype(low)
            joint[i, 2 * local + lo : 2 * local + hi] = mm(
                grad_head, probs.astype(low), 1, 1
            ).astype(low)
        grads = joint[i]
        sums = mm(ones, grads, 1, 1)[:1]
        gap = jnp.zeros((1, 256 - local), wide)
        rest = jnp.zeros((1, width - 512), wide)
        sums = jnp.concatenate([sums[:, :local], gap, sums[:, 2 * local :], gap, rest], 1)
        small[...] = jnp.where(index == 10 + (info[3] ^ (first + i)), sums, small[...])
        scratch[: 3 * local] = mm(grads, tokens[...], 1, 0).astype(low)
        scratch[3 * local :] = mm(ctx[...], residual_low[...], 1, 0).astype(low)
        place_pieces(info, scratch, keep, send, i)


def attn_back(first, info, tokens, residual_low, small, out_own, own, out_rest, rest):
    seq, width = tokens.shape
    local = out_own.shape[0]
    arrays = []
    for k in (first, first + 1):
        arrays += (out_own,) + tuple(own) if k == 0 else (out_rest,) + tuple(rest)
    half = halves_shape(2, 4 * local, width)
    return pl.pallas_call(
        partial(attn_back_kernel, first),
        in_specs=[smem()] + [vmem()] * 11,
        out_specs=[vmem()] * 4,
        out_shape=[
            shaped((16, width), wide),
            shaped((2, 3 * local, seq), low),
            shaped(half, low),
            shaped(half, low),
        ],
        scratch_shapes=[pltpu.VMEM((4 * local, width), low)],
        compiler_params=params(),
        cost_estimate=cost(9),
        name="attn_back",
    )(info, tokens, residual_low, small, *arrays)


def grad_tokens_kernel(grad, joint_a, joint_b, w_query, w_key, w_value, rest_w, out):
    local, rows = w_query.shape[0], joint_a.shape[1]
    total = grad[...]
    for i, weights in enumerate((w_query, w_key, w_value)):
        total = total + mm(joint_a[0, i * local : (i + 1) * local], weights[...], 0, 0)
    for k in range(1, 4):
        joint = joint_a[k] if k < 2 else joint_b[k - 2]
        total = total + mm(joint, rest_w[k - 1, :rows], 0, 0)
    out[...] = total.astype(low)


def grad_tokens_of(grad, joint_a, joint_b, weights, rest_w):
    return pl.pallas_call(
        grad_tokens_kernel,
        in_specs=[vmem()] * 7,
        out_specs=vmem(),
        out_shape=shaped(grad.shape, low),
        compiler_params=params(),
        cost_estimate=cost(4),
        name="grad_tokens",
    )(grad, joint_a, joint_b, *weights, rest_w)


def finish_ffn_kernel(info, held, held_mates, corner, corner_mate, down, up):
    rows = corner.shape[1]
    for s, (pieces, last) in enumerate(((held, corner), (held_mates, corner_mate))):
        holder = info[1] ^ s
        for move in range(4):
            source = last if move == 3 else pieces.at[move]
            start = pl.multiple_of((holder * 4 + (info[2] ^ move)) * rows, rows)
            down[pl.ds(start, rows), :] = source[0].astype(wide)
            up[pl.ds(start, rows), :] = source[1].astype(wide)


def finish_ffn(info, *pieces):
    _, rows, cols = pieces[-1].shape
    return pl.pallas_call(
        finish_ffn_kernel,
        in_specs=[smem()] + [vmem()] * 4,
        out_specs=[vmem()] * 2,
        out_shape=[shaped((GROUP * rows, cols), wide)] * 2,
        compiler_params=params(),
        cost_estimate=cost(3),
        name="finish_ffn",
    )(info, *pieces)


def finish_attn_kernel(info, *refs):
    query, key, value, out, whole = refs[8:]
    for s in range(2):
        holder = info[1] ^ s
        for move in range(4):
            view = refs[4 * s + move]
            rows = view.shape[0]
            start = pl.multiple_of((holder * 4 + (info[2] ^ move)) * rows, rows)
            whole[pl.ds(start, rows), :] = view[...].astype(wide)
    local = whole.shape[0] // 4
    query[...] = whole[:local]
    key[...] = whole[local : 2 * local]
    value[...] = whole[2 * local : 3 * local]
    out[...] = whole[3 * local :]


def finish_attn(info, pieces):
    rows, cols = pieces[0].shape
    size = GROUP * rows
    local = size // 4
    return pl.pallas_call(
        finish_attn_kernel,
        in_specs=[smem()] + [vmem()] * 8,
        out_specs=[vmem()] * 4,
        out_shape=[shaped((local, cols), wide)] * 4,
        scratch_shapes=[pltpu.VMEM((size, cols), wide)],
        compiler_params=params(),
        cost_estimate=cost(2),
        name="finish_attn",
    )(info, *pieces)


class Links:
    def __init__(self, dp_size, parts):
        self.dp_size, self.parts = dp_size, parts

    def move(self, array, partner):
        pairs = []
        for d in range(self.dp_size):
            for t in range(self.parts):
                to_d, to_t = partner(d, t)
                pairs.append((d * self.parts + t, to_d * self.parts + to_t))
        return lax.ppermute(array, ("dp", "tensor"), pairs)

    def bit(self, array, bit):
        return self.move(array, lambda d, t: (d ^ bit, t))

    def core(self, array):
        return self.bit(array, 1)

    def plane(self, array, step):
        return self.move(array, lambda d, t: (d ^ (2 if (d & 1) == step else 4), t))

    def everywhere(self, array, bits):
        return [self.bit(array, bit) for bit in bits]

    def across(self, array, k):
        return self.move(array, lambda d, t: (d, t ^ k))

    def line(self, array, step):
        return self.move(array, lambda d, t: (d, t ^ (1 if (d & 1) == step else 2)))


def add(left, right):
    return (left.astype(wide) + right.astype(wide)).astype(low)


def after(*values):
    return lax.optimization_barrier(values)


def per_device(
    dp_size,
    parts,
    tokens,
    page_lengths,
    w_query,
    b_query,
    w_key,
    w_value,
    b_value,
    w_out,
    b_out,
    ln1_gain,
    ln1_bias,
    w_up,
    b_up,
    w_down,
    b_down,
    ln2_gain,
    ln2_bias,
    cotangent,
):
    links = Links(dp_size, parts)
    me = lax.axis_index("tensor")
    place = lax.axis_index("dp") % GROUP
    core, quarter = place & 1, place >> 1
    is_odd = core == 1
    width = tokens.shape[1]
    local = w_query.shape[1]
    rows = width // GROUP
    length = lax.dynamic_slice_in_dim(page_lengths, me, 1, 0)
    info = jnp.concatenate([length, jnp.stack([core, quarter, me]).astype(jnp.int32)])
    attn_w = (w_query.T, w_key.T, w_value.T, w_out)
    piece = core * 4 + quarter

    def cut(array, index):
        return lax.dynamic_slice_in_dim(array, index * rows, rows, 0)

    a0 = lax.select_n(piece >> 1, *(cut(array, piece & 1) for array in attn_w))
    bias_own = jnp.concatenate([b_query, b_value, b_up])
    bias_rows = jnp.pad(bias_own, (0, 8 * width - bias_own.size)).reshape(8, width)
    a0, piece_d = after(a0, piece)
    d0 = cut(w_down, piece_d)
    u0 = jnp.concatenate([cut(w_up, piece), bias_rows], axis=0)
    vec = jnp.stack([b_out, ln1_gain, ln1_bias, b_down, ln2_gain, ln2_bias, b_down, b_down])
    vec = vec.astype(wide)
    a1, d1 = links.line(a0, 0), links.line(d0, 0)
    a1, d1, u0, vec, tokens_in = after(a1, d1, u0, vec, tokens)
    a2 = links.line(jnp.stack([a0, a1]), 1)
    u1 = links.line(u0, 0)
    own = list(attn_own(info, tokens_in, attn_w[:3], bias_own.astype(wide)[None, None]))
    a2, u1, own[2] = after(a2, u1, own[2])
    a3 = jnp.concatenate([a1[None], a2])
    a4 = links.plane(a3, 0)
    u2 = links.line(jnp.stack([u0, u1]), 1)
    a4, u2, d1 = after(a4, u2, d1)
    u3 = jnp.concatenate([u1[None], u2])
    bias_rest = u3[:, rows:].reshape(parts - 1, 8 * width)[:, : bias_own.size]
    near, far = bias_rest[0], bias_rest[1]
    bias = jnp.stack(
        [bias_own, jnp.where(is_odd, far, near), jnp.where(is_odd, near, far), bias_rest[2]]
    )
    bias = bias.astype(wide)[:, None]
    u3 = u3[:, :rows]
    a5 = links.plane(jnp.stack([a3, a4]), 1)
    u4 = links.plane(u3, 0)
    d2 = links.line(jnp.stack([d0, d1]), 1)
    a5, u4, d2, bias = after(a5, u4, d2, bias)
    d3 = jnp.concatenate([d1[None], d2])
    pieces_a = [a3, a4, a5] + [links.core(array) for array in (a3, a4, a5)]
    u5 = links.plane(jnp.stack([u3, u4]), 1)
    d4 = links.plane(d3, 0)
    qkv, attn_rest_w, ctx, lse, out_rest = attn_rest(info, tokens, bias, pieces_a)
    skip, normed_low, hat, inv = ffn_in(tokens, own[1], ctx, vec, w_out, out_rest)
    u5, d4, lse, inv = after(u5, d4, lse, inv)
    pieces_u = [u3, u4, u5] + [links.core(array) for array in (u3, u4, u5)]
    d5 = links.plane(jnp.stack([d3, d4]), 1)
    act, slope, up, mark = ffn_up(info, normed_low, bias, w_up, pieces_u, inv)
    d5, mark = after(d5, mark)
    pieces_d = [d3, d4, d5] + [links.core(array) for array in (d3, d4, d5)]
    output, grad_branch, branch_low, small, keep_d, send_d, down = ffn_down(
        info, act, skip, vec, cotangent, w_down, pieces_d, mark
    )
    rest = (qkv, ctx, lse)

    def plane_a(keep, got):
        return links.plane(add(keep[1], got[1]), 0), add(keep[0], got[0])

    def plane_b(kept, got):
        return links.plane(add(kept[1], got[1]), 1), add(kept[0], got[0])

    def line_a(both):
        both = both.reshape(-1, 2, parts // 2, rows, width)
        sent = jnp.where(is_odd, both[:, :, 1], both[:, 1])
        return links.line(sent, 1), jnp.where(is_odd, both[:, :, 0], both[:, 0])

    def line_b(kept, got):
        both = add(kept, got)
        return links.line(both[:, 1], 0), both[:, 0]

    def settle(kept, got):
        total = kept.astype(wide) + got.astype(wide)
        bit = GROUP
        while bit < dp_size:
            total = total + links.bit(total, bit)
            bit *= 2
        return total.astype(low)

    def mates(held):
        return held + [links.core(array) for array in held]

    got_d = links.core(send_d)
    got_d, small = after(got_d, small)
    near_d, kept_d = plane_a(keep_d, got_d)
    grad_residual, residual_low, small, keep_u, send_u = ffn_back(
        info, branch_low, grad_branch, slope, normed_low, hat, inv, vec, small, up, down
    )
    near_d, send_u, small = after(near_d, send_u, small)
    got_u = links.core(send_u)
    far_d, kept_d = plane_b(kept_d, near_d)
    small, joint_a, keep_a, send_a = attn_back(
        0, info, tokens, residual_low, small, w_out, own, out_rest, rest
    )
    got_u, far_d, send_a, small = after(got_u, far_d, send_a, small)
    near_u, kept_u = plane_a(keep_u, got_u)
    got_a = links.core(send_a)
    line_d, kept_d = line_a(add(kept_d, far_d))
    small, joint_b, keep_b, send_b = attn_back(
        2, info, tokens, residual_low, small, w_out, own, out_rest, rest
    )
    near_u, got_a, line_d, send_b, small, grad_residual = after(
        near_u, got_a, line_d, send_b, small, grad_residual
    )
    got_b = links.core(send_b)
    far_u, kept_u = plane_b(kept_u, near_u)
    last_d, kept_d = line_b(kept_d, line_d)
    grad_tokens = grad_tokens_of(grad_residual, joint_a, joint_b, attn_w[:3], attn_rest_w)
    small_got = links.core(small)
    got_b, far_u, last_d, grad_tokens, small_got = after(got_b, far_u, last_d, grad_tokens, small_got)
    small = small + small_got
    size = parts * 2 * rows

    def joined(share, small):
        return jnp.concatenate([share.reshape(-1, width), small.astype(low)], axis=0)

    keep_ab, got_ab = jnp.stack([keep_a, keep_b], axis=2), jnp.stack([got_a, got_b], axis=2)
    near_a = links.plane(joined(add(keep_ab[1], got_ab[1]), small), 0)
    kept_a = add(keep_ab[0], got_ab[0])
    line_u, kept_u = line_a(add(kept_u, far_u))
    near_a, line_u = after(near_a, line_u)
    small = small + near_a[size:].astype(wide)
    near_a = near_a[:size].reshape(kept_a.shape)
    far_a = links.plane(joined(add(kept_a[1], near_a[1]), small), 1)
    kept_a = add(kept_a[0], near_a[0])
    last_u, kept_u = line_b(kept_u, line_u)
    far_a, last_u = after(far_a, last_u)
    size = parts * rows
    small = small + far_a[size:].astype(wide)
    share = add(kept_a, far_a[:size].reshape(kept_a.shape)).reshape(parts, rows, width)
    across = [links.across(joined(share[k], small), k) for k in range(parts - 1, 0, -1)]
    sum_f = jnp.stack([settle(kept_d, last_d)[0], settle(kept_u, last_u)[0]])
    f_x, f_y = links.everywhere(sum_f, (2, 4))
    across, f_x, f_y = after(across, f_x, f_y)
    sum_a = share[0].astype(wide)
    for array in across:
        sum_a = sum_a + array[:rows].astype(wide)
        small = small + array[rows:].astype(wide)
    bit = GROUP
    while bit < dp_size:
        sum_a = sum_a + links.bit(sum_a, bit)
        small = small + links.bit(small, bit)
        bit *= 2
    sum_a = sum_a.astype(low)
    around = links.everywhere(sum_a, (2, 4, 6))
    f_xy = links.plane(jnp.where(is_odd, f_x, f_y), 0)
    held = jnp.stack([sum_f, f_x, f_y])
    held_mates = links.core(held)
    pair = lax.dynamic_index_in_dim(small, 10 + me, 0, keepdims=False)
    grad_b_up = lax.dynamic_index_in_dim(small, 6 + me, 0, keepdims=False)
    around, small, pair, grad_b_up, f_xy, held_mates = after(
        around, small, pair, grad_b_up, f_xy, held_mates
    )
    grad_w_down, grad_w_up = finish_ffn(info, held, held_mates, f_xy, links.core(f_xy))
    grad_w_query, grad_w_key, grad_w_value, grad_w_out = finish_attn(info, mates([sum_a] + around))
    grad_w_query, grad_w_key, grad_w_value = grad_w_query.T, grad_w_key.T, grad_w_value.T
    return (
        output,
        grad_tokens,
        grad_w_query,
        pair[:local],
        grad_w_key,
        grad_w_value,
        pair[256 : 256 + local],
        grad_w_out,
        small[0],
        small[1],
        small[2],
        grad_w_up,
        grad_b_up,
        grad_w_down,
        small[3],
        small[4],
        small[5],
    )


def solution(mesh):
    columns, rows, both = P(None, "tensor"), P("tensor", None), P(("dp", "tensor"), None)
    share = P("tensor")
    return jax.shard_map(
        partial(per_device, mesh.shape["dp"], mesh.shape["tensor"]),
        mesh=mesh,
        in_specs=(
            both,
            P("dp"),
            columns,
            share,
            columns,
            columns,
            share,
            rows,
            P(),
            P(),
            P(),
            columns,
            share,
            rows,
            P(),
            P(),
            P(),
            both,
        ),
        out_specs=(
            both,
            both,
            columns,
            share,
            columns,
            columns,
            share,
            rows,
            P(),
            P(),
            P(),
            columns,
            share,
            rows,
            P(),
            P(),
            P(),
        ),
        check_vma=False,
    )
```

```python
from functools import partial

import jax
import jax.numpy as jnp
from jax import lax
from jax.experimental import pallas as pl
from jax.experimental.pallas import tpu as pltpu
from jax.sharding import PartitionSpec as P

HD = 64
SEQ = 512
GROUP = 8
LOG2E = 1.4426950408889634
TAIL_P = 0.39
TAIL = (
    0.23532521908406087,
    0.09138841455460205,
    0.6495593986198918,
    -0.6354002786931026,
    0.8866643698688825,
    -0.22753712513305413,
)

epsilon = 1e-12
masked_score = -1000000000.0
low = jnp.bfloat16
wide = jnp.float32
PEAK = 1.1e15
LIMIT = 12


def mm(left, right, left_dim, right_dim):
    return lax.dot_general(
        left, right, (((left_dim,), (right_dim,)), ((), ())), preferred_element_type=wide
    )


def vmem():
    return pl.BlockSpec(memory_space=pltpu.VMEM)


def smem():
    return pl.BlockSpec(memory_space=pltpu.SMEM)


def hbm():
    return pl.BlockSpec(memory_space=pl.ANY)


def cost(microseconds):
    return pl.CostEstimate(
        flops=int(microseconds * 1e-6 * PEAK), bytes_accessed=1 << 20, transcendentals=0
    )


def params(mebibytes=LIMIT):
    return pltpu.CompilerParams(vmem_limit_bytes=mebibytes << 20)


def shaped(shape, dtype):
    return jax.ShapeDtypeStruct(shape, dtype)


def masked_pad(length, seq):
    row = lax.broadcasted_iota(jnp.int32, (16, seq), 0)
    key = lax.broadcasted_iota(jnp.int32, (16, seq), 1)
    bias = jnp.where((row == 0) & (key >= length), masked_score, 0.0).astype(low)
    ones = jnp.where(row == 0, 1.0, 0.0).astype(low)
    return bias, ones


def as_column(row, ones):
    first = lax.broadcasted_iota(jnp.int32, (16, row.shape[1]), 0) == 0
    return mm(jnp.where(first, row, 0.0).astype(low), ones, 0, 0)


def group_forward(tokens, weights, bias, length, qkv_ref, ctx_ref, lse_ref):
    local = weights[0].shape[0]
    seq = tokens.shape[0]
    scale = HD**-0.5 * LOG2E
    key_pad, ones = masked_pad(length, seq)
    query = (mm(weights[0], tokens, 1, 1) + as_column(bias[:, :local], ones)).astype(low)
    key = mm(weights[1], tokens, 1, 1).astype(low)
    value = mm(weights[2], tokens, 1, 1) + as_column(bias[:, local : 2 * local], ones)
    value = value.astype(low)
    qkv_ref[:local] = query
    qkv_ref[local : 2 * local] = key
    qkv_ref[2 * local :] = value
    for h in range(local // HD):
        part = slice(h * HD, (h + 1) * HD)
        scores = mm(
            jnp.concatenate([key[part], key_pad], 0), jnp.concatenate([query[part], ones], 0), 0, 0
        )
        top = jnp.max(scores, axis=0, keepdims=True)
        probs = jnp.exp2((scores - top) * scale)
        total = jnp.sum(probs, axis=0, keepdims=True)
        context = mm(value[part], probs.astype(low), 1, 0)
        ctx_ref[part] = (context * (1.0 / total)).astype(low)
        lse_ref[h : h + 1] = top * scale + jnp.log2(total)


def gelu_parts(x):
    t = 1.0 / (1.0 + (TAIL_P * 0.5**0.5) * jnp.abs(x))
    poly = TAIL[-1]
    for factor in TAIL[-2::-1]:
        poly = poly * t + factor
    bell = jnp.exp2(x * x * (-0.5 * LOG2E))
    half = 0.5 * poly * t * bell
    cdf = jnp.where(x >= 0, 1.0 - half, half)
    return x * cdf, cdf + x * bell * (0.5 / jnp.pi) ** 0.5


def norm_parts(values):
    centred = values - jnp.mean(values, axis=1, keepdims=True)
    inverse = lax.rsqrt(jnp.mean(centred * centred, axis=1, keepdims=True) + epsilon)
    return centred * inverse, inverse


def norm_back(scaled, normal, inverse):
    return inverse * (
        scaled
        - jnp.mean(scaled, axis=1, keepdims=True)
        - normal * jnp.mean(scaled * normal, axis=1, keepdims=True)
    )


def assemble(info, refs, target, own=None):
    if own is not None:
        target[0] = own[...]
    skip = 1 if own is None else 0
    for s in range(2):
        first, second, third = refs[3 * s : 3 * s + 3]
        holder = info[1] ^ s
        order = (1 + holder, 2 - holder, 3)
        views = (first, second, third.at[0], third.at[1])
        for view, move in zip(views, (0,) + order):
            rows = view.shape[1]
            start = pl.multiple_of((holder * 4 + (info[2] ^ move)) * rows, rows)
            for entry, k in enumerate(order):
                target[k - skip, pl.ds(start, rows), :] = view[entry]


def place_pieces(info, scratch, keep_ref, send_ref, entry):
    rows = scratch.shape[0] // GROUP
    for s, target in enumerate((keep_ref, send_ref)):
        half = info[1] ^ s
        for q in range(4):
            move = info[2] ^ q
            x_bit, y_bit = move & 1, move >> 1
            a = jnp.where(half == 0, x_bit, y_bit)
            start = pl.multiple_of((half * 4 + q) * rows, rows)
            target[a, x_bit + y_bit - a, entry] = scratch[pl.ds(start, rows), :]


def attn_own_kernel(info, tokens, w_query, w_key, w_value, bias, qkv, ctx, lse):
    weights = (w_query[...], w_key[...], w_value[...])
    group_forward(tokens[...], weights, bias[0], info[0], qkv.at[0], ctx.at[0], lse.at[0])


def attn_own(info, tokens, weights, bias):
    local, seq = weights[0].shape[0], tokens.shape[0]
    return pl.pallas_call(
        attn_own_kernel,
        in_specs=[smem()] + [vmem()] * 5,
        out_specs=[vmem()] * 3,
        out_shape=[
            shaped((1, 3 * local, seq), low),
            shaped((1, local, seq), low),
            shaped((1, 8, seq), wide),
        ],
        compiler_params=params(),
        cost_estimate=cost(4),
        name="attn_own",
    )(info, tokens, *weights, bias)


def attn_rest_kernel(info, tokens, bias, *refs):
    qkv_out, whole, ctx, lse, out_w, weights, qkv, sems = refs[6:]
    others, local = ctx.shape[:2]
    assemble(info, refs[:6], weights)
    sent = [pltpu.make_async_copy(weights, whole, sems.at[others])]
    sent[0].start()
    out_w[...] = weights[:, 3 * local :]

    def group(k, _):
        joint = tuple(weights[k, i * local : (i + 1) * local] for i in range(3))
        group_forward(
            tokens[...], joint, bias[k + 1], info[0], qkv.at[k], ctx.at[k], lse.at[k]
        )
        pltpu.make_async_copy(qkv.at[k], qkv_out.at[k], sems.at[k]).start()
        return 0

    lax.fori_loop(0, others, group, 0)
    sent += [pltpu.make_async_copy(qkv.at[k], qkv_out.at[k], sems.at[k]) for k in range(others)]
    for copy in sent:
        copy.wait()


def attn_rest(info, tokens, bias, pieces):
    others, rows, cols = pieces[0].shape
    size, seq = rows * GROUP, tokens.shape[0]
    local = size // 4
    joint, whole = (others, 3 * local, seq), (others, size, cols)
    return pl.pallas_call(
        attn_rest_kernel,
        in_specs=[smem()] + [vmem()] * 8,
        out_specs=[pl.BlockSpec(memory_space=pltpu.HBM)] * 2 + [vmem()] * 3,
        out_shape=[
            shaped(joint, low),
            shaped(whole, low),
            shaped((others, local, seq), low),
            shaped((others, 8, seq), wide),
            shaped((others, local, cols), low),
        ],
        scratch_shapes=[
            pltpu.VMEM(whole, low),
            pltpu.VMEM(joint, low),
            pltpu.SemaphoreType.DMA((others + 1,)),
        ],
        compiler_params=params(),
        cost_estimate=cost(8),
        name="attn_rest",
    )(info, tokens, bias, *pieces)


def ffn_in_kernel(tokens, ctx_own, ctx_rest, vec, out_own, out_rest, skip, normed_ref, hat_ref, inv_ref):
    others = ctx_rest.shape[0]
    rows = vec[...]
    b_out, gain_one, bias_one, b_down = (rows[i : i + 1] for i in range(4))
    attended = mm(ctx_own[0], out_own[...], 0, 0)
    for k in range(others):
        attended = attended + mm(ctx_rest[k], out_rest[k], 0, 0)
    hat, inv = norm_parts(tokens[...].astype(wide) + attended + b_out)
    hat_ref[...] = hat
    inv_ref[...] = jnp.broadcast_to(inv, inv_ref.shape)
    normed = hat * gain_one + bias_one
    normed_ref[...] = normed.astype(low)
    skip[...] = normed + b_down


def ffn_in(tokens, ctx_own, ctx_rest, vec, out_own, out_rest):
    seq, width = tokens.shape
    others, local = ctx_rest.shape[:2]
    return pl.pallas_call(
        ffn_in_kernel,
        in_specs=[vmem()] * 6,
        out_specs=[vmem()] * 4,
        out_shape=[
            shaped((seq, width), wide),
            shaped((seq, width), low),
            shaped((seq, width), wide),
            shaped((seq, 128), wide),
        ],
        compiler_params=params(),
        cost_estimate=cost(5),
        name="ffn_in",
    )(tokens, ctx_own, ctx_rest, vec, out_own, out_rest)


def ffn_up_kernel(info, normed, bias, up_own, *refs):
    _, act, slope, up, mark = refs[6:]
    size = up.shape[2]
    first = bias.shape[2] - size
    mark[...] = jnp.zeros(mark.shape, wide)
    assemble(info, refs[:6], up, up_own)

    def forward(k, _):
        preact = mm(normed[...], up[k], 1, 0) + bias[k][:, first:].astype(wide)
        value, derivative = gelu_parts(preact)
        act[k] = value.astype(low)
        slope[k] = derivative.astype(low)
        return 0

    lax.fori_loop(0, act.shape[0], forward, 0)


def ffn_up(info, normed, bias, up_own, pieces, mark):
    seq, width = normed.shape
    others, size = pieces[0].shape[0], up_own.shape[1]
    return pl.pallas_call(
        ffn_up_kernel,
        in_specs=[smem()] + [vmem()] * (3 + 6) + [hbm()],
        out_specs=[vmem()] * 4,
        out_shape=[
            shaped((others + 1, seq, size), low),
            shaped((others + 1, seq, size), low),
            shaped((others + 1, width, size), low),
            shaped((8, 128), wide),
        ],
        compiler_params=params(),
        cost_estimate=cost(11),
        name="ffn_up",
    )(info, normed, bias, up_own, *pieces, mark)


def ffn_down_kernel(info, skip, vec, cot, act, down_own, *refs):
    _, out, grad_ref, branch_ref, small, keep, send, down, scratch = refs[6:]
    parts = act.shape[0]
    assemble(info, refs[:6], down, down_own)
    grad_ref[...] = skip[...]

    def branch(k, _):
        grad_ref[...] += mm(act[k], down[k], 1, 0)
        return 0

    lax.fori_loop(0, parts, branch, 0)
    total = grad_ref[...]
    gain_two, bias_two = vec[4:5], vec[5:6]
    hat_two, inv_two = norm_parts(total)
    out[...] = (hat_two * gain_two + bias_two).astype(low)
    grad = cot[...].astype(wide)
    grad_branch = norm_back(grad * gain_two, hat_two, inv_two)
    grad_ref[...] = grad_branch
    branch_low = grad_branch.astype(low)
    branch_ref[...] = branch_low
    small[...] = jnp.zeros(small.shape, wide)
    small[3:4] = jnp.sum(grad_branch, axis=0, keepdims=True)
    small[4:5] = jnp.sum(grad * hat_two, axis=0, keepdims=True)
    small[5:6] = jnp.sum(grad, axis=0, keepdims=True)

    def weight(k, _):
        scratch[...] = mm(act[k], branch_ref[...], 0, 0).astype(low)
        place_pieces(info, scratch, keep, send, k)
        return 0

    lax.fori_loop(0, parts, weight, 0)


def halves_shape(entries, rows, cols):
    return (2, 2, entries, rows // GROUP, cols)


def ffn_down(info, act, skip, vec, cot, down_own, pieces, mark):
    parts, seq, size = act.shape
    width = skip.shape[1]
    half = halves_shape(parts, size, width)
    return pl.pallas_call(
        ffn_down_kernel,
        in_specs=[smem()] + [vmem()] * (5 + 6) + [hbm()],
        out_specs=[vmem()] * 7,
        out_shape=[
            shaped((seq, width), low),
            shaped((seq, width), wide),
            shaped((seq, width), low),
            shaped((16, width), wide),
            shaped(half, low),
            shaped(half, low),
            shaped((parts, size, width), low),
        ],
        scratch_shapes=[pltpu.VMEM((size, width), low)],
        compiler_params=params(),
        cost_estimate=cost(12),
        name="ffn_down",
    )(info, skip, vec, cot, act, down_own, *pieces, mark)


def ffn_back_kernel(
    info, branch_low, grad_branch, normed_low, hat_ref, inv_ref, vec, small_in, slope, up, down,
    grad_ref, residual_ref, small, keep, send, turned, total, scratch,
):
    parts = slope.shape[0]
    index = lax.broadcasted_iota(jnp.int32, small.shape, 0)
    small[...] = small_in[...]
    total[...] = grad_branch[...]
    turned[...] = normed_low[...].T

    def backward(k, _):
        grad_pre = mm(branch_low[...], down[k], 1, 1) * slope[k].astype(wide)
        grad_pre = grad_pre.astype(low)
        sums = jnp.sum(grad_pre.astype(wide), axis=0, keepdims=True)
        small[...] = jnp.where(index == 6 + (info[3] ^ k), sums, small[...])
        scratch[...] = mm(turned[...], grad_pre, 1, 0).astype(low)
        place_pieces(info, scratch, keep, send, k)
        total[...] += mm(grad_pre, up[k], 1, 1)
        return 0

    lax.fori_loop(0, parts, backward, 0)
    grad_normed = total[...]
    hat = hat_ref[...]
    grad_residual = norm_back(grad_normed * vec[1:2], hat, inv_ref[:, :1])
    grad_ref[...] = grad_residual
    residual_ref[...] = grad_residual.astype(low)
    small[0:1] = jnp.sum(grad_residual, axis=0, keepdims=True)
    small[1:2] = jnp.sum(grad_normed * hat, axis=0, keepdims=True)
    small[2:3] = jnp.sum(grad_normed, axis=0, keepdims=True)


def ffn_back(info, branch_low, grad_branch, slope, normed_low, hat, inv, vec, small, up, down):
    _, width, size = up.shape
    parts, seq = slope.shape[:2]
    half = halves_shape(parts, width, size)
    return pl.pallas_call(
        ffn_back_kernel,
        in_specs=[smem()] + [vmem()] * 10,
        out_specs=[vmem()] * 5,
        out_shape=[
            shaped((seq, width), wide),
            shaped((seq, width), low),
            shaped((16, width), wide),
            shaped(half, low),
            shaped(half, low),
        ],
        scratch_shapes=[
            pltpu.VMEM((width, seq), low),
            pltpu.VMEM((seq, width), wide),
            pltpu.VMEM((width, size), low),
        ],
        compiler_params=params(),
        cost_estimate=cost(11),
        name="ffn_back",
    )(info, branch_low, grad_branch, normed_low, hat, inv, vec, small, slope, up, down)


def attn_back_kernel(first, info, tokens, residual_low, small_in, *refs):
    groups = (refs[:4], refs[4:8])
    small, joint, keep, send, scratch = refs[8:]
    local = groups[0][2].shape[1]
    seq, width = tokens.shape
    scale = HD**-0.5
    index = lax.broadcasted_iota(jnp.int32, small.shape, 0)
    small[...] = small_in[...]
    key_pad, query_pad = masked_pad(info[0], seq)
    ones = jnp.ones((8, seq), low)
    for i, (out_w, qkv_ref, ctx_ref, lse_ref) in enumerate(groups):
        k = first + i
        out_rows = out_w[...] if k == 0 else out_w[k - 1]
        qkv, ctx, lse = (ref.at[max(k - 1, 0)] for ref in (qkv_ref, ctx_ref, lse_ref))
        grad_ctx = mm(out_rows, residual_low[...], 1, 1).astype(low)
        for h in range(local // HD):
            lo, hi = h * HD, (h + 1) * HD
            query = qkv[lo:hi]
            key = qkv[local + lo : local + hi]
            value = qkv[2 * local + lo : 2 * local + hi]
            grad_head = grad_ctx[lo:hi]
            scores = mm(
                jnp.concatenate([key, key_pad], 0), jnp.concatenate([query, query_pad], 0), 0, 0
            )
            probs = jnp.exp2(scores * (scale * LOG2E) - lse[h : h + 1])
            grad_probs = mm(value, grad_head, 0, 0)
            product = probs * grad_probs
            grad_scores = (product - probs * jnp.sum(product, axis=0, keepdims=True)).astype(low)
            joint[i, lo:hi] = (mm(key, grad_scores, 1, 0) * scale).astype(low)
            joint[i, local + lo : local + hi] = (mm(query, grad_scores, 1, 1) * scale).astype(low)
            joint[i, 2 * local + lo : 2 * local + hi] = mm(
                grad_head, probs.astype(low), 1, 1
            ).astype(low)
        grads = joint[i]
        sums = mm(ones, grads, 1, 1)[:1]
        gap = jnp.zeros((1, 256 - local), wide)
        rest = jnp.zeros((1, width - 512), wide)
        sums = jnp.concatenate([sums[:, :local], gap, sums[:, 2 * local :], gap, rest], 1)
        small[...] = jnp.where(index == 10 + (info[3] ^ (first + i)), sums, small[...])
        scratch[: 3 * local] = mm(grads, tokens[...], 1, 0).astype(low)
        scratch[3 * local :] = mm(ctx[...], residual_low[...], 1, 0).astype(low)
        place_pieces(info, scratch, keep, send, i)


def attn_back(first, info, tokens, residual_low, small, out_own, own, out_rest, rest):
    seq, width = tokens.shape
    local = out_own.shape[0]
    arrays = []
    for k in (first, first + 1):
        arrays += (out_own,) + tuple(own) if k == 0 else (out_rest,) + tuple(rest)
    half = halves_shape(2, 4 * local, width)
    return pl.pallas_call(
        partial(attn_back_kernel, first),
        in_specs=[smem()] + [vmem()] * 11,
        out_specs=[vmem()] * 4,
        out_shape=[
            shaped((16, width), wide),
            shaped((2, 3 * local, seq), low),
            shaped(half, low),
            shaped(half, low),
        ],
        scratch_shapes=[pltpu.VMEM((4 * local, width), low)],
        compiler_params=params(),
        cost_estimate=cost(9),
        name="attn_back",
    )(info, tokens, residual_low, small, *arrays)


def grad_tokens_kernel(grad, joint_a, joint_b, w_query, w_key, w_value, rest_w, out):
    local, rows = w_query.shape[0], joint_a.shape[1]
    total = grad[...]
    for i, weights in enumerate((w_query, w_key, w_value)):
        total = total + mm(joint_a[0, i * local : (i + 1) * local], weights[...], 0, 0)
    for k in range(1, 4):
        joint = joint_a[k] if k < 2 else joint_b[k - 2]
        total = total + mm(joint, rest_w[k - 1, :rows], 0, 0)
    out[...] = total.astype(low)


def grad_tokens_of(grad, joint_a, joint_b, weights, rest_w):
    return pl.pallas_call(
        grad_tokens_kernel,
        in_specs=[vmem()] * 7,
        out_specs=vmem(),
        out_shape=shaped(grad.shape, low),
        compiler_params=params(),
        cost_estimate=cost(4),
        name="grad_tokens",
    )(grad, joint_a, joint_b, *weights, rest_w)


def finish_ffn_kernel(info, held, held_mates, down, up, mark):
    rows = held.shape[2]
    mark[...] = jnp.zeros(mark.shape, wide)
    for s, pieces in enumerate((held, held_mates)):
        holder = info[1] ^ s
        for move in range(3):
            start = pl.multiple_of((holder * 4 + (info[2] ^ move)) * rows, rows)
            down[pl.ds(start, rows), :] = pieces[move, 0].astype(wide)
            up[pl.ds(start, rows), :] = pieces[move, 1].astype(wide)
        start = pl.multiple_of((holder * 4 + (info[2] ^ 3)) * rows, rows)
        down[pl.ds(start, rows), :] = jnp.zeros((rows, down.shape[1]), wide)
        up[pl.ds(start, rows), :] = jnp.zeros((rows, up.shape[1]), wide)


def finish_ffn(info, held, mates):
    _, _, rows, cols = held.shape
    return pl.pallas_call(
        finish_ffn_kernel,
        in_specs=[smem()] + [vmem()] * 2,
        out_specs=[vmem()] * 3,
        out_shape=[shaped((GROUP * rows, cols), wide)] * 2 + [shaped((8, 128), wide)],
        compiler_params=params(),
        cost_estimate=cost(3),
        name="finish_ffn",
    )(info, held, mates)


def finish_ffn_corner_kernel(info, corner, corner_mate, mark, down_in, up_in, down, up, ready, sems):
    rows = corner.shape[1]
    copies = []
    for s, pieces in enumerate((corner, corner_mate)):
        holder = info[1] ^ s
        start = pl.multiple_of((holder * 4 + (info[2] ^ 3)) * rows, rows)
        for i, target in enumerate((down, up)):
            ready[s, i] = pieces[i].astype(wide)
            copies.append(
                pltpu.make_async_copy(ready.at[s, i], target.at[pl.ds(start, rows), :], sems.at[s, i])
            )
            copies[-1].start()
    for copy in copies:
        copy.wait()


def finish_ffn_corner(info, corner, corner_mate, mark, down, up):
    _, rows, cols = corner.shape
    return pl.pallas_call(
        finish_ffn_corner_kernel,
        in_specs=[smem()] + [vmem()] * 2 + [hbm()] * 3,
        out_specs=[hbm()] * 2,
        out_shape=[shaped(down.shape, wide)] * 2,
        scratch_shapes=[pltpu.VMEM((2, 2, rows, cols), wide), pltpu.SemaphoreType.DMA((2, 2))],
        input_output_aliases={4: 0, 5: 1},
        compiler_params=params(),
        cost_estimate=cost(1),
        name="finish_ffn_corner",
    )(info, corner, corner_mate, mark, down, up)


def finish_attn_kernel(info, *refs):
    query, key, value, out, whole = refs[8:]
    for s in range(2):
        holder = info[1] ^ s
        for move in range(4):
            view = refs[4 * s + move]
            rows = view.shape[0]
            start = pl.multiple_of((holder * 4 + (info[2] ^ move)) * rows, rows)
            whole[pl.ds(start, rows), :] = view[...].astype(wide)
    local = whole.shape[0] // 4
    query[...] = whole[:local]
    key[...] = whole[local : 2 * local]
    value[...] = whole[2 * local : 3 * local]
    out[...] = whole[3 * local :]


def finish_attn(info, pieces):
    rows, cols = pieces[0].shape
    size = GROUP * rows
    local = size // 4
    return pl.pallas_call(
        finish_attn_kernel,
        in_specs=[smem()] + [vmem()] * 8,
        out_specs=[vmem()] * 4,
        out_shape=[shaped((local, cols), wide)] * 4,
        scratch_shapes=[pltpu.VMEM((size, cols), wide)],
        compiler_params=params(),
        cost_estimate=cost(2),
        name="finish_attn",
    )(info, *pieces)


class Links:
    def __init__(self, dp_size, parts):
        self.dp_size, self.parts = dp_size, parts

    def move(self, array, partner):
        pairs = []
        for d in range(self.dp_size):
            for t in range(self.parts):
                to_d, to_t = partner(d, t)
                pairs.append((d * self.parts + t, to_d * self.parts + to_t))
        return lax.ppermute(array, ("dp", "tensor"), pairs)

    def bit(self, array, bit):
        return self.move(array, lambda d, t: (d ^ bit, t))

    def core(self, array):
        return self.bit(array, 1)

    def plane(self, array, step):
        return self.move(array, lambda d, t: (d ^ (2 if (d & 1) == step else 4), t))

    def everywhere(self, array, bits):
        return [self.bit(array, bit) for bit in bits]

    def across(self, array, k):
        return self.move(array, lambda d, t: (d, t ^ k))

    def line(self, array, step):
        return self.move(array, lambda d, t: (d, t ^ (1 if (d & 1) == step else 2)))


def add(left, right):
    return (left.astype(wide) + right.astype(wide)).astype(low)


def after(*values):
    return lax.optimization_barrier(values)


def per_device(
    dp_size,
    parts,
    tokens,
    page_lengths,
    w_query,
    b_query,
    w_key,
    w_value,
    b_value,
    w_out,
    b_out,
    ln1_gain,
    ln1_bias,
    w_up,
    b_up,
    w_down,
    b_down,
    ln2_gain,
    ln2_bias,
    cotangent,
):
    links = Links(dp_size, parts)
    me = lax.axis_index("tensor")
    place = lax.axis_index("dp") % GROUP
    core, quarter = place & 1, place >> 1
    is_odd = core == 1
    width = tokens.shape[1]
    local = w_query.shape[1]
    rows = width // GROUP
    length = lax.dynamic_slice_in_dim(page_lengths, me, 1, 0)
    info = jnp.concatenate([length, jnp.stack([core, quarter, me]).astype(jnp.int32)])
    attn_w = (w_query.T, w_key.T, w_value.T, w_out)
    piece = core * 4 + quarter

    def cut(array, index):
        return lax.dynamic_slice_in_dim(array, index * rows, rows, 0)

    a0 = lax.select_n(piece >> 1, *(cut(array, piece & 1) for array in attn_w))
    bias_own = jnp.concatenate([b_query, b_value, b_up])
    bias_rows = jnp.pad(bias_own, (0, 8 * width - bias_own.size)).reshape(8, width)
    a0, piece_d = after(a0, piece)
    d0 = cut(w_down, piece_d)
    u0 = jnp.concatenate([cut(w_up, piece), bias_rows], axis=0)
    vec = jnp.stack([b_out, ln1_gain, ln1_bias, b_down, ln2_gain, ln2_bias, b_down, b_down])
    vec = vec.astype(wide)
    a1, d1 = links.line(a0, 0), links.line(d0, 0)
    a1, u0, vec, tokens_in = after(a1, u0, vec, tokens)
    a2 = links.line(jnp.stack([a0, a1]), 1)
    u1 = links.line(u0, 0)
    own = list(attn_own(info, tokens_in, attn_w[:3], bias_own.astype(wide)[None, None]))
    a2, u1, d1, own[2] = after(a2, u1, d1, own[2])
    a3 = jnp.concatenate([a1[None], a2])
    a4 = links.plane(a3, 0)
    u2 = links.line(jnp.stack([u0, u1]), 1)
    a4, d1 = after(a4, d1)
    u3 = jnp.concatenate([u1[None], u2])
    bias_rest = u3[:, rows:].reshape(parts - 1, 8 * width)[:, : bias_own.size]
    near, far = bias_rest[0], bias_rest[1]
    bias = jnp.stack(
        [bias_own, jnp.where(is_odd, far, near), jnp.where(is_odd, near, far), bias_rest[2]]
    )
    bias = bias.astype(wide)[:, None]
    u3 = u3[:, :rows]
    a5 = links.plane(jnp.stack([a3, a4]), 1)
    u4 = links.plane(u3, 0)
    d2 = links.line(jnp.stack([d0, d1]), 1)
    a5, u4, d2, bias = after(a5, u4, d2, bias)
    d3 = jnp.concatenate([d1[None], d2])
    pieces_a = [a3, a4, a5] + [links.core(array) for array in (a3, a4, a5)]
    u5 = links.plane(jnp.stack([u3, u4]), 1)
    d4 = links.plane(d3, 0)
    qkv, attn_rest_w, ctx, lse, out_rest = attn_rest(info, tokens, bias, pieces_a)
    skip, normed_low, hat, inv = ffn_in(tokens, own[1], ctx, vec, w_out, out_rest)
    u5, d4, lse, inv = after(u5, d4, lse, inv)
    pieces_u = [u3, u4, u5] + [links.core(array) for array in (u3, u4, u5)]
    d5 = links.plane(jnp.stack([d3, d4]), 1)
    act, slope, up, mark = ffn_up(info, normed_low, bias, w_up, pieces_u, inv)
    d5, mark = after(d5, mark)
    pieces_d = [d3, d4, d5] + [links.core(array) for array in (d3, d4, d5)]
    output, grad_branch, branch_low, small, keep_d, send_d, down = ffn_down(
        info, act, skip, vec, cotangent, w_down, pieces_d, mark
    )
    rest = (qkv, ctx, lse)

    def plane_a(keep, got):
        return links.plane(add(keep[1], got[1]), 0), add(keep[0], got[0])

    def plane_b(kept, got):
        return links.plane(add(kept[1], got[1]), 1), add(kept[0], got[0])

    def line_a(both):
        both = both.reshape(-1, 2, parts // 2, rows, width)
        sent = jnp.where(is_odd, both[:, :, 1], both[:, 1])
        return links.line(sent, 1), jnp.where(is_odd, both[:, :, 0], both[:, 0])

    def line_b(kept, got):
        both = add(kept, got)
        return links.line(both[:, 1], 0), both[:, 0]

    def settle(kept, got):
        total = kept.astype(wide) + got.astype(wide)
        bit = GROUP
        while bit < dp_size:
            total = total + links.bit(total, bit)
            bit *= 2
        return total.astype(low)

    def mates(held):
        return held + [links.core(array) for array in held]

    got_d = links.core(send_d)
    got_d, small = after(got_d, small)
    near_d, kept_d = plane_a(keep_d, got_d)
    grad_residual, residual_low, small, keep_u, send_u = ffn_back(
        info, branch_low, grad_branch, slope, normed_low, hat, inv, vec, small, up, down
    )
    near_d, send_u, small = after(near_d, send_u, small)
    got_u = links.core(send_u)
    far_d, kept_d = plane_b(kept_d, near_d)
    small, joint_a, keep_a, send_a = attn_back(
        0, info, tokens, residual_low, small, w_out, own, out_rest, rest
    )
    got_u, far_d, send_a, small = after(got_u, far_d, send_a, small)
    near_u, kept_u = plane_a(keep_u, got_u)
    got_a = links.core(send_a)
    line_d, kept_d = line_a(add(kept_d, far_d))
    small, joint_b, keep_b, send_b = attn_back(
        2, info, tokens, residual_low, small, w_out, own, out_rest, rest
    )
    near_u, got_a, line_d, send_b, small, grad_residual = after(
        near_u, got_a, line_d, send_b, small, grad_residual
    )
    got_b = links.core(send_b)
    far_u, kept_u = plane_b(kept_u, near_u)
    last_d, kept_d = line_b(kept_d, line_d)
    grad_tokens = grad_tokens_of(grad_residual, joint_a, joint_b, attn_w[:3], attn_rest_w)
    small_got = links.core(small)
    got_b, far_u, last_d, grad_tokens, small_got = after(got_b, far_u, last_d, grad_tokens, small_got)
    small = small + small_got
    size = parts * 2 * rows

    def joined(share, small):
        return jnp.concatenate([share.reshape(-1, width), small.astype(low)], axis=0)

    keep_ab, got_ab = jnp.stack([keep_a, keep_b], axis=2), jnp.stack([got_a, got_b], axis=2)
    near_a = links.plane(joined(add(keep_ab[1], got_ab[1]), small), 0)
    kept_a = add(keep_ab[0], got_ab[0])
    line_u, kept_u = line_a(add(kept_u, far_u))
    near_a, line_u = after(near_a, line_u)
    small = small + near_a[size:].astype(wide)
    near_a = near_a[:size].reshape(kept_a.shape)
    far_a = links.plane(joined(add(kept_a[1], near_a[1]), small), 1)
    kept_a = add(kept_a[0], near_a[0])
    last_u, kept_u = line_b(kept_u, line_u)
    far_a, last_u = after(far_a, last_u)
    size = parts * rows
    small = small + far_a[size:].astype(wide)
    share = add(kept_a, far_a[:size].reshape(kept_a.shape)).reshape(parts, rows, width)
    across = [links.across(joined(share[k], small), k) for k in range(parts - 1, 0, -1)]
    sum_f = jnp.stack([settle(kept_d, last_d)[0], settle(kept_u, last_u)[0]])
    f_x, f_y = links.everywhere(sum_f, (2, 4))
    across, f_x, f_y = after(across, f_x, f_y)
    sum_a = share[0].astype(wide)
    for array in across:
        sum_a = sum_a + array[:rows].astype(wide)
        small = small + array[rows:].astype(wide)
    bit = GROUP
    while bit < dp_size:
        sum_a = sum_a + links.bit(sum_a, bit)
        small = small + links.bit(small, bit)
        bit *= 2
    sum_a = sum_a.astype(low)
    around = links.everywhere(sum_a, (2, 4, 6))
    f_xy = links.plane(jnp.where(is_odd, f_x, f_y), 0)
    held = jnp.stack([sum_f, f_x, f_y])
    *early, mark = finish_ffn(info, held, links.core(held))
    pair = lax.dynamic_index_in_dim(small, 10 + me, 0, keepdims=False)
    grad_b_up = lax.dynamic_index_in_dim(small, 6 + me, 0, keepdims=False)
    around, small, pair, grad_b_up, mark = after(around, small, pair, grad_b_up, mark)
    grad_w_down, grad_w_up = finish_ffn_corner(info, f_xy, links.core(f_xy), mark, *early)
    grad_w_query, grad_w_key, grad_w_value, grad_w_out = finish_attn(info, mates([sum_a] + around))
    grad_w_query, grad_w_key, grad_w_value = grad_w_query.T, grad_w_key.T, grad_w_value.T
    return (
        output,
        grad_tokens,
        grad_w_query,
        pair[:local],
        grad_w_key,
        grad_w_value,
        pair[256 : 256 + local],
        grad_w_out,
        small[0],
        small[1],
        small[2],
        grad_w_up,
        grad_b_up,
        grad_w_down,
        small[3],
        small[4],
        small[5],
    )


def solution(mesh):
    columns, rows, both = P(None, "tensor"), P("tensor", None), P(("dp", "tensor"), None)
    share = P("tensor")
    return jax.shard_map(
        partial(per_device, mesh.shape["dp"], mesh.shape["tensor"]),
        mesh=mesh,
        in_specs=(
            both,
            P("dp"),
            columns,
            share,
            columns,
            columns,
            share,
            rows,
            P(),
            P(),
            P(),
            columns,
            share,
            rows,
            P(),
            P(),
            P(),
            both,
        ),
        out_specs=(
            both,
            both,
            columns,
            share,
            columns,
            columns,
            share,
            rows,
            P(),
            P(),
            P(),
            columns,
            share,
            rows,
            P(),
            P(),
            P(),
        ),
        check_vma=False,
    )
```

```python
from functools import partial

import jax
import jax.numpy as jnp
from jax import lax
from jax.experimental import pallas as pl
from jax.experimental.pallas import tpu as pltpu
from jax.sharding import PartitionSpec as P

HD = 64
SEQ = 512
GROUP = 8
LOG2E = 1.4426950408889634
TAIL_P = 0.39
TAIL = (
    0.23532521908406087,
    0.09138841455460205,
    0.6495593986198918,
    -0.6354002786931026,
    0.8866643698688825,
    -0.22753712513305413,
)

epsilon = 1e-12
masked_score = -1000000000.0
low = jnp.bfloat16
wide = jnp.float32
PEAK = 1.1e15
LIMIT = 12


def mm(left, right, left_dim, right_dim):
    return lax.dot_general(
        left, right, (((left_dim,), (right_dim,)), ((), ())), preferred_element_type=wide
    )


def vmem():
    return pl.BlockSpec(memory_space=pltpu.VMEM)


def smem():
    return pl.BlockSpec(memory_space=pltpu.SMEM)


def hbm():
    return pl.BlockSpec(memory_space=pl.ANY)


def cost(microseconds):
    return pl.CostEstimate(
        flops=int(microseconds * 1e-6 * PEAK), bytes_accessed=1 << 20, transcendentals=0
    )


def params(mebibytes=LIMIT):
    return pltpu.CompilerParams(vmem_limit_bytes=mebibytes << 20)


def shaped(shape, dtype):
    return jax.ShapeDtypeStruct(shape, dtype)


def masked_pad(length, seq):
    row = lax.broadcasted_iota(jnp.int32, (16, seq), 0)
    key = lax.broadcasted_iota(jnp.int32, (16, seq), 1)
    bias = jnp.where((row == 0) & (key >= length), masked_score, 0.0).astype(low)
    ones = jnp.where(row == 0, 1.0, 0.0).astype(low)
    return bias, ones


def as_column(row, ones):
    first = lax.broadcasted_iota(jnp.int32, (16, row.shape[1]), 0) == 0
    return mm(jnp.where(first, row, 0.0).astype(low), ones, 0, 0)


def group_forward(tokens, weights, bias, length, qkv_ref, ctx_ref, lse_ref):
    local = weights[0].shape[0]
    seq = tokens.shape[0]
    scale = HD**-0.5 * LOG2E
    key_pad, ones = masked_pad(length, seq)
    query = (mm(weights[0], tokens, 1, 1) + as_column(bias[:, :local], ones)).astype(low)
    key = mm(weights[1], tokens, 1, 1).astype(low)
    value = mm(weights[2], tokens, 1, 1) + as_column(bias[:, local : 2 * local], ones)
    value = value.astype(low)
    qkv_ref[:local] = query
    qkv_ref[local : 2 * local] = key
    qkv_ref[2 * local :] = value
    for h in range(local // HD):
        part = slice(h * HD, (h + 1) * HD)
        scores = mm(
            jnp.concatenate([key[part], key_pad], 0), jnp.concatenate([query[part], ones], 0), 0, 0
        )
        top = jnp.max(scores, axis=0, keepdims=True)
        probs = jnp.exp2((scores - top) * scale)
        total = jnp.sum(probs, axis=0, keepdims=True)
        context = mm(value[part], probs.astype(low), 1, 0)
        ctx_ref[part] = (context * (1.0 / total)).astype(low)
        lse_ref[h : h + 1] = top * scale + jnp.log2(total)


def gelu_parts(x):
    t = 1.0 / (1.0 + (TAIL_P * 0.5**0.5) * jnp.abs(x))
    poly = TAIL[-1]
    for factor in TAIL[-2::-1]:
        poly = poly * t + factor
    bell = jnp.exp2(x * x * (-0.5 * LOG2E))
    half = 0.5 * poly * t * bell
    cdf = jnp.where(x >= 0, 1.0 - half, half)
    return x * cdf, cdf + x * bell * (0.5 / jnp.pi) ** 0.5


def norm_parts(values):
    centred = values - jnp.mean(values, axis=1, keepdims=True)
    inverse = lax.rsqrt(jnp.mean(centred * centred, axis=1, keepdims=True) + epsilon)
    return centred * inverse, inverse


def norm_back(scaled, normal, inverse):
    return inverse * (
        scaled
        - jnp.mean(scaled, axis=1, keepdims=True)
        - normal * jnp.mean(scaled * normal, axis=1, keepdims=True)
    )


def assemble(info, refs, target, own=None):
    if own is not None:
        target[0] = own[...]
    skip = 1 if own is None else 0
    for s in range(2):
        views = refs[4 * s : 4 * s + 4]
        holder = info[1] ^ s
        order = (1 + holder, 2 - holder, 3)
        for view, move in zip(views, (0,) + order):
            rows = view.shape[1]
            start = pl.multiple_of((holder * 4 + (info[2] ^ move)) * rows, rows)
            for entry, k in enumerate(order):
                target[k - skip, pl.ds(start, rows), :] = view[entry]


def place_pieces(info, scratch, keep_ref, send_ref, entry):
    rows = scratch.shape[0] // GROUP
    for s, target in enumerate((keep_ref, send_ref)):
        half = info[1] ^ s
        for q in range(4):
            move = info[2] ^ q
            x_bit, y_bit = move & 1, move >> 1
            a = jnp.where(half == 0, x_bit, y_bit)
            start = pl.multiple_of((half * 4 + q) * rows, rows)
            target[a, x_bit + y_bit - a, entry] = scratch[pl.ds(start, rows), :]


def attn_own_kernel(info, tokens, w_query, w_key, w_value, bias, qkv, ctx, lse):
    weights = (w_query[...], w_key[...], w_value[...])
    group_forward(tokens[...], weights, bias[0], info[0], qkv.at[0], ctx.at[0], lse.at[0])


def attn_own(info, tokens, weights, bias):
    local, seq = weights[0].shape[0], tokens.shape[0]
    return pl.pallas_call(
        attn_own_kernel,
        in_specs=[smem()] + [vmem()] * 5,
        out_specs=[vmem()] * 3,
        out_shape=[
            shaped((1, 3 * local, seq), low),
            shaped((1, local, seq), low),
            shaped((1, 8, seq), wide),
        ],
        compiler_params=params(),
        cost_estimate=cost(4),
        name="attn_own",
    )(info, tokens, *weights, bias)


def attn_rest_kernel(info, tokens, bias, *refs):
    qkv_out, whole, ctx, lse, out_w, weights, qkv, sems = refs[8:]
    others, local = ctx.shape[:2]
    assemble(info, refs[:8], weights)
    sent = [pltpu.make_async_copy(weights, whole, sems.at[others])]
    sent[0].start()
    out_w[...] = weights[:, 3 * local :]

    def group(k, _):
        joint = tuple(weights[k, i * local : (i + 1) * local] for i in range(3))
        group_forward(
            tokens[...], joint, bias[k + 1], info[0], qkv.at[k], ctx.at[k], lse.at[k]
        )
        pltpu.make_async_copy(qkv.at[k], qkv_out.at[k], sems.at[k]).start()
        return 0

    lax.fori_loop(0, others, group, 0)
    sent += [pltpu.make_async_copy(qkv.at[k], qkv_out.at[k], sems.at[k]) for k in range(others)]
    for copy in sent:
        copy.wait()


def attn_rest(info, tokens, bias, pieces):
    others, rows, cols = pieces[0].shape
    size, seq = rows * GROUP, tokens.shape[0]
    local = size // 4
    joint, whole = (others, 3 * local, seq), (others, size, cols)
    return pl.pallas_call(
        attn_rest_kernel,
        in_specs=[smem()] + [vmem()] * 10,
        out_specs=[pl.BlockSpec(memory_space=pltpu.HBM)] * 2 + [vmem()] * 3,
        out_shape=[
            shaped(joint, low),
            shaped(whole, low),
            shaped((others, local, seq), low),
            shaped((others, 8, seq), wide),
            shaped((others, local, cols), low),
        ],
        scratch_shapes=[
            pltpu.VMEM(whole, low),
            pltpu.VMEM(joint, low),
            pltpu.SemaphoreType.DMA((others + 1,)),
        ],
        compiler_params=params(),
        cost_estimate=cost(8),
        name="attn_rest",
    )(info, tokens, bias, *pieces)


def ffn_in_kernel(tokens, ctx_own, ctx_rest, vec, out_own, out_rest, skip, normed_ref, hat_ref, inv_ref):
    others = ctx_rest.shape[0]
    rows = vec[...]
    b_out, gain_one, bias_one, b_down = (rows[i : i + 1] for i in range(4))
    attended = mm(ctx_own[0], out_own[...], 0, 0)
    for k in range(others):
        attended = attended + mm(ctx_rest[k], out_rest[k], 0, 0)
    hat, inv = norm_parts(tokens[...].astype(wide) + attended + b_out)
    hat_ref[...] = hat
    inv_ref[...] = jnp.broadcast_to(inv, inv_ref.shape)
    normed = hat * gain_one + bias_one
    normed_ref[...] = normed.astype(low)
    skip[...] = normed + b_down


def ffn_in(tokens, ctx_own, ctx_rest, vec, out_own, out_rest):
    seq, width = tokens.shape
    others, local = ctx_rest.shape[:2]
    return pl.pallas_call(
        ffn_in_kernel,
        in_specs=[vmem()] * 6,
        out_specs=[vmem()] * 4,
        out_shape=[
            shaped((seq, width), wide),
            shaped((seq, width), low),
            shaped((seq, width), wide),
            shaped((seq, 128), wide),
        ],
        compiler_params=params(),
        cost_estimate=cost(5),
        name="ffn_in",
    )(tokens, ctx_own, ctx_rest, vec, out_own, out_rest)


def ffn_up_kernel(info, normed, bias, up_own, *refs):
    _, act, slope, up, mark = refs[8:]
    size = up.shape[2]
    first = bias.shape[2] - size
    mark[...] = jnp.zeros(mark.shape, wide)
    assemble(info, refs[:8], up, up_own)

    def forward(k, _):
        preact = mm(normed[...], up[k], 1, 0) + bias[k][:, first:].astype(wide)
        value, derivative = gelu_parts(preact)
        act[k] = value.astype(low)
        slope[k] = derivative.astype(low)
        return 0

    lax.fori_loop(0, act.shape[0], forward, 0)


def ffn_up(info, normed, bias, up_own, pieces, mark):
    seq, width = normed.shape
    others, size = pieces[0].shape[0], up_own.shape[1]
    return pl.pallas_call(
        ffn_up_kernel,
        in_specs=[smem()] + [vmem()] * (3 + 8) + [hbm()],
        out_specs=[vmem()] * 4,
        out_shape=[
            shaped((others + 1, seq, size), low),
            shaped((others + 1, seq, size), low),
            shaped((others + 1, width, size), low),
            shaped((8, 128), wide),
        ],
        compiler_params=params(),
        cost_estimate=cost(11),
        name="ffn_up",
    )(info, normed, bias, up_own, *pieces, mark)


def ffn_down_kernel(info, skip, vec, cot, act, down_own, *refs):
    _, out, grad_ref, branch_ref, small, down = refs[8:]
    parts = act.shape[0]
    assemble(info, refs[:8], down, down_own)
    grad_ref[...] = skip[...]

    def branch(k, _):
        grad_ref[...] += mm(act[k], down[k], 1, 0)
        return 0

    lax.fori_loop(0, parts, branch, 0)
    total = grad_ref[...]
    gain_two, bias_two = vec[4:5], vec[5:6]
    hat_two, inv_two = norm_parts(total)
    out[...] = (hat_two * gain_two + bias_two).astype(low)
    grad = cot[...].astype(wide)
    grad_branch = norm_back(grad * gain_two, hat_two, inv_two)
    grad_ref[...] = grad_branch
    branch_low = grad_branch.astype(low)
    branch_ref[...] = branch_low
    small[...] = jnp.zeros(small.shape, wide)
    small[3:4] = jnp.sum(grad_branch, axis=0, keepdims=True)
    small[4:5] = jnp.sum(grad * hat_two, axis=0, keepdims=True)
    small[5:6] = jnp.sum(grad, axis=0, keepdims=True)


def down_grad_kernel(first, info, act, branch_low, keep, send, mark, scratch):
    mark[...] = jnp.zeros(mark.shape, wide)

    def weight(i, _):
        scratch[...] = mm(act[first + i], branch_low[...], 0, 0).astype(low)
        place_pieces(info, scratch, keep, send, i)
        return 0

    lax.fori_loop(0, 2, weight, 0)


def down_grad(first, info, act, branch_low, mark):
    size, width = act.shape[2], branch_low.shape[1]
    half = halves_shape(2, size, width)
    return pl.pallas_call(
        partial(down_grad_ordered, first),
        in_specs=[smem()] + [vmem()] * 2 + [hbm()],
        out_specs=[vmem()] * 3,
        out_shape=[shaped(half, low), shaped(half, low), shaped((8, 128), wide)],
        scratch_shapes=[pltpu.VMEM((size, width), low)],
        compiler_params=params(),
        cost_estimate=cost(2),
        name="down_grad",
    )(info, act, branch_low, mark)


def down_grad_ordered(first, info, act, branch_low, _, *refs):
    down_grad_kernel(first, info, act, branch_low, *refs)


def halves_shape(entries, rows, cols):
    return (2, 2, entries, rows // GROUP, cols)


def ffn_down(info, act, skip, vec, cot, down_own, pieces, mark):
    parts, seq, size = act.shape
    width = skip.shape[1]
    return pl.pallas_call(
        ffn_down_kernel,
        in_specs=[smem()] + [vmem()] * (5 + 8) + [hbm()],
        out_specs=[vmem()] * 5,
        out_shape=[
            shaped((seq, width), low),
            shaped((seq, width), wide),
            shaped((seq, width), low),
            shaped((16, width), wide),
            shaped((parts, size, width), low),
        ],
        compiler_params=params(),
        cost_estimate=cost(12),
        name="ffn_down",
    )(info, skip, vec, cot, act, down_own, *pieces, mark)


def ffn_back_kernel(
    info, branch_low, grad_branch, normed_low, hat_ref, inv_ref, vec, small_in, slope, up, down,
    grad_ref, residual_ref, small, keep, send, turned, total, scratch,
):
    parts = slope.shape[0]
    index = lax.broadcasted_iota(jnp.int32, small.shape, 0)
    small[...] = small_in[...]
    total[...] = grad_branch[...]
    turned[...] = normed_low[...].T

    def backward(k, _):
        grad_pre = mm(branch_low[...], down[k], 1, 1) * slope[k].astype(wide)
        grad_pre = grad_pre.astype(low)
        sums = jnp.sum(grad_pre.astype(wide), axis=0, keepdims=True)
        small[...] = jnp.where(index == 6 + (info[3] ^ k), sums, small[...])
        scratch[...] = mm(turned[...], grad_pre, 1, 0).astype(low)
        place_pieces(info, scratch, keep, send, k)
        total[...] += mm(grad_pre, up[k], 1, 1)
        return 0

    lax.fori_loop(0, parts, backward, 0)
    grad_normed = total[...]
    hat = hat_ref[...]
    grad_residual = norm_back(grad_normed * vec[1:2], hat, inv_ref[:, :1])
    grad_ref[...] = grad_residual
    residual_ref[...] = grad_residual.astype(low)
    small[0:1] = jnp.sum(grad_residual, axis=0, keepdims=True)
    small[1:2] = jnp.sum(grad_normed * hat, axis=0, keepdims=True)
    small[2:3] = jnp.sum(grad_normed, axis=0, keepdims=True)


def ffn_back(info, branch_low, grad_branch, slope, normed_low, hat, inv, vec, small, up, down):
    _, width, size = up.shape
    parts, seq = slope.shape[:2]
    half = halves_shape(parts, width, size)
    return pl.pallas_call(
        ffn_back_kernel,
        in_specs=[smem()] + [vmem()] * 10,
        out_specs=[vmem()] * 5,
        out_shape=[
            shaped((seq, width), wide),
            shaped((seq, width), low),
            shaped((16, width), wide),
            shaped(half, low),
            shaped(half, low),
        ],
        scratch_shapes=[
            pltpu.VMEM((width, seq), low),
            pltpu.VMEM((seq, width), wide),
            pltpu.VMEM((width, size), low),
        ],
        compiler_params=params(),
        cost_estimate=cost(11),
        name="ffn_back",
    )(info, branch_low, grad_branch, normed_low, hat, inv, vec, small, slope, up, down)


def attn_back_kernel(first, info, tokens, residual_low, small_in, *refs):
    groups = (refs[:4], refs[4:8])
    small, joint, keep, send, scratch = refs[8:]
    local = groups[0][2].shape[1]
    seq, width = tokens.shape
    scale = HD**-0.5
    index = lax.broadcasted_iota(jnp.int32, small.shape, 0)
    small[...] = small_in[...]
    key_pad, query_pad = masked_pad(info[0], seq)
    ones = jnp.ones((8, seq), low)

    def group(i, out_rows, qkv, ctx, lse):
        grad_ctx = mm(out_rows, residual_low[...], 1, 1).astype(low)
        for h in range(local // HD):
            lo, hi = h * HD, (h + 1) * HD
            query = qkv[lo:hi]
            key = qkv[local + lo : local + hi]
            value = qkv[2 * local + lo : 2 * local + hi]
            grad_head = grad_ctx[lo:hi]
            scores = mm(
                jnp.concatenate([key, key_pad], 0), jnp.concatenate([query, query_pad], 0), 0, 0
            )
            probs = jnp.exp2(scores * (scale * LOG2E) - lse[h : h + 1])
            grad_probs = mm(value, grad_head, 0, 0)
            product = probs * grad_probs
            grad_scores = (product - probs * jnp.sum(product, axis=0, keepdims=True)).astype(low)
            joint[i, lo:hi] = (mm(key, grad_scores, 1, 0) * scale).astype(low)
            joint[i, local + lo : local + hi] = (mm(query, grad_scores, 1, 1) * scale).astype(low)
            joint[i, 2 * local + lo : 2 * local + hi] = mm(
                grad_head, probs.astype(low), 1, 1
            ).astype(low)
        grads = joint[i]
        sums = mm(ones, grads, 1, 1)[:1]
        gap = jnp.zeros((1, 256 - local), wide)
        rest = jnp.zeros((1, width - 512), wide)
        sums = jnp.concatenate([sums[:, :local], gap, sums[:, 2 * local :], gap, rest], 1)
        small[...] = jnp.where(index == 10 + (info[3] ^ (first + i)), sums, small[...])
        scratch[: 3 * local] = mm(grads, tokens[...], 1, 0).astype(low)
        scratch[3 * local :] = mm(ctx[...], residual_low[...], 1, 0).astype(low)
        place_pieces(info, scratch, keep, send, i)

    if first == 0:
        for i, (out_w, qkv_ref, ctx_ref, lse_ref) in enumerate(groups):
            group(i, out_w[...] if i == 0 else out_w[0], qkv_ref.at[0], ctx_ref.at[0], lse_ref.at[0])
        return
    out_w, qkv_ref, ctx_ref, lse_ref = groups[0]

    def step(i, _):
        k = first - 1 + i
        group(i, out_w[k], qkv_ref.at[k], ctx_ref.at[k], lse_ref.at[k])
        return 0

    lax.fori_loop(0, 2, step, 0)


def attn_back(first, info, tokens, residual_low, small, out_own, own, out_rest, rest):
    seq, width = tokens.shape
    local = out_own.shape[0]
    arrays = []
    for k in (first, first + 1):
        arrays += (out_own,) + tuple(own) if k == 0 else (out_rest,) + tuple(rest)
    half = halves_shape(2, 4 * local, width)
    return pl.pallas_call(
        partial(attn_back_kernel, first),
        in_specs=[smem()] + [vmem()] * 11,
        out_specs=[vmem()] * 4,
        out_shape=[
            shaped((16, width), wide),
            shaped((2, 3 * local, seq), low),
            shaped(half, low),
            shaped(half, low),
        ],
        scratch_shapes=[pltpu.VMEM((4 * local, width), low)],
        compiler_params=params(),
        cost_estimate=cost(9),
        name="attn_back",
    )(info, tokens, residual_low, small, *arrays)


def grad_tokens_kernel(grad, joint_a, joint_b, w_query, w_key, w_value, rest_w, out):
    local, rows = w_query.shape[0], joint_a.shape[1]
    total = grad[...]
    for i, weights in enumerate((w_query, w_key, w_value)):
        total = total + mm(joint_a[0, i * local : (i + 1) * local], weights[...], 0, 0)
    for k in range(1, 4):
        joint = joint_a[k] if k < 2 else joint_b[k - 2]
        total = total + mm(joint, rest_w[k - 1, :rows], 0, 0)
    out[...] = total.astype(low)


def grad_tokens_of(grad, joint_a, joint_b, weights, rest_w):
    return pl.pallas_call(
        grad_tokens_kernel,
        in_specs=[vmem()] * 7,
        out_specs=vmem(),
        out_shape=shaped(grad.shape, low),
        compiler_params=params(),
        cost_estimate=cost(4),
        name="grad_tokens",
    )(grad, joint_a, joint_b, *weights, rest_w)


def finish_ffn_kernel(info, held, held_mates, down, up, mark):
    rows = held.shape[2]
    mark[...] = jnp.zeros(mark.shape, wide)
    for s, pieces in enumerate((held, held_mates)):
        holder = info[1] ^ s
        for move in range(3):
            start = pl.multiple_of((holder * 4 + (info[2] ^ move)) * rows, rows)
            down[pl.ds(start, rows), :] = pieces[move, 0].astype(wide)
            up[pl.ds(start, rows), :] = pieces[move, 1].astype(wide)
        start = pl.multiple_of((holder * 4 + (info[2] ^ 3)) * rows, rows)
        down[pl.ds(start, rows), :] = jnp.zeros((rows, down.shape[1]), wide)
        up[pl.ds(start, rows), :] = jnp.zeros((rows, up.shape[1]), wide)


def finish_ffn(info, held, mates):
    _, _, rows, cols = held.shape
    return pl.pallas_call(
        finish_ffn_kernel,
        in_specs=[smem()] + [vmem()] * 2,
        out_specs=[vmem()] * 3,
        out_shape=[shaped((GROUP * rows, cols), wide)] * 2 + [shaped((8, 128), wide)],
        compiler_params=params(),
        cost_estimate=cost(3),
        name="finish_ffn",
    )(info, held, mates)


def finish_ffn_corner_kernel(info, corner, corner_mate, mark, down_in, up_in, down, up, ready, sems):
    rows = corner.shape[1]
    copies = []
    for s, pieces in enumerate((corner, corner_mate)):
        holder = info[1] ^ s
        start = pl.multiple_of((holder * 4 + (info[2] ^ 3)) * rows, rows)
        for i, target in enumerate((down, up)):
            ready[s, i] = pieces[i].astype(wide)
            copies.append(
                pltpu.make_async_copy(ready.at[s, i], target.at[pl.ds(start, rows), :], sems.at[s, i])
            )
            copies[-1].start()
    for copy in copies:
        copy.wait()


def finish_ffn_corner(info, corner, corner_mate, mark, down, up):
    _, rows, cols = corner.shape
    return pl.pallas_call(
        finish_ffn_corner_kernel,
        in_specs=[smem()] + [vmem()] * 2 + [hbm()] * 3,
        out_specs=[hbm()] * 2,
        out_shape=[shaped(down.shape, wide)] * 2,
        scratch_shapes=[pltpu.VMEM((2, 2, rows, cols), wide), pltpu.SemaphoreType.DMA((2, 2))],
        input_output_aliases={4: 0, 5: 1},
        compiler_params=params(),
        cost_estimate=cost(1),
        name="finish_ffn_corner",
    )(info, corner, corner_mate, mark, down, up)


def finish_attn_kernel(info, *refs):
    query, key, value, out, whole = refs[8:]
    for s in range(2):
        holder = info[1] ^ s
        for move in range(4):
            view = refs[4 * s + move]
            rows = view.shape[0]
            start = pl.multiple_of((holder * 4 + (info[2] ^ move)) * rows, rows)
            whole[pl.ds(start, rows), :] = view[...].astype(wide)
    local = whole.shape[0] // 4
    query[...] = whole[:local]
    key[...] = whole[local : 2 * local]
    value[...] = whole[2 * local : 3 * local]
    out[...] = whole[3 * local :]


def finish_attn(info, pieces):
    rows, cols = pieces[0].shape
    size = GROUP * rows
    local = size // 4
    return pl.pallas_call(
        finish_attn_kernel,
        in_specs=[smem()] + [vmem()] * 8,
        out_specs=[vmem()] * 4,
        out_shape=[shaped((local, cols), wide)] * 4,
        scratch_shapes=[pltpu.VMEM((size, cols), wide)],
        compiler_params=params(),
        cost_estimate=cost(2),
        name="finish_attn",
    )(info, *pieces)


class Links:
    def __init__(self, dp_size, parts):
        self.dp_size, self.parts = dp_size, parts

    def move(self, array, partner):
        pairs = []
        for d in range(self.dp_size):
            for t in range(self.parts):
                to_d, to_t = partner(d, t)
                pairs.append((d * self.parts + t, to_d * self.parts + to_t))
        return lax.ppermute(array, ("dp", "tensor"), pairs)

    def bit(self, array, bit):
        return self.move(array, lambda d, t: (d ^ bit, t))

    def core(self, array):
        return self.bit(array, 1)

    def plane(self, array, step):
        return self.move(array, lambda d, t: (d ^ (2 if (d & 1) == step else 4), t))

    def everywhere(self, array, bits):
        return [self.bit(array, bit) for bit in bits]

    def across(self, array, k):
        return self.move(array, lambda d, t: (d, t ^ k))

    def line(self, array, step):
        return self.move(array, lambda d, t: (d, t ^ (1 if (d & 1) == step else 2)))


def add(left, right):
    return (left.astype(wide) + right.astype(wide)).astype(low)


def after(*values):
    return lax.optimization_barrier(values)


def per_device(
    dp_size,
    parts,
    tokens,
    page_lengths,
    w_query,
    b_query,
    w_key,
    w_value,
    b_value,
    w_out,
    b_out,
    ln1_gain,
    ln1_bias,
    w_up,
    b_up,
    w_down,
    b_down,
    ln2_gain,
    ln2_bias,
    cotangent,
):
    links = Links(dp_size, parts)
    me = lax.axis_index("tensor")
    place = lax.axis_index("dp") % GROUP
    core, quarter = place & 1, place >> 1
    is_odd = core == 1
    width = tokens.shape[1]
    local = w_query.shape[1]
    rows = width // GROUP
    length = lax.dynamic_slice_in_dim(page_lengths, me, 1, 0)
    info = jnp.concatenate([length, jnp.stack([core, quarter, me]).astype(jnp.int32)])
    attn_w = (w_query.T, w_key.T, w_value.T, w_out)
    piece = core * 4 + quarter

    def cut(array, index):
        return lax.dynamic_slice_in_dim(array, index * rows, rows, 0)

    def mates(held):
        return held + [links.core(array) for array in held]

    a0 = lax.select_n(piece >> 1, *(cut(array, piece & 1) for array in attn_w))
    bias_own = jnp.concatenate([b_query, b_value, b_up])
    bias_rows = jnp.pad(bias_own, (0, 8 * width - bias_own.size)).reshape(8, width)
    a0, piece_d = after(a0, piece)
    d0 = cut(w_down, piece_d)
    u0 = jnp.concatenate([cut(w_up, piece), bias_rows], axis=0)
    vec = jnp.stack([b_out, ln1_gain, ln1_bias, b_down, ln2_gain, ln2_bias, b_down, b_down])
    vec = vec.astype(wide)
    a1, ax = links.line(a0, 0), links.line(a0, 1)
    d1 = links.line(d0, 0)
    a1, u0, vec, tokens_in = after(a1, u0, vec, tokens)
    ay = links.line(a1, 1)
    u1, ux = links.line(u0, 0), links.line(u0, 1)
    own = list(attn_own(info, tokens_in, attn_w[:3], bias_own.astype(wide)[None, None]))
    ax, ay, u1, d1, own[2] = after(ax, ay, u1, d1, own[2])
    a3 = jnp.stack([a1, ax, ay])
    a4, a5 = links.plane(a3, 0), links.plane(a3, 1)
    uy = links.line(u1, 1)
    dx = links.line(d0, 1)
    a4, ux, uy, d1 = after(a4, ux, uy, d1)
    u3 = jnp.stack([u1, ux, uy])
    bias_rest = u3[:, rows:].reshape(parts - 1, 8 * width)[:, : bias_own.size]
    near, far = bias_rest[0], bias_rest[1]
    bias = jnp.stack(
        [bias_own, jnp.where(is_odd, far, near), jnp.where(is_odd, near, far), bias_rest[2]]
    )
    bias = bias.astype(wide)[:, None]
    u3 = u3[:, :rows]
    a6 = links.plane(a4, 1)
    u4, u5 = links.plane(u3, 0), links.plane(u3, 1)
    dy = links.line(d1, 1)
    a5, a6, u4, dx, dy, bias = after(a5, a6, u4, dx, dy, bias)
    d3 = jnp.stack([d1, dx, dy])
    pieces_a = mates([a3, a4, a5, a6])
    u6 = links.plane(u4, 1)
    d4, d5 = links.plane(d3, 0), links.plane(d3, 1)
    qkv, attn_rest_w, ctx, lse, out_rest = attn_rest(info, tokens, bias, pieces_a)
    skip, normed_low, hat, inv = ffn_in(tokens, own[1], ctx, vec, w_out, out_rest)
    u5, u6, d4, lse, inv = after(u5, u6, d4, lse, inv)
    pieces_u = mates([u3, u4, u5, u6])
    d6 = links.plane(d4, 1)
    act, slope, up, mark = ffn_up(info, normed_low, bias, w_up, pieces_u, inv)
    d5, d6, mark = after(d5, d6, mark)
    pieces_d = mates([d3, d4, d5, d6])
    output, grad_branch, branch_low, small, down = ffn_down(
        info, act, skip, vec, cotangent, w_down, pieces_d, mark
    )
    rest = (qkv, ctx, lse)

    def plane_a(keep, got):
        return links.plane(add(keep[1], got[1]), 0), add(keep[0], got[0])

    def plane_b(kept, got):
        return links.plane(add(kept[1], got[1]), 1), add(kept[0], got[0])

    def line_a(both):
        both = both.reshape(-1, 2, parts // 2, rows, width)
        sent = jnp.where(is_odd, both[:, :, 1], both[:, 1])
        return links.line(sent, 1), jnp.where(is_odd, both[:, :, 0], both[:, 0])

    def line_b(kept, got):
        both = add(kept, got)
        return links.line(both[:, 1], 0), both[:, 0]

    def settle(kept, got):
        total = kept.astype(wide) + got.astype(wide)
        bit = GROUP
        while bit < dp_size:
            total = total + links.bit(total, bit)
            bit *= 2
        return total.astype(low)

    keep_c, send_c, mark = down_grad(0, info, act, branch_low, mark)
    got_c = links.core(send_c)
    keep_d, send_d, mark = down_grad(2, info, act, branch_low, mark)
    got_c, send_d, mark = after(got_c, send_d, mark)
    near_c, kept_c = plane_a(keep_c, got_c)
    got_d = links.core(send_d)
    got_d, small = after(got_d, small)
    near_d, kept_d = plane_a(keep_d, got_d)
    grad_residual, residual_low, small, keep_u, send_u = ffn_back(
        info, branch_low, grad_branch, slope, normed_low, hat, inv, vec, small, up, down
    )
    near_c, near_d, send_u, small = after(near_c, near_d, send_u, small)
    got_u = links.core(send_u)
    far_d = links.plane(jnp.concatenate([add(kept_c[1], near_c[1]), add(kept_d[1], near_d[1])]), 1)
    kept_d = jnp.concatenate([add(kept_c[0], near_c[0]), add(kept_d[0], near_d[0])])
    small, joint_a, keep_a, send_a = attn_back(
        0, info, tokens, residual_low, small, w_out, own, out_rest, rest
    )
    got_u, far_d, send_a, small = after(got_u, far_d, send_a, small)
    near_u, kept_u = plane_a(keep_u, got_u)
    got_a = links.core(send_a)
    line_d, kept_d = line_a(add(kept_d, far_d))
    small, joint_b, keep_b, send_b = attn_back(
        2, info, tokens, residual_low, small, w_out, own, out_rest, rest
    )
    near_u, got_a, line_d, send_b, small, grad_residual = after(
        near_u, got_a, line_d, send_b, small, grad_residual
    )
    got_b = links.core(send_b)
    far_u, kept_u = plane_b(kept_u, near_u)
    last_d, kept_d = line_b(kept_d, line_d)
    grad_tokens = grad_tokens_of(grad_residual, joint_a, joint_b, attn_w[:3], attn_rest_w)
    small_got = links.core(small)
    got_b, far_u, last_d, grad_tokens, small_got = after(got_b, far_u, last_d, grad_tokens, small_got)
    small = small + small_got
    size = parts * 2 * rows

    def joined(share, small):
        return jnp.concatenate([share.reshape(-1, width), small.astype(low)], axis=0)

    keep_ab, got_ab = jnp.stack([keep_a, keep_b], axis=2), jnp.stack([got_a, got_b], axis=2)
    near_a = links.plane(joined(add(keep_ab[1], got_ab[1]), small), 0)
    kept_a = add(keep_ab[0], got_ab[0])
    line_u, kept_u = line_a(add(kept_u, far_u))
    near_a, line_u = after(near_a, line_u)
    small = small + near_a[size:].astype(wide)
    near_a = near_a[:size].reshape(kept_a.shape)
    far_a = links.plane(joined(add(kept_a[1], near_a[1]), small), 1)
    kept_a = add(kept_a[0], near_a[0])
    last_u, kept_u = line_b(kept_u, line_u)
    far_a, last_u = after(far_a, last_u)
    size = parts * rows
    small = small + far_a[size:].astype(wide)
    share = add(kept_a, far_a[:size].reshape(kept_a.shape)).reshape(parts, rows, width)
    across = [links.across(joined(share[k], small), k) for k in range(parts - 1, 0, -1)]
    sum_f = jnp.stack([settle(kept_d, last_d)[0], settle(kept_u, last_u)[0]])
    f_x, f_y = links.everywhere(sum_f, (2, 4))
    across, f_x, f_y = after(across, f_x, f_y)
    sum_a = share[0].astype(wide)
    for array in across:
        sum_a = sum_a + array[:rows].astype(wide)
        small = small + array[rows:].astype(wide)
    bit = GROUP
    while bit < dp_size:
        sum_a = sum_a + links.bit(sum_a, bit)
        small = small + links.bit(small, bit)
        bit *= 2
    sum_a = sum_a.astype(low)
    around = links.everywhere(sum_a, (2, 4, 6))
    f_xy = links.plane(jnp.where(is_odd, f_x, f_y), 0)
    held = jnp.stack([sum_f, f_x, f_y])
    *early, mark = finish_ffn(info, held, links.core(held))
    pair = lax.dynamic_index_in_dim(small, 10 + me, 0, keepdims=False)
    grad_b_up = lax.dynamic_index_in_dim(small, 6 + me, 0, keepdims=False)
    around, small, pair, grad_b_up, mark = after(around, small, pair, grad_b_up, mark)
    grad_w_down, grad_w_up = finish_ffn_corner(info, f_xy, links.core(f_xy), mark, *early)
    grad_w_query, grad_w_key, grad_w_value, grad_w_out = finish_attn(info, mates([sum_a] + around))
    grad_w_query, grad_w_key, grad_w_value = grad_w_query.T, grad_w_key.T, grad_w_value.T
    return (
        output,
        grad_tokens,
        grad_w_query,
        pair[:local],
        grad_w_key,
        grad_w_value,
        pair[256 : 256 + local],
        grad_w_out,
        small[0],
        small[1],
        small[2],
        grad_w_up,
        grad_b_up,
        grad_w_down,
        small[3],
        small[4],
        small[5],
    )


def solution(mesh):
    columns, rows, both = P(None, "tensor"), P("tensor", None), P(("dp", "tensor"), None)
    share = P("tensor")
    return jax.shard_map(
        partial(per_device, mesh.shape["dp"], mesh.shape["tensor"]),
        mesh=mesh,
        in_specs=(
            both,
            P("dp"),
            columns,
            share,
            columns,
            columns,
            share,
            rows,
            P(),
            P(),
            P(),
            columns,
            share,
            rows,
            P(),
            P(),
            P(),
            both,
        ),
        out_specs=(
            both,
            both,
            columns,
            share,
            columns,
            columns,
            share,
            rows,
            P(),
            P(),
            P(),
            columns,
            share,
            rows,
            P(),
            P(),
            P(),
        ),
        check_vma=False,
    )
```

```python
from functools import partial

import jax
import jax.numpy as jnp
from jax import lax
from jax.experimental import pallas as pl
from jax.experimental.pallas import tpu as pltpu
from jax.sharding import PartitionSpec as P

HD = 64
SEQ = 512
GROUP = 8
LOG2E = 1.4426950408889634
TAIL_P = 0.39
TAIL = (
    0.23532521908406087,
    0.09138841455460205,
    0.6495593986198918,
    -0.6354002786931026,
    0.8866643698688825,
    -0.22753712513305413,
)

epsilon = 1e-12
masked_score = -1000000000.0
low = jnp.bfloat16
wide = jnp.float32
PEAK = 1.1e15
LIMIT = 12


def mm(left, right, left_dim, right_dim):
    return lax.dot_general(
        left, right, (((left_dim,), (right_dim,)), ((), ())), preferred_element_type=wide
    )


def vmem():
    return pl.BlockSpec(memory_space=pltpu.VMEM)


def smem():
    return pl.BlockSpec(memory_space=pltpu.SMEM)


def hbm():
    return pl.BlockSpec(memory_space=pl.ANY)


def cost(microseconds):
    return pl.CostEstimate(
        flops=int(microseconds * 1e-6 * PEAK), bytes_accessed=1 << 20, transcendentals=0
    )


def params(mebibytes=LIMIT):
    return pltpu.CompilerParams(vmem_limit_bytes=mebibytes << 20)


def shaped(shape, dtype):
    return jax.ShapeDtypeStruct(shape, dtype)


def masked_pad(length, seq):
    row = lax.broadcasted_iota(jnp.int32, (16, seq), 0)
    key = lax.broadcasted_iota(jnp.int32, (16, seq), 1)
    bias = jnp.where((row == 0) & (key >= length), masked_score, 0.0).astype(low)
    ones = jnp.where(row == 0, 1.0, 0.0).astype(low)
    return bias, ones


def as_column(row, ones):
    first = lax.broadcasted_iota(jnp.int32, (16, row.shape[1]), 0) == 0
    return mm(jnp.where(first, row, 0.0).astype(low), ones, 0, 0)


def group_forward(tokens, weights, bias, length, qkv_ref, ctx_ref, lse_ref):
    local = weights[0].shape[0]
    seq = tokens.shape[0]
    scale = HD**-0.5 * LOG2E
    key_pad, ones = masked_pad(length, seq)
    query = (mm(weights[0], tokens, 1, 1) + as_column(bias[:, :local], ones)).astype(low)
    key = mm(weights[1], tokens, 1, 1).astype(low)
    value = mm(weights[2], tokens, 1, 1) + as_column(bias[:, local : 2 * local], ones)
    value = value.astype(low)
    qkv_ref[:local] = query
    qkv_ref[local : 2 * local] = key
    qkv_ref[2 * local :] = value
    for h in range(local // HD):
        part = slice(h * HD, (h + 1) * HD)
        scores = mm(
            jnp.concatenate([key[part], key_pad], 0), jnp.concatenate([query[part], ones], 0), 0, 0
        )
        top = jnp.max(scores, axis=0, keepdims=True)
        probs = jnp.exp2((scores - top) * scale)
        total = jnp.sum(probs, axis=0, keepdims=True)
        context = mm(value[part], probs.astype(low), 1, 0)
        ctx_ref[part] = (context * (1.0 / total)).astype(low)
        lse_ref[h : h + 1] = top * scale + jnp.log2(total)


def gelu_parts(x):
    t = 1.0 / (1.0 + (TAIL_P * 0.5**0.5) * jnp.abs(x))
    poly = TAIL[-1]
    for factor in TAIL[-2::-1]:
        poly = poly * t + factor
    bell = jnp.exp2(x * x * (-0.5 * LOG2E))
    half = 0.5 * poly * t * bell
    cdf = jnp.where(x >= 0, 1.0 - half, half)
    return x * cdf, cdf + x * bell * (0.5 / jnp.pi) ** 0.5


def norm_parts(values):
    centred = values - jnp.mean(values, axis=1, keepdims=True)
    inverse = lax.rsqrt(jnp.mean(centred * centred, axis=1, keepdims=True) + epsilon)
    return centred * inverse, inverse


def norm_back(scaled, normal, inverse):
    return inverse * (
        scaled
        - jnp.mean(scaled, axis=1, keepdims=True)
        - normal * jnp.mean(scaled * normal, axis=1, keepdims=True)
    )


def assemble(info, refs, target, own=None):
    if own is not None:
        target[0] = own[...]
    skip = 1 if own is None else 0
    for s in range(2):
        views = refs[4 * s : 4 * s + 4]
        holder = info[1] ^ s
        order = (1 + holder, 2 - holder, 3)
        for view, move in zip(views, (0,) + order):
            rows = view.shape[1]
            start = pl.multiple_of((holder * 4 + (info[2] ^ move)) * rows, rows)
            for entry, k in enumerate(order):
                target[k - skip, pl.ds(start, rows), :] = view[entry]


def place_pieces(info, scratch, keep_ref, send_ref, entry):
    rows = scratch.shape[0] // GROUP
    for s, target in enumerate((keep_ref, send_ref)):
        half = info[1] ^ s
        for q in range(4):
            move = info[2] ^ q
            x_bit, y_bit = move & 1, move >> 1
            a = jnp.where(half == 0, x_bit, y_bit)
            start = pl.multiple_of((half * 4 + q) * rows, rows)
            target[a, x_bit + y_bit - a, entry] = scratch[pl.ds(start, rows), :]


def attn_own_kernel(info, tokens, w_query, w_key, w_value, bias, qkv, ctx, lse):
    weights = (w_query[...], w_key[...], w_value[...])
    group_forward(tokens[...], weights, bias[0], info[0], qkv.at[0], ctx.at[0], lse.at[0])


def attn_own(info, tokens, weights, bias):
    local, seq = weights[0].shape[0], tokens.shape[0]
    return pl.pallas_call(
        attn_own_kernel,
        in_specs=[smem()] + [vmem()] * 5,
        out_specs=[vmem()] * 3,
        out_shape=[
            shaped((1, 3 * local, seq), low),
            shaped((1, local, seq), low),
            shaped((1, 8, seq), wide),
        ],
        compiler_params=params(),
        cost_estimate=cost(4),
        name="attn_own",
    )(info, tokens, *weights, bias)


def attn_rest_kernel(info, tokens, bias, *refs):
    qkv_out, whole, ctx, lse, out_w, weights, qkv, sems = refs[8:]
    others, local = ctx.shape[:2]
    assemble(info, refs[:8], weights)
    sent = [pltpu.make_async_copy(weights, whole, sems.at[others])]
    sent[0].start()
    out_w[...] = weights[:, 3 * local :]

    def group(k, _):
        joint = tuple(weights[k, i * local : (i + 1) * local] for i in range(3))
        group_forward(
            tokens[...], joint, bias[k + 1], info[0], qkv.at[k], ctx.at[k], lse.at[k]
        )
        pltpu.make_async_copy(qkv.at[k], qkv_out.at[k], sems.at[k]).start()
        return 0

    lax.fori_loop(0, others, group, 0)
    sent += [pltpu.make_async_copy(qkv.at[k], qkv_out.at[k], sems.at[k]) for k in range(others)]
    for copy in sent:
        copy.wait()


def attn_rest(info, tokens, bias, pieces):
    others, rows, cols = pieces[0].shape
    size, seq = rows * GROUP, tokens.shape[0]
    local = size // 4
    joint, whole = (others, 3 * local, seq), (others, size, cols)
    return pl.pallas_call(
        attn_rest_kernel,
        in_specs=[smem()] + [vmem()] * 10,
        out_specs=[pl.BlockSpec(memory_space=pltpu.HBM)] * 2 + [vmem()] * 3,
        out_shape=[
            shaped(joint, low),
            shaped(whole, low),
            shaped((others, local, seq), low),
            shaped((others, 8, seq), wide),
            shaped((others, local, cols), low),
        ],
        scratch_shapes=[
            pltpu.VMEM(whole, low),
            pltpu.VMEM(joint, low),
            pltpu.SemaphoreType.DMA((others + 1,)),
        ],
        compiler_params=params(),
        cost_estimate=cost(8),
        name="attn_rest",
    )(info, tokens, bias, *pieces)


def ffn_in_kernel(tokens, ctx_own, ctx_rest, vec, out_own, out_rest, skip, normed_ref, hat_ref, inv_ref):
    others = ctx_rest.shape[0]
    rows = vec[...]
    b_out, gain_one, bias_one, b_down = (rows[i : i + 1] for i in range(4))
    attended = mm(ctx_own[0], out_own[...], 0, 0)
    for k in range(others):
        attended = attended + mm(ctx_rest[k], out_rest[k], 0, 0)
    hat, inv = norm_parts(tokens[...].astype(wide) + attended + b_out)
    hat_ref[...] = hat
    inv_ref[...] = jnp.broadcast_to(inv, inv_ref.shape)
    normed = hat * gain_one + bias_one
    normed_ref[...] = normed.astype(low)
    skip[...] = normed + b_down


def ffn_in(tokens, ctx_own, ctx_rest, vec, out_own, out_rest):
    seq, width = tokens.shape
    others, local = ctx_rest.shape[:2]
    return pl.pallas_call(
        ffn_in_kernel,
        in_specs=[vmem()] * 6,
        out_specs=[vmem()] * 4,
        out_shape=[
            shaped((seq, width), wide),
            shaped((seq, width), low),
            shaped((seq, width), wide),
            shaped((seq, 128), wide),
        ],
        compiler_params=params(),
        cost_estimate=cost(5),
        name="ffn_in",
    )(tokens, ctx_own, ctx_rest, vec, out_own, out_rest)


def ffn_up_kernel(info, normed, bias, up_own, *refs):
    _, act, slope, up, mark = refs[8:]
    size = up.shape[2]
    first = bias.shape[2] - size
    mark[...] = jnp.zeros(mark.shape, wide)
    assemble(info, refs[:8], up, up_own)

    def forward(k, _):
        preact = mm(normed[...], up[k], 1, 0) + bias[k][:, first:].astype(wide)
        value, derivative = gelu_parts(preact)
        act[k] = value.astype(low)
        slope[k] = derivative.astype(low)
        return 0

    lax.fori_loop(0, act.shape[0], forward, 0)


def ffn_up(info, normed, bias, up_own, pieces, mark):
    seq, width = normed.shape
    others, size = pieces[0].shape[0], up_own.shape[1]
    return pl.pallas_call(
        ffn_up_kernel,
        in_specs=[smem()] + [vmem()] * (3 + 8) + [hbm()],
        out_specs=[vmem()] * 4,
        out_shape=[
            shaped((others + 1, seq, size), low),
            shaped((others + 1, seq, size), low),
            shaped((others + 1, width, size), low),
            shaped((8, 128), wide),
        ],
        compiler_params=params(),
        cost_estimate=cost(11),
        name="ffn_up",
    )(info, normed, bias, up_own, *pieces, mark)


def ffn_down_kernel(info, skip, vec, cot, act, down_own, *refs):
    _, out, grad_ref, branch_ref, small, down = refs[8:]
    parts = act.shape[0]
    assemble(info, refs[:8], down, down_own)
    grad_ref[...] = skip[...]

    def branch(k, _):
        grad_ref[...] += mm(act[k], down[k], 1, 0)
        return 0

    lax.fori_loop(0, parts, branch, 0)
    total = grad_ref[...]
    gain_two, bias_two = vec[4:5], vec[5:6]
    hat_two, inv_two = norm_parts(total)
    out[...] = (hat_two * gain_two + bias_two).astype(low)
    grad = cot[...].astype(wide)
    grad_branch = norm_back(grad * gain_two, hat_two, inv_two)
    grad_ref[...] = grad_branch
    branch_low = grad_branch.astype(low)
    branch_ref[...] = branch_low
    small[...] = jnp.zeros(small.shape, wide)
    small[3:4] = jnp.sum(grad_branch, axis=0, keepdims=True)
    small[4:5] = jnp.sum(grad * hat_two, axis=0, keepdims=True)
    small[5:6] = jnp.sum(grad, axis=0, keepdims=True)


def down_grad_kernel(first, info, act, branch_low, keep, send, mark, scratch):
    mark[...] = jnp.zeros(mark.shape, wide)

    def weight(i, _):
        scratch[...] = mm(act[first + i], branch_low[...], 0, 0).astype(low)
        place_pieces(info, scratch, keep, send, i)
        return 0

    lax.fori_loop(0, 2, weight, 0)


def down_grad(first, info, act, branch_low, mark):
    size, width = act.shape[2], branch_low.shape[1]
    half = halves_shape(2, size, width)
    return pl.pallas_call(
        partial(down_grad_ordered, first),
        in_specs=[smem()] + [vmem()] * 2 + [hbm()],
        out_specs=[vmem()] * 3,
        out_shape=[shaped(half, low), shaped(half, low), shaped((8, 128), wide)],
        scratch_shapes=[pltpu.VMEM((size, width), low)],
        compiler_params=params(),
        cost_estimate=cost(2),
        name="down_grad",
    )(info, act, branch_low, mark)


def down_grad_ordered(first, info, act, branch_low, _, *refs):
    down_grad_kernel(first, info, act, branch_low, *refs)


def halves_shape(entries, rows, cols):
    return (2, 2, entries, rows // GROUP, cols)


def ffn_down(info, act, skip, vec, cot, down_own, pieces, mark):
    parts, seq, size = act.shape
    width = skip.shape[1]
    return pl.pallas_call(
        ffn_down_kernel,
        in_specs=[smem()] + [vmem()] * (5 + 8) + [hbm()],
        out_specs=[vmem()] * 5,
        out_shape=[
            shaped((seq, width), low),
            shaped((seq, width), wide),
            shaped((seq, width), low),
            shaped((16, width), wide),
            shaped((parts, size, width), low),
        ],
        compiler_params=params(),
        cost_estimate=cost(12),
        name="ffn_down",
    )(info, skip, vec, cot, act, down_own, *pieces, mark)


def ffn_back_kernel(
    info, branch_low, grad_branch, normed_low, hat_ref, inv_ref, vec, small_in, slope, up, down,
    grad_ref, residual_ref, small, keep, send, turned, total, scratch,
):
    parts = slope.shape[0]
    index = lax.broadcasted_iota(jnp.int32, small.shape, 0)
    small[...] = small_in[...]
    total[...] = grad_branch[...]
    turned[...] = normed_low[...].T

    def backward(k, _):
        grad_pre = mm(branch_low[...], down[k], 1, 1) * slope[k].astype(wide)
        grad_pre = grad_pre.astype(low)
        sums = jnp.sum(grad_pre.astype(wide), axis=0, keepdims=True)
        small[...] = jnp.where(index == 6 + (info[3] ^ k), sums, small[...])
        scratch[...] = mm(turned[...], grad_pre, 1, 0).astype(low)
        place_pieces(info, scratch, keep, send, k)
        total[...] += mm(grad_pre, up[k], 1, 1)
        return 0

    lax.fori_loop(0, parts, backward, 0)
    grad_normed = total[...]
    hat = hat_ref[...]
    grad_residual = norm_back(grad_normed * vec[1:2], hat, inv_ref[:, :1])
    grad_ref[...] = grad_residual
    residual_ref[...] = grad_residual.astype(low)
    small[0:1] = jnp.sum(grad_residual, axis=0, keepdims=True)
    small[1:2] = jnp.sum(grad_normed * hat, axis=0, keepdims=True)
    small[2:3] = jnp.sum(grad_normed, axis=0, keepdims=True)


def ffn_back(info, branch_low, grad_branch, slope, normed_low, hat, inv, vec, small, up, down):
    _, width, size = up.shape
    parts, seq = slope.shape[:2]
    half = halves_shape(parts, width, size)
    return pl.pallas_call(
        ffn_back_kernel,
        in_specs=[smem()] + [vmem()] * 10,
        out_specs=[vmem()] * 5,
        out_shape=[
            shaped((seq, width), wide),
            shaped((seq, width), low),
            shaped((16, width), wide),
            shaped(half, low),
            shaped(half, low),
        ],
        scratch_shapes=[
            pltpu.VMEM((width, seq), low),
            pltpu.VMEM((seq, width), wide),
            pltpu.VMEM((width, size), low),
        ],
        compiler_params=params(),
        cost_estimate=cost(11),
        name="ffn_back",
    )(info, branch_low, grad_branch, normed_low, hat, inv, vec, small, slope, up, down)


def attn_back_kernel(first, info, tokens, residual_low, small_in, *refs):
    groups = (refs[:4], refs[4:8])
    small, joint, keep, send, scratch = refs[8:]
    local = groups[0][2].shape[1]
    seq, width = tokens.shape
    scale = HD**-0.5
    index = lax.broadcasted_iota(jnp.int32, small.shape, 0)
    small[...] = small_in[...]
    key_pad, query_pad = masked_pad(info[0], seq)
    ones = jnp.ones((8, seq), low)

    def group(i, out_rows, qkv, ctx, lse):
        grad_ctx = mm(out_rows, residual_low[...], 1, 1).astype(low)
        for h in range(local // HD):
            lo, hi = h * HD, (h + 1) * HD
            query = qkv[lo:hi]
            key = qkv[local + lo : local + hi]
            value = qkv[2 * local + lo : 2 * local + hi]
            grad_head = grad_ctx[lo:hi]
            scores = mm(
                jnp.concatenate([key, key_pad], 0), jnp.concatenate([query, query_pad], 0), 0, 0
            )
            probs = jnp.exp2(scores * (scale * LOG2E) - lse[h : h + 1])
            grad_probs = mm(value, grad_head, 0, 0)
            product = probs * grad_probs
            grad_scores = (product - probs * jnp.sum(product, axis=0, keepdims=True)).astype(low)
            joint[i, lo:hi] = (mm(key, grad_scores, 1, 0) * scale).astype(low)
            joint[i, local + lo : local + hi] = (mm(query, grad_scores, 1, 1) * scale).astype(low)
            joint[i, 2 * local + lo : 2 * local + hi] = mm(
                grad_head, probs.astype(low), 1, 1
            ).astype(low)
        grads = joint[i]
        sums = mm(ones, grads, 1, 1)[:1]
        gap = jnp.zeros((1, 256 - local), wide)
        rest = jnp.zeros((1, width - 512), wide)
        sums = jnp.concatenate([sums[:, :local], gap, sums[:, 2 * local :], gap, rest], 1)
        small[...] = jnp.where(index == 10 + (info[3] ^ (first + i)), sums, small[...])
        scratch[: 3 * local] = mm(grads, tokens[...], 1, 0).astype(low)
        scratch[3 * local :] = mm(ctx[...], residual_low[...], 1, 0).astype(low)
        place_pieces(info, scratch, keep, send, i)

    if first == 0:
        for i, (out_w, qkv_ref, ctx_ref, lse_ref) in enumerate(groups):
            group(i, out_w[...] if i == 0 else out_w[0], qkv_ref.at[0], ctx_ref.at[0], lse_ref.at[0])
        return
    out_w, qkv_ref, ctx_ref, lse_ref = groups[0]

    def step(i, _):
        k = first - 1 + i
        group(i, out_w[k], qkv_ref.at[k], ctx_ref.at[k], lse_ref.at[k])
        return 0

    lax.fori_loop(0, 2, step, 0)


def attn_back(first, info, tokens, residual_low, small, out_own, own, out_rest, rest):
    seq, width = tokens.shape
    local = out_own.shape[0]
    arrays = []
    for k in (first, first + 1):
        arrays += (out_own,) + tuple(own) if k == 0 else (out_rest,) + tuple(rest)
    half = halves_shape(2, 4 * local, width)
    return pl.pallas_call(
        partial(attn_back_kernel, first),
        in_specs=[smem()] + [vmem()] * 11,
        out_specs=[vmem()] * 4,
        out_shape=[
            shaped((16, width), wide),
            shaped((2, 3 * local, seq), low),
            shaped(half, low),
            shaped(half, low),
        ],
        scratch_shapes=[pltpu.VMEM((4 * local, width), low)],
        compiler_params=params(),
        cost_estimate=cost(9),
        name="attn_back",
    )(info, tokens, residual_low, small, *arrays)


def grad_tokens_kernel(grad, joint_a, joint_b, w_query, w_key, w_value, rest_w, out):
    local, rows = w_query.shape[0], joint_a.shape[1]
    total = grad[...]
    for i, weights in enumerate((w_query, w_key, w_value)):
        total = total + mm(joint_a[0, i * local : (i + 1) * local], weights[...], 0, 0)
    for k in range(1, 4):
        joint = joint_a[k] if k < 2 else joint_b[k - 2]
        total = total + mm(joint, rest_w[k - 1, :rows], 0, 0)
    out[...] = total.astype(low)


def grad_tokens_of(grad, joint_a, joint_b, weights, rest_w):
    return pl.pallas_call(
        grad_tokens_kernel,
        in_specs=[vmem()] * 7,
        out_specs=vmem(),
        out_shape=shaped(grad.shape, low),
        compiler_params=params(),
        cost_estimate=cost(4),
        name="grad_tokens",
    )(grad, joint_a, joint_b, *weights, rest_w)


def finish_ffn_kernel(info, held, held_mates, down, up, mark):
    rows = held.shape[2]
    mark[...] = jnp.zeros(mark.shape, wide)
    for s, pieces in enumerate((held, held_mates)):
        holder = info[1] ^ s
        for move in range(3):
            start = pl.multiple_of((holder * 4 + (info[2] ^ move)) * rows, rows)
            down[pl.ds(start, rows), :] = pieces[move, 0].astype(wide)
            up[pl.ds(start, rows), :] = pieces[move, 1].astype(wide)
        start = pl.multiple_of((holder * 4 + (info[2] ^ 3)) * rows, rows)
        down[pl.ds(start, rows), :] = jnp.zeros((rows, down.shape[1]), wide)
        up[pl.ds(start, rows), :] = jnp.zeros((rows, up.shape[1]), wide)


def finish_ffn(info, held, mates):
    _, _, rows, cols = held.shape
    return pl.pallas_call(
        finish_ffn_kernel,
        in_specs=[smem()] + [vmem()] * 2,
        out_specs=[vmem()] * 3,
        out_shape=[shaped((GROUP * rows, cols), wide)] * 2 + [shaped((8, 128), wide)],
        compiler_params=params(),
        cost_estimate=cost(3),
        name="finish_ffn",
    )(info, held, mates)


def finish_ffn_corner_kernel(info, corner, corner_mate, mark, down_in, up_in, down, up, ready, sems):
    rows = corner.shape[1]
    copies = []
    for s, pieces in enumerate((corner, corner_mate)):
        holder = info[1] ^ s
        start = pl.multiple_of((holder * 4 + (info[2] ^ 3)) * rows, rows)
        for i, target in enumerate((down, up)):
            ready[s, i] = pieces[i].astype(wide)
            copies.append(
                pltpu.make_async_copy(ready.at[s, i], target.at[pl.ds(start, rows), :], sems.at[s, i])
            )
            copies[-1].start()
    for copy in copies:
        copy.wait()


def finish_ffn_corner(info, corner, corner_mate, mark, down, up):
    _, rows, cols = corner.shape
    return pl.pallas_call(
        finish_ffn_corner_kernel,
        in_specs=[smem()] + [vmem()] * 2 + [hbm()] * 3,
        out_specs=[hbm()] * 2,
        out_shape=[shaped(down.shape, wide)] * 2,
        scratch_shapes=[pltpu.VMEM((2, 2, rows, cols), wide), pltpu.SemaphoreType.DMA((2, 2))],
        input_output_aliases={4: 0, 5: 1},
        compiler_params=params(),
        cost_estimate=cost(1),
        name="finish_ffn_corner",
    )(info, corner, corner_mate, mark, down, up)


def finish_attn_kernel(info, *refs):
    query, key, value, out, whole = refs[8:]
    for s in range(2):
        holder = info[1] ^ s
        for move in range(4):
            view = refs[4 * s + move]
            rows = view.shape[0]
            start = pl.multiple_of((holder * 4 + (info[2] ^ move)) * rows, rows)
            whole[pl.ds(start, rows), :] = view[...].astype(wide)
    local = whole.shape[0] // 4
    query[...] = whole[:local]
    key[...] = whole[local : 2 * local]
    value[...] = whole[2 * local : 3 * local]
    out[...] = whole[3 * local :]


def finish_attn(info, pieces):
    rows, cols = pieces[0].shape
    size = GROUP * rows
    local = size // 4
    return pl.pallas_call(
        finish_attn_kernel,
        in_specs=[smem()] + [vmem()] * 8,
        out_specs=[vmem()] * 4,
        out_shape=[shaped((local, cols), wide)] * 4,
        scratch_shapes=[pltpu.VMEM((size, cols), wide)],
        compiler_params=params(),
        cost_estimate=cost(2),
        name="finish_attn",
    )(info, *pieces)


class Links:
    def __init__(self, dp_size, parts):
        self.dp_size, self.parts = dp_size, parts

    def move(self, array, partner):
        pairs = []
        for d in range(self.dp_size):
            for t in range(self.parts):
                to_d, to_t = partner(d, t)
                pairs.append((d * self.parts + t, to_d * self.parts + to_t))
        return lax.ppermute(array, ("dp", "tensor"), pairs)

    def bit(self, array, bit):
        return self.move(array, lambda d, t: (d ^ bit, t))

    def core(self, array):
        return self.bit(array, 1)

    def plane(self, array, step):
        return self.move(array, lambda d, t: (d ^ (2 if (d & 1) == step else 4), t))

    def everywhere(self, array, bits):
        return [self.bit(array, bit) for bit in bits]

    def across(self, array, k):
        return self.move(array, lambda d, t: (d, t ^ k))

    def line(self, array, step):
        return self.move(array, lambda d, t: (d, t ^ (1 if (d & 1) == step else 2)))


def add(left, right):
    return (left.astype(wide) + right.astype(wide)).astype(low)


def after(*values):
    return lax.optimization_barrier(values)


def per_device(
    dp_size,
    parts,
    tokens,
    page_lengths,
    w_query,
    b_query,
    w_key,
    w_value,
    b_value,
    w_out,
    b_out,
    ln1_gain,
    ln1_bias,
    w_up,
    b_up,
    w_down,
    b_down,
    ln2_gain,
    ln2_bias,
    cotangent,
):
    links = Links(dp_size, parts)
    me = lax.axis_index("tensor")
    place = lax.axis_index("dp") % GROUP
    core, quarter = place & 1, place >> 1
    is_odd = core == 1
    width = tokens.shape[1]
    local = w_query.shape[1]
    rows = width // GROUP
    length = lax.dynamic_slice_in_dim(page_lengths, me, 1, 0)
    info = jnp.concatenate([length, jnp.stack([core, quarter, me]).astype(jnp.int32)])
    attn_w = (w_query.T, w_key.T, w_value.T, w_out)
    piece = core * 4 + quarter

    def cut(array, index):
        return lax.dynamic_slice_in_dim(array, index * rows, rows, 0)

    def mates(held):
        return held + [links.core(array) for array in held]

    a0 = lax.select_n(piece >> 1, *(cut(array, piece & 1) for array in attn_w))
    bias_own = jnp.concatenate([b_query, b_value, b_up])
    bias_rows = jnp.pad(bias_own, (0, 8 * width - bias_own.size)).reshape(8, width)
    a0, piece_d = after(a0, piece)
    d0 = cut(w_down, piece_d)
    u0 = jnp.concatenate([cut(w_up, piece), bias_rows], axis=0)
    vec = jnp.stack([b_out, ln1_gain, ln1_bias, b_down, ln2_gain, ln2_bias, b_down, b_down])
    vec = vec.astype(wide)
    a1, ax = links.line(a0, 0), links.line(a0, 1)
    d1 = links.line(d0, 0)
    a1, u0, vec, tokens_in = after(a1, u0, vec, tokens)
    ay = links.line(a1, 1)
    u1, ux = links.line(u0, 0), links.line(u0, 1)
    own = list(attn_own(info, tokens_in, attn_w[:3], bias_own.astype(wide)[None, None]))
    ax, ay, u1, d1, own[2] = after(ax, ay, u1, d1, own[2])
    a3 = jnp.stack([a1, ax, ay])
    a4, a5 = links.plane(a3, 0), links.plane(a3, 1)
    uy = links.line(u1, 1)
    dx = links.line(d0, 1)
    a4, ux, uy, d1 = after(a4, ux, uy, d1)
    u3 = jnp.stack([u1, ux, uy])
    bias_rest = u3[:, rows:].reshape(parts - 1, 8 * width)[:, : bias_own.size]
    near, far = bias_rest[0], bias_rest[1]
    bias = jnp.stack(
        [bias_own, jnp.where(is_odd, far, near), jnp.where(is_odd, near, far), bias_rest[2]]
    )
    bias = bias.astype(wide)[:, None]
    u3 = u3[:, :rows]
    a6 = links.plane(a4, 1)
    u4, u5 = links.plane(u3, 0), links.plane(u3, 1)
    dy = links.line(d1, 1)
    a5, a6, u4, dx, dy, bias = after(a5, a6, u4, dx, dy, bias)
    d3 = jnp.stack([d1, dx, dy])
    pieces_a = mates([a3, a4, a5, a6])
    u6 = links.plane(u4, 1)
    d4, d5 = links.plane(d3, 0), links.plane(d3, 1)
    qkv, attn_rest_w, ctx, lse, out_rest = attn_rest(info, tokens, bias, pieces_a)
    skip, normed_low, hat, inv = ffn_in(tokens, own[1], ctx, vec, w_out, out_rest)
    u5, u6, d4, lse, inv = after(u5, u6, d4, lse, inv)
    pieces_u = mates([u3, u4, u5, u6])
    d6 = links.plane(d4, 1)
    act, slope, up, mark = ffn_up(info, normed_low, bias, w_up, pieces_u, inv)
    d5, d6, mark = after(d5, d6, mark)
    pieces_d = mates([d3, d4, d5, d6])
    output, grad_branch, branch_low, small, down = ffn_down(
        info, act, skip, vec, cotangent, w_down, pieces_d, mark
    )
    rest = (qkv, ctx, lse)

    def plane_a(keep, got):
        return links.plane(add(keep[1], got[1]), 0), add(keep[0], got[0])

    def plane_b(kept, got):
        return links.plane(add(kept[1], got[1]), 1), add(kept[0], got[0])

    def line_a(both):
        both = both.reshape(-1, 2, parts // 2, rows, width)
        sent = jnp.where(is_odd, both[:, :, 1], both[:, 1])
        return links.line(sent, 1), jnp.where(is_odd, both[:, :, 0], both[:, 0])

    def line_b(kept, got):
        both = add(kept, got)
        return links.line(both[:, 1], 0), both[:, 0]

    def settle(kept, got):
        total = kept.astype(wide) + got.astype(wide)
        bit = GROUP
        while bit < dp_size:
            total = total + links.bit(total, bit)
            bit *= 2
        return total.astype(low)

    keep_c, send_c, mark = down_grad(0, info, act, branch_low, mark)
    got_c = links.core(send_c)
    keep_d, send_d, mark = down_grad(2, info, act, branch_low, mark)
    got_c, send_d, mark = after(got_c, send_d, mark)
    near_c, kept_c = plane_a(keep_c, got_c)
    got_d = links.core(send_d)
    got_d, small = after(got_d, small)
    near_d, kept_d = plane_a(keep_d, got_d)
    grad_residual, residual_low, small, keep_u, send_u = ffn_back(
        info, branch_low, grad_branch, slope, normed_low, hat, inv, vec, small, up, down
    )
    near_c, near_d, send_u, small = after(near_c, near_d, send_u, small)
    got_u = links.core(send_u)
    far_d = links.plane(jnp.concatenate([add(kept_c[1], near_c[1]), add(kept_d[1], near_d[1])]), 1)
    kept_d = jnp.concatenate([add(kept_c[0], near_c[0]), add(kept_d[0], near_d[0])])
    small, joint_a, keep_a, send_a = attn_back(
        0, info, tokens, residual_low, small, w_out, own, out_rest, rest
    )
    got_u, far_d, send_a, small = after(got_u, far_d, send_a, small)
    near_u, kept_u = plane_a(keep_u, got_u)
    got_a = links.core(send_a)
    line_d, kept_d = line_a(add(kept_d, far_d))
    small, joint_b, keep_b, send_b = attn_back(
        2, info, tokens, residual_low, small, w_out, own, out_rest, rest
    )
    near_u, got_a, line_d, send_b, small, grad_residual = after(
        near_u, got_a, line_d, send_b, small, grad_residual
    )
    got_b = links.core(send_b)
    far_u, kept_u = plane_b(kept_u, near_u)
    last_d, kept_d = line_b(kept_d, line_d)
    grad_tokens = grad_tokens_of(grad_residual, joint_a, joint_b, attn_w[:3], attn_rest_w)
    small_got = links.core(small)
    got_a, got_b, far_u, last_d, grad_tokens, small_got = after(
        got_a, got_b, far_u, last_d, grad_tokens, small_got
    )
    small = small + small_got

    def joined(share, small):
        return jnp.concatenate([share.reshape(-1, width), small.astype(low)], axis=0)

    near_a, kept_a = plane_a(keep_a, got_a)
    near_b = links.plane(joined(add(keep_b[1], got_b[1]), small), 0)
    kept_b = add(keep_b[0], got_b[0])
    line_u, kept_u = line_a(add(kept_u, far_u))
    near_a, near_b, line_u = after(near_a, near_b, line_u)
    size = 4 * rows
    far_a, kept_a = plane_b(kept_a, near_a)
    small = small + near_b[size:].astype(wide)
    near_b = near_b[:size].reshape(kept_b.shape)
    size = 2 * rows
    far_b = links.plane(joined(add(kept_b[1], near_b[1]), small), 1)
    kept_b = add(kept_b[0], near_b[0])
    last_u, kept_u = line_b(kept_u, line_u)
    far_a, far_b = after(far_a, far_b)
    small = small + far_b[size:].astype(wide)
    share = jnp.concatenate([add(kept_a, far_a), add(kept_b, far_b[:size].reshape(kept_b.shape))])
    across = [links.across(joined(share[k], small), k) for k in range(parts - 1, 0, -1)]
    sum_f = jnp.stack([settle(kept_d, last_d)[0], settle(kept_u, last_u)[0]])
    f_x, f_y = links.everywhere(sum_f, (2, 4))
    across, f_x, f_y = after(across, f_x, f_y)
    sum_a = share[0].astype(wide)
    for array in across:
        sum_a = sum_a + array[:rows].astype(wide)
        small = small + array[rows:].astype(wide)
    bit = GROUP
    while bit < dp_size:
        sum_a = sum_a + links.bit(sum_a, bit)
        small = small + links.bit(small, bit)
        bit *= 2
    sum_a = sum_a.astype(low)
    around = links.everywhere(sum_a, (2, 4, 6))
    f_xy = links.plane(jnp.where(is_odd, f_x, f_y), 0)
    held = jnp.stack([sum_f, f_x, f_y])
    *early, mark = finish_ffn(info, held, links.core(held))
    pair = lax.dynamic_index_in_dim(small, 10 + me, 0, keepdims=False)
    grad_b_up = lax.dynamic_index_in_dim(small, 6 + me, 0, keepdims=False)
    around, small, pair, grad_b_up, mark = after(around, small, pair, grad_b_up, mark)
    grad_w_down, grad_w_up = finish_ffn_corner(info, f_xy, links.core(f_xy), mark, *early)
    grad_w_query, grad_w_key, grad_w_value, grad_w_out = finish_attn(info, mates([sum_a] + around))
    grad_w_query, grad_w_key, grad_w_value = grad_w_query.T, grad_w_key.T, grad_w_value.T
    return (
        output,
        grad_tokens,
        grad_w_query,
        pair[:local],
        grad_w_key,
        grad_w_value,
        pair[256 : 256 + local],
        grad_w_out,
        small[0],
        small[1],
        small[2],
        grad_w_up,
        grad_b_up,
        grad_w_down,
        small[3],
        small[4],
        small[5],
    )


def solution(mesh):
    columns, rows, both = P(None, "tensor"), P("tensor", None), P(("dp", "tensor"), None)
    share = P("tensor")
    return jax.shard_map(
        partial(per_device, mesh.shape["dp"], mesh.shape["tensor"]),
        mesh=mesh,
        in_specs=(
            both,
            P("dp"),
            columns,
            share,
            columns,
            columns,
            share,
            rows,
            P(),
            P(),
            P(),
            columns,
            share,
            rows,
            P(),
            P(),
            P(),
            both,
        ),
        out_specs=(
            both,
            both,
            columns,
            share,
            columns,
            columns,
            share,
            rows,
            P(),
            P(),
            P(),
            columns,
            share,
            rows,
            P(),
            P(),
            P(),
        ),
        check_vma=False,
    )
```

```python
from functools import partial

import jax
import jax.numpy as jnp
from jax import lax
from jax.experimental import pallas as pl
from jax.experimental.pallas import tpu as pltpu
from jax.sharding import PartitionSpec as P

HD = 64
SEQ = 512
GROUP = 8
LOG2E = 1.4426950408889634
TAIL_P = 0.39
TAIL = (
    0.23532521908406087,
    0.09138841455460205,
    0.6495593986198918,
    -0.6354002786931026,
    0.8866643698688825,
    -0.22753712513305413,
)

epsilon = 1e-12
masked_score = -1000000000.0
low = jnp.bfloat16
wide = jnp.float32
PEAK = 1.1e15
LIMIT = 16


def mm(left, right, left_dim, right_dim):
    return lax.dot_general(
        left, right, (((left_dim,), (right_dim,)), ((), ())), preferred_element_type=wide
    )


def vmem():
    return pl.BlockSpec(memory_space=pltpu.VMEM)


def smem():
    return pl.BlockSpec(memory_space=pltpu.SMEM)


def hbm():
    return pl.BlockSpec(memory_space=pl.ANY)


def cost(microseconds):
    return pl.CostEstimate(
        flops=int(microseconds * 1e-6 * PEAK), bytes_accessed=1 << 20, transcendentals=0
    )


def params(mebibytes=LIMIT):
    return pltpu.CompilerParams(vmem_limit_bytes=mebibytes << 20)


def shaped(shape, dtype):
    return jax.ShapeDtypeStruct(shape, dtype)


def masked_pad(length, seq):
    row = lax.broadcasted_iota(jnp.int32, (16, seq), 0)
    key = lax.broadcasted_iota(jnp.int32, (16, seq), 1)
    bias = jnp.where((row == 0) & (key >= length), masked_score, 0.0).astype(low)
    ones = jnp.where(row == 0, 1.0, 0.0).astype(low)
    return bias, ones


def as_column(row, ones):
    first = lax.broadcasted_iota(jnp.int32, (16, row.shape[1]), 0) == 0
    return mm(jnp.where(first, row, 0.0).astype(low), ones, 0, 0)


def group_forward(tokens, weights, bias, length, qkv_ref, ctx_ref, lse_ref):
    local = weights[0].shape[0]
    seq = tokens.shape[0]
    scale = HD**-0.5 * LOG2E
    key_pad, ones = masked_pad(length, seq)
    query = (mm(weights[0], tokens, 1, 1) + as_column(bias[:, :local], ones)).astype(low)
    key = mm(weights[1], tokens, 1, 1).astype(low)
    value = mm(weights[2], tokens, 1, 1) + as_column(bias[:, local : 2 * local], ones)
    value = value.astype(low)
    qkv_ref[:local] = query
    qkv_ref[local : 2 * local] = key
    qkv_ref[2 * local :] = value
    for h in range(local // HD):
        part = slice(h * HD, (h + 1) * HD)
        scores = mm(
            jnp.concatenate([key[part], key_pad], 0), jnp.concatenate([query[part], ones], 0), 0, 0
        )
        top = jnp.max(scores, axis=0, keepdims=True)
        probs = jnp.exp2((scores - top) * scale)
        total = jnp.sum(probs, axis=0, keepdims=True)
        context = mm(value[part], probs.astype(low), 1, 0)
        ctx_ref[part] = (context * (1.0 / total)).astype(low)
        lse_ref[h : h + 1] = top * scale + jnp.log2(total)


def gelu_parts(x):
    t = 1.0 / (1.0 + (TAIL_P * 0.5**0.5) * jnp.abs(x))
    poly = TAIL[-1]
    for factor in TAIL[-2::-1]:
        poly = poly * t + factor
    bell = jnp.exp2(x * x * (-0.5 * LOG2E))
    half = 0.5 * poly * t * bell
    cdf = jnp.where(x >= 0, 1.0 - half, half)
    return x * cdf, cdf + x * bell * (0.5 / jnp.pi) ** 0.5


def norm_parts(values):
    centred = values - jnp.mean(values, axis=1, keepdims=True)
    inverse = lax.rsqrt(jnp.mean(centred * centred, axis=1, keepdims=True) + epsilon)
    return centred * inverse, inverse


def norm_back(scaled, normal, inverse):
    return inverse * (
        scaled
        - jnp.mean(scaled, axis=1, keepdims=True)
        - normal * jnp.mean(scaled * normal, axis=1, keepdims=True)
    )


def assemble(info, refs, target, own=None):
    if own is not None:
        target[0] = own[...]
    skip = 1 if own is None else 0
    for s in range(2):
        views = refs[4 * s : 4 * s + 4]
        holder = info[1] ^ s
        order = (1 + holder, 2 - holder, 3)
        for view, move in zip(views, (0,) + order):
            rows = view.shape[1]
            start = pl.multiple_of((holder * 4 + (info[2] ^ move)) * rows, rows)
            for entry, k in enumerate(order):
                target[k - skip, pl.ds(start, rows), :] = view[entry]


def place_pieces(info, scratch, keep_ref, send_ref, entry):
    rows = scratch.shape[0] // GROUP
    for s, target in enumerate((keep_ref, send_ref)):
        half = info[1] ^ s
        for q in range(4):
            move = info[2] ^ q
            x_bit, y_bit = move & 1, move >> 1
            a = jnp.where(half == 0, x_bit, y_bit)
            start = pl.multiple_of((half * 4 + q) * rows, rows)
            target[a, x_bit + y_bit - a, entry] = scratch[pl.ds(start, rows), :]


def attn_own_kernel(info, tokens, w_query, w_key, w_value, bias, qkv, ctx, lse):
    weights = (w_query[...], w_key[...], w_value[...])
    group_forward(tokens[...], weights, bias[0], info[0], qkv.at[0], ctx.at[0], lse.at[0])


def attn_own(info, tokens, weights, bias):
    local, seq = weights[0].shape[0], tokens.shape[0]
    return pl.pallas_call(
        attn_own_kernel,
        in_specs=[smem()] + [vmem()] * 5,
        out_specs=[vmem()] * 3,
        out_shape=[
            shaped((1, 3 * local, seq), low),
            shaped((1, local, seq), low),
            shaped((1, 8, seq), wide),
        ],
        compiler_params=params(),
        cost_estimate=cost(4),
        name="attn_own",
    )(info, tokens, *weights, bias)


def attn_rest_kernel(info, tokens, bias, *refs):
    qkv_out, whole, ctx, lse, out_w, weights, qkv, sems = refs[8:]
    others, local = ctx.shape[:2]
    assemble(info, refs[:8], weights)
    sent = [pltpu.make_async_copy(weights, whole, sems.at[others])]
    sent[0].start()
    out_w[...] = weights[:, 3 * local :]

    def group(k, _):
        joint = tuple(weights[k, i * local : (i + 1) * local] for i in range(3))
        group_forward(
            tokens[...], joint, bias[k + 1], info[0], qkv.at[k], ctx.at[k], lse.at[k]
        )
        pltpu.make_async_copy(qkv.at[k], qkv_out.at[k], sems.at[k]).start()
        return 0

    lax.fori_loop(0, others, group, 0)
    sent += [pltpu.make_async_copy(qkv.at[k], qkv_out.at[k], sems.at[k]) for k in range(others)]
    for copy in sent:
        copy.wait()


def attn_rest(info, tokens, bias, pieces):
    others, rows, cols = pieces[0].shape
    size, seq = rows * GROUP, tokens.shape[0]
    local = size // 4
    joint, whole = (others, 3 * local, seq), (others, size, cols)
    return pl.pallas_call(
        attn_rest_kernel,
        in_specs=[smem()] + [vmem()] * 10,
        out_specs=[pl.BlockSpec(memory_space=pltpu.HBM)] * 2 + [vmem()] * 3,
        out_shape=[
            shaped(joint, low),
            shaped(whole, low),
            shaped((others, local, seq), low),
            shaped((others, 8, seq), wide),
            shaped((others, local, cols), low),
        ],
        scratch_shapes=[
            pltpu.VMEM(whole, low),
            pltpu.VMEM(joint, low),
            pltpu.SemaphoreType.DMA((others + 1,)),
        ],
        compiler_params=params(),
        cost_estimate=cost(8),
        name="attn_rest",
    )(info, tokens, bias, *pieces)


def ffn_in_kernel(tokens, ctx_own, ctx_rest, vec, out_own, out_rest, skip, normed_ref, hat_ref, inv_ref):
    others = ctx_rest.shape[0]
    rows = vec[...]
    b_out, gain_one, bias_one, b_down = (rows[i : i + 1] for i in range(4))
    attended = mm(ctx_own[0], out_own[...], 0, 0)
    for k in range(others):
        attended = attended + mm(ctx_rest[k], out_rest[k], 0, 0)
    hat, inv = norm_parts(tokens[...].astype(wide) + attended + b_out)
    hat_ref[...] = hat
    inv_ref[...] = jnp.broadcast_to(inv, inv_ref.shape)
    normed = hat * gain_one + bias_one
    normed_ref[...] = normed.astype(low)
    skip[...] = normed + b_down


def ffn_in(tokens, ctx_own, ctx_rest, vec, out_own, out_rest):
    seq, width = tokens.shape
    others, local = ctx_rest.shape[:2]
    return pl.pallas_call(
        ffn_in_kernel,
        in_specs=[vmem()] * 6,
        out_specs=[vmem()] * 4,
        out_shape=[
            shaped((seq, width), wide),
            shaped((seq, width), low),
            shaped((seq, width), wide),
            shaped((seq, 128), wide),
        ],
        compiler_params=params(),
        cost_estimate=cost(5),
        name="ffn_in",
    )(tokens, ctx_own, ctx_rest, vec, out_own, out_rest)


def ffn_up_kernel(info, normed, bias, up_own, *refs):
    _, act, slope, up, mark = refs[8:]
    size = up.shape[2]
    first = bias.shape[2] - size
    mark[...] = jnp.zeros(mark.shape, wide)
    assemble(info, refs[:8], up, up_own)

    def forward(k, _):
        preact = mm(normed[...], up[k], 1, 0) + bias[k][:, first:].astype(wide)
        value, derivative = gelu_parts(preact)
        act[k] = value.astype(low)
        slope[k] = derivative.astype(low)
        return 0

    lax.fori_loop(0, act.shape[0], forward, 0)


def ffn_up(info, normed, bias, up_own, pieces, mark):
    seq, width = normed.shape
    others, size = pieces[0].shape[0], up_own.shape[1]
    return pl.pallas_call(
        ffn_up_kernel,
        in_specs=[smem()] + [vmem()] * (3 + 8) + [hbm()],
        out_specs=[vmem()] * 4,
        out_shape=[
            shaped((others + 1, seq, size), low),
            shaped((others + 1, seq, size), low),
            shaped((others + 1, width, size), low),
            shaped((8, 128), wide),
        ],
        compiler_params=params(),
        cost_estimate=cost(11),
        name="ffn_up",
    )(info, normed, bias, up_own, *pieces, mark)


def ffn_down_kernel(info, skip, vec, cot, act, down_own, *refs):
    _, out, grad_ref, branch_ref, small, down = refs[8:]
    parts = act.shape[0]
    assemble(info, refs[:8], down, down_own)
    grad_ref[...] = skip[...]
    total = grad_ref[...]
    for k in range(parts):
        total = total + mm(act[k], down[k], 1, 0)
    gain_two, bias_two = vec[4:5], vec[5:6]
    hat_two, inv_two = norm_parts(total)
    out[...] = (hat_two * gain_two + bias_two).astype(low)
    grad = cot[...].astype(wide)
    grad_branch = norm_back(grad * gain_two, hat_two, inv_two)
    grad_ref[...] = grad_branch
    branch_low = grad_branch.astype(low)
    branch_ref[...] = branch_low
    small[...] = jnp.zeros(small.shape, wide)
    small[3:4] = jnp.sum(grad_branch, axis=0, keepdims=True)
    small[4:5] = jnp.sum(grad * hat_two, axis=0, keepdims=True)
    small[5:6] = jnp.sum(grad, axis=0, keepdims=True)


def down_grad_kernel(first, info, act, branch_low, keep, send, mark, scratch):
    mark[...] = jnp.zeros(mark.shape, wide)

    def weight(i, _):
        scratch[...] = mm(act[first + i], branch_low[...], 0, 0).astype(low)
        place_pieces(info, scratch, keep, send, i)
        return 0

    lax.fori_loop(0, 2, weight, 0)


def down_grad(first, info, act, branch_low, mark):
    size, width = act.shape[2], branch_low.shape[1]
    half = halves_shape(2, size, width)
    return pl.pallas_call(
        partial(down_grad_ordered, first),
        in_specs=[smem()] + [vmem()] * 2 + [hbm()],
        out_specs=[vmem()] * 3,
        out_shape=[shaped(half, low), shaped(half, low), shaped((8, 128), wide)],
        scratch_shapes=[pltpu.VMEM((size, width), low)],
        compiler_params=params(),
        cost_estimate=cost(2),
        name="down_grad",
    )(info, act, branch_low, mark)


def down_grad_ordered(first, info, act, branch_low, _, *refs):
    down_grad_kernel(first, info, act, branch_low, *refs)


def halves_shape(entries, rows, cols):
    return (2, 2, entries, rows // GROUP, cols)


def ffn_down(info, act, skip, vec, cot, down_own, pieces, mark):
    parts, seq, size = act.shape
    width = skip.shape[1]
    return pl.pallas_call(
        ffn_down_kernel,
        in_specs=[smem()] + [vmem()] * (5 + 8) + [hbm()],
        out_specs=[vmem()] * 5,
        out_shape=[
            shaped((seq, width), low),
            shaped((seq, width), wide),
            shaped((seq, width), low),
            shaped((16, width), wide),
            shaped((parts, size, width), low),
        ],
        compiler_params=params(),
        cost_estimate=cost(12),
        name="ffn_down",
    )(info, skip, vec, cot, act, down_own, *pieces, mark)


def ffn_back_kernel(
    info, branch_low, grad_branch, normed_low, hat_ref, inv_ref, vec, small_in, slope, up, down,
    grad_ref, residual_ref, small, keep, send, turned, total, scratch,
):
    parts = slope.shape[0]
    index = lax.broadcasted_iota(jnp.int32, small.shape, 0)
    small[...] = small_in[...]
    total[...] = grad_branch[...]
    turned[...] = normed_low[...].T

    def backward(k, _):
        grad_pre = mm(branch_low[...], down[k], 1, 1) * slope[k].astype(wide)
        grad_pre = grad_pre.astype(low)
        sums = jnp.sum(grad_pre.astype(wide), axis=0, keepdims=True)
        small[...] = jnp.where(index == 6 + (info[3] ^ k), sums, small[...])
        scratch[...] = mm(turned[...], grad_pre, 1, 0).astype(low)
        place_pieces(info, scratch, keep, send, k)
        total[...] += mm(grad_pre, up[k], 1, 1)
        return 0

    lax.fori_loop(0, parts, backward, 0)
    grad_normed = total[...]
    hat = hat_ref[...]
    grad_residual = norm_back(grad_normed * vec[1:2], hat, inv_ref[:, :1])
    grad_ref[...] = grad_residual
    residual_ref[...] = grad_residual.astype(low)
    small[0:1] = jnp.sum(grad_residual, axis=0, keepdims=True)
    small[1:2] = jnp.sum(grad_normed * hat, axis=0, keepdims=True)
    small[2:3] = jnp.sum(grad_normed, axis=0, keepdims=True)


def ffn_back(info, branch_low, grad_branch, slope, normed_low, hat, inv, vec, small, up, down):
    _, width, size = up.shape
    parts, seq = slope.shape[:2]
    half = halves_shape(parts, width, size)
    return pl.pallas_call(
        ffn_back_kernel,
        in_specs=[smem()] + [vmem()] * 10,
        out_specs=[vmem()] * 5,
        out_shape=[
            shaped((seq, width), wide),
            shaped((seq, width), low),
            shaped((16, width), wide),
            shaped(half, low),
            shaped(half, low),
        ],
        scratch_shapes=[
            pltpu.VMEM((width, seq), low),
            pltpu.VMEM((seq, width), wide),
            pltpu.VMEM((width, size), low),
        ],
        compiler_params=params(),
        cost_estimate=cost(11),
        name="ffn_back",
    )(info, branch_low, grad_branch, normed_low, hat, inv, vec, small, slope, up, down)


def attn_back_kernel(first, info, tokens, residual_low, small_in, *refs):
    groups = (refs[:4], refs[4:8])
    small, joint, keep, send, scratch = refs[8:]
    local = groups[0][2].shape[1]
    seq, width = tokens.shape
    scale = HD**-0.5
    index = lax.broadcasted_iota(jnp.int32, small.shape, 0)
    small[...] = small_in[...]
    key_pad, query_pad = masked_pad(info[0], seq)
    ones = jnp.ones((8, seq), low)

    def group(i, out_rows, qkv, ctx, lse):
        grad_ctx = mm(out_rows, residual_low[...], 1, 1).astype(low)
        for h in range(local // HD):
            lo, hi = h * HD, (h + 1) * HD
            query = qkv[lo:hi]
            key = qkv[local + lo : local + hi]
            value = qkv[2 * local + lo : 2 * local + hi]
            grad_head = grad_ctx[lo:hi]
            scores = mm(
                jnp.concatenate([key, key_pad], 0), jnp.concatenate([query, query_pad], 0), 0, 0
            )
            probs = jnp.exp2(scores * (scale * LOG2E) - lse[h : h + 1])
            grad_probs = mm(value, grad_head, 0, 0)
            product = probs * grad_probs
            grad_scores = (product - probs * jnp.sum(product, axis=0, keepdims=True)).astype(low)
            joint[i, lo:hi] = (mm(key, grad_scores, 1, 0) * scale).astype(low)
            joint[i, local + lo : local + hi] = (mm(query, grad_scores, 1, 1) * scale).astype(low)
            joint[i, 2 * local + lo : 2 * local + hi] = mm(
                grad_head, probs.astype(low), 1, 1
            ).astype(low)
        grads = joint[i]
        sums = mm(ones, grads, 1, 1)[:1]
        gap = jnp.zeros((1, 256 - local), wide)
        rest = jnp.zeros((1, width - 512), wide)
        sums = jnp.concatenate([sums[:, :local], gap, sums[:, 2 * local :], gap, rest], 1)
        small[...] = jnp.where(index == 10 + (info[3] ^ (first + i)), sums, small[...])
        scratch[: 3 * local] = mm(grads, tokens[...], 1, 0).astype(low)
        scratch[3 * local :] = mm(ctx[...], residual_low[...], 1, 0).astype(low)
        place_pieces(info, scratch, keep, send, i)

    if first == 0:
        for i, (out_w, qkv_ref, ctx_ref, lse_ref) in enumerate(groups):
            group(i, out_w[...] if i == 0 else out_w[0], qkv_ref.at[0], ctx_ref.at[0], lse_ref.at[0])
        return
    out_w, qkv_ref, ctx_ref, lse_ref = groups[0]

    def step(i, _):
        k = first - 1 + i
        group(i, out_w[k], qkv_ref.at[k], ctx_ref.at[k], lse_ref.at[k])
        return 0

    lax.fori_loop(0, 2, step, 0)


def attn_back(first, info, tokens, residual_low, small, out_own, own, out_rest, rest):
    seq, width = tokens.shape
    local = out_own.shape[0]
    arrays = []
    for k in (first, first + 1):
        arrays += (out_own,) + tuple(own) if k == 0 else (out_rest,) + tuple(rest)
    half = halves_shape(2, 4 * local, width)
    return pl.pallas_call(
        partial(attn_back_kernel, first),
        in_specs=[smem()] + [vmem()] * 11,
        out_specs=[vmem()] * 4,
        out_shape=[
            shaped((16, width), wide),
            shaped((2, 3 * local, seq), low),
            shaped(half, low),
            shaped(half, low),
        ],
        scratch_shapes=[pltpu.VMEM((4 * local, width), low)],
        compiler_params=params(),
        cost_estimate=cost(9),
        name="attn_back",
    )(info, tokens, residual_low, small, *arrays)


def grad_tokens_kernel(grad, joint_a, joint_b, w_query, w_key, w_value, rest_w, out):
    local, rows = w_query.shape[0], joint_a.shape[1]
    total = grad[...]
    for i, weights in enumerate((w_query, w_key, w_value)):
        total = total + mm(joint_a[0, i * local : (i + 1) * local], weights[...], 0, 0)
    for k in range(1, 4):
        joint = joint_a[k] if k < 2 else joint_b[k - 2]
        total = total + mm(joint, rest_w[k - 1, :rows], 0, 0)
    out[...] = total.astype(low)


def grad_tokens_of(grad, joint_a, joint_b, weights, rest_w):
    return pl.pallas_call(
        grad_tokens_kernel,
        in_specs=[vmem()] * 7,
        out_specs=vmem(),
        out_shape=shaped(grad.shape, low),
        compiler_params=params(),
        cost_estimate=cost(4),
        name="grad_tokens",
    )(grad, joint_a, joint_b, *weights, rest_w)


def finish_ffn_kernel(info, held, held_mates, down, up, mark):
    rows = held.shape[2]
    mark[...] = jnp.zeros(mark.shape, wide)
    for s, pieces in enumerate((held, held_mates)):
        holder = info[1] ^ s
        for move in range(3):
            start = pl.multiple_of((holder * 4 + (info[2] ^ move)) * rows, rows)
            down[pl.ds(start, rows), :] = pieces[move, 0].astype(wide)
            up[pl.ds(start, rows), :] = pieces[move, 1].astype(wide)
        start = pl.multiple_of((holder * 4 + (info[2] ^ 3)) * rows, rows)
        down[pl.ds(start, rows), :] = jnp.zeros((rows, down.shape[1]), wide)
        up[pl.ds(start, rows), :] = jnp.zeros((rows, up.shape[1]), wide)


def finish_ffn(info, held, mates):
    _, _, rows, cols = held.shape
    return pl.pallas_call(
        finish_ffn_kernel,
        in_specs=[smem()] + [vmem()] * 2,
        out_specs=[vmem()] * 3,
        out_shape=[shaped((GROUP * rows, cols), wide)] * 2 + [shaped((8, 128), wide)],
        compiler_params=params(),
        cost_estimate=cost(3),
        name="finish_ffn",
    )(info, held, mates)


def finish_ffn_corner_kernel(info, corner, corner_mate, mark, down_in, up_in, down, up, ready, sems):
    rows = corner.shape[1]
    copies = []
    for s, pieces in enumerate((corner, corner_mate)):
        holder = info[1] ^ s
        start = pl.multiple_of((holder * 4 + (info[2] ^ 3)) * rows, rows)
        for i, target in enumerate((down, up)):
            ready[s, i] = pieces[i].astype(wide)
            copies.append(
                pltpu.make_async_copy(ready.at[s, i], target.at[pl.ds(start, rows), :], sems.at[s, i])
            )
            copies[-1].start()
    for copy in copies:
        copy.wait()


def finish_ffn_corner(info, corner, corner_mate, mark, down, up):
    _, rows, cols = corner.shape
    return pl.pallas_call(
        finish_ffn_corner_kernel,
        in_specs=[smem()] + [vmem()] * 2 + [hbm()] * 3,
        out_specs=[hbm()] * 2,
        out_shape=[shaped(down.shape, wide)] * 2,
        scratch_shapes=[pltpu.VMEM((2, 2, rows, cols), wide), pltpu.SemaphoreType.DMA((2, 2))],
        input_output_aliases={4: 0, 5: 1},
        compiler_params=params(),
        cost_estimate=cost(1),
        name="finish_ffn_corner",
    )(info, corner, corner_mate, mark, down, up)


def finish_attn_kernel(info, *refs):
    query, key, value, out, whole = refs[8:]
    for s in range(2):
        holder = info[1] ^ s
        for move in range(4):
            view = refs[4 * s + move]
            rows = view.shape[0]
            start = pl.multiple_of((holder * 4 + (info[2] ^ move)) * rows, rows)
            whole[pl.ds(start, rows), :] = view[...].astype(wide)
    local = whole.shape[0] // 4
    query[...] = whole[:local]
    key[...] = whole[local : 2 * local]
    value[...] = whole[2 * local : 3 * local]
    out[...] = whole[3 * local :]


def finish_attn(info, pieces):
    rows, cols = pieces[0].shape
    size = GROUP * rows
    local = size // 4
    return pl.pallas_call(
        finish_attn_kernel,
        in_specs=[smem()] + [vmem()] * 8,
        out_specs=[vmem()] * 4,
        out_shape=[shaped((local, cols), wide)] * 4,
        scratch_shapes=[pltpu.VMEM((size, cols), wide)],
        compiler_params=params(),
        cost_estimate=cost(2),
        name="finish_attn",
    )(info, *pieces)


class Links:
    def __init__(self, dp_size, parts):
        self.dp_size, self.parts = dp_size, parts

    def move(self, array, partner):
        pairs = []
        for d in range(self.dp_size):
            for t in range(self.parts):
                to_d, to_t = partner(d, t)
                pairs.append((d * self.parts + t, to_d * self.parts + to_t))
        return lax.ppermute(array, ("dp", "tensor"), pairs)

    def bit(self, array, bit):
        return self.move(array, lambda d, t: (d ^ bit, t))

    def core(self, array):
        return self.bit(array, 1)

    def plane(self, array, step):
        return self.move(array, lambda d, t: (d ^ (2 if (d & 1) == step else 4), t))

    def everywhere(self, array, bits):
        return [self.bit(array, bit) for bit in bits]

    def across(self, array, k):
        return self.move(array, lambda d, t: (d, t ^ k))

    def line(self, array, step):
        return self.move(array, lambda d, t: (d, t ^ (1 if (d & 1) == step else 2)))


def add(left, right):
    return (left.astype(wide) + right.astype(wide)).astype(low)


def after(*values):
    return lax.optimization_barrier(values)


def per_device(
    dp_size,
    parts,
    tokens,
    page_lengths,
    w_query,
    b_query,
    w_key,
    w_value,
    b_value,
    w_out,
    b_out,
    ln1_gain,
    ln1_bias,
    w_up,
    b_up,
    w_down,
    b_down,
    ln2_gain,
    ln2_bias,
    cotangent,
):
    links = Links(dp_size, parts)
    me = lax.axis_index("tensor")
    place = lax.axis_index("dp") % GROUP
    core, quarter = place & 1, place >> 1
    is_odd = core == 1
    width = tokens.shape[1]
    local = w_query.shape[1]
    rows = width // GROUP
    length = lax.dynamic_slice_in_dim(page_lengths, me, 1, 0)
    info = jnp.concatenate([length, jnp.stack([core, quarter, me]).astype(jnp.int32)])
    attn_w = (w_query.T, w_key.T, w_value.T, w_out)
    piece = core * 4 + quarter

    def cut(array, index):
        return lax.dynamic_slice_in_dim(array, index * rows, rows, 0)

    def mates(held):
        return held + [links.core(array) for array in held]

    a0 = lax.select_n(piece >> 1, *(cut(array, piece & 1) for array in attn_w))
    bias_own = jnp.concatenate([b_query, b_value, b_up])
    bias_rows = jnp.pad(bias_own, (0, 8 * width - bias_own.size)).reshape(8, width)
    a0, piece_d = after(a0, piece)
    d0 = cut(w_down, piece_d)
    u0 = jnp.concatenate([cut(w_up, piece), bias_rows], axis=0)
    vec = jnp.stack([b_out, ln1_gain, ln1_bias, b_down, ln2_gain, ln2_bias, b_down, b_down])
    vec = vec.astype(wide)
    a1, ax = links.line(a0, 0), links.line(a0, 1)
    d1 = links.line(d0, 0)
    a1, u0, vec, tokens_in = after(a1, u0, vec, tokens)
    ay = links.line(a1, 1)
    u1, ux = links.line(u0, 0), links.line(u0, 1)
    own = list(attn_own(info, tokens_in, attn_w[:3], bias_own.astype(wide)[None, None]))
    ax, ay, u1, d1, own[2] = after(ax, ay, u1, d1, own[2])
    a3 = jnp.stack([a1, ax, ay])
    a4, a5 = links.plane(a3, 0), links.plane(a3, 1)
    uy = links.line(u1, 1)
    dx = links.line(d0, 1)
    a4, ux, uy, d1 = after(a4, ux, uy, d1)
    u3 = jnp.stack([u1, ux, uy])
    bias_rest = u3[:, rows:].reshape(parts - 1, 8 * width)[:, : bias_own.size]
    near, far = bias_rest[0], bias_rest[1]
    bias = jnp.stack(
        [bias_own, jnp.where(is_odd, far, near), jnp.where(is_odd, near, far), bias_rest[2]]
    )
    bias = bias.astype(wide)[:, None]
    u3 = u3[:, :rows]
    a6 = links.plane(a4, 1)
    u4, u5 = links.plane(u3, 0), links.plane(u3, 1)
    dy = links.line(d1, 1)
    a5, a6, u4, dx, dy, bias = after(a5, a6, u4, dx, dy, bias)
    d3 = jnp.stack([d1, dx, dy])
    pieces_a = mates([a3, a4, a5, a6])
    u6 = links.plane(u4, 1)
    d4, d5 = links.plane(d3, 0), links.plane(d3, 1)
    qkv, attn_rest_w, ctx, lse, out_rest = attn_rest(info, tokens, bias, pieces_a)
    skip, normed_low, hat, inv = ffn_in(tokens, own[1], ctx, vec, w_out, out_rest)
    u5, u6, d4, lse, inv = after(u5, u6, d4, lse, inv)
    pieces_u = mates([u3, u4, u5, u6])
    d6 = links.plane(d4, 1)
    act, slope, up, mark = ffn_up(info, normed_low, bias, w_up, pieces_u, inv)
    d5, d6, mark = after(d5, d6, mark)
    pieces_d = mates([d3, d4, d5, d6])
    output, grad_branch, branch_low, small, down = ffn_down(
        info, act, skip, vec, cotangent, w_down, pieces_d, mark
    )
    rest = (qkv, ctx, lse)

    def plane_a(keep, got):
        return links.plane(add(keep[1], got[1]), 0), add(keep[0], got[0])

    def plane_b(kept, got):
        return links.plane(add(kept[1], got[1]), 1), add(kept[0], got[0])

    def line_a(both):
        both = both.reshape(-1, 2, parts // 2, rows, width)
        sent = jnp.where(is_odd, both[:, :, 1], both[:, 1])
        return links.line(sent, 1), jnp.where(is_odd, both[:, :, 0], both[:, 0])

    def line_b(kept, got):
        both = add(kept, got)
        return links.line(both[:, 1], 0), both[:, 0]

    def settle(kept, got):
        total = kept.astype(wide) + got.astype(wide)
        bit = GROUP
        while bit < dp_size:
            total = total + links.bit(total, bit)
            bit *= 2
        return total.astype(low)

    keep_c, send_c, mark = down_grad(0, info, act, branch_low, mark)
    got_c = links.core(send_c)
    keep_d, send_d, mark = down_grad(2, info, act, branch_low, mark)
    got_c, send_d, mark = after(got_c, send_d, mark)
    near_c, kept_c = plane_a(keep_c, got_c)
    got_d = links.core(send_d)
    got_d, small = after(got_d, small)
    near_d, kept_d = plane_a(keep_d, got_d)
    grad_residual, residual_low, small, keep_u, send_u = ffn_back(
        info, branch_low, grad_branch, slope, normed_low, hat, inv, vec, small, up, down
    )
    near_c, near_d, send_u, small = after(near_c, near_d, send_u, small)
    got_u = links.core(send_u)
    far_d = links.plane(jnp.concatenate([add(kept_c[1], near_c[1]), add(kept_d[1], near_d[1])]), 1)
    kept_d = jnp.concatenate([add(kept_c[0], near_c[0]), add(kept_d[0], near_d[0])])
    small, joint_a, keep_a, send_a = attn_back(
        0, info, tokens, residual_low, small, w_out, own, out_rest, rest
    )
    got_u, far_d, send_a, small = after(got_u, far_d, send_a, small)
    near_u, kept_u = plane_a(keep_u, got_u)
    got_a = links.core(send_a)
    line_d, kept_d = line_a(add(kept_d, far_d))
    small, joint_b, keep_b, send_b = attn_back(
        2, info, tokens, residual_low, small, w_out, own, out_rest, rest
    )
    near_u, got_a, line_d, send_b, small, grad_residual = after(
        near_u, got_a, line_d, send_b, small, grad_residual
    )
    got_b = links.core(send_b)
    far_u, kept_u = plane_b(kept_u, near_u)
    last_d, kept_d = line_b(kept_d, line_d)
    grad_tokens = grad_tokens_of(grad_residual, joint_a, joint_b, attn_w[:3], attn_rest_w)
    small_got = links.core(small)
    got_a, got_b, far_u, last_d, grad_tokens, small_got = after(
        got_a, got_b, far_u, last_d, grad_tokens, small_got
    )
    small = small + small_got

    def joined(share, small):
        return jnp.concatenate([share.reshape(-1, width), small.astype(low)], axis=0)

    near_a, kept_a = plane_a(keep_a, got_a)
    near_b = links.plane(joined(add(keep_b[1], got_b[1]), small), 0)
    kept_b = add(keep_b[0], got_b[0])
    line_u, kept_u = line_a(add(kept_u, far_u))
    near_a, near_b, line_u = after(near_a, near_b, line_u)
    size = 4 * rows
    far_a, kept_a = plane_b(kept_a, near_a)
    small = small + near_b[size:].astype(wide)
    near_b = near_b[:size].reshape(kept_b.shape)
    size = 2 * rows
    far_b = links.plane(joined(add(kept_b[1], near_b[1]), small), 1)
    kept_b = add(kept_b[0], near_b[0])
    last_u, kept_u = line_b(kept_u, line_u)
    far_a, far_b = after(far_a, far_b)
    small = small + far_b[size:].astype(wide)
    share = jnp.concatenate([add(kept_a, far_a), add(kept_b, far_b[:size].reshape(kept_b.shape))])
    across = [links.across(joined(share[k], small), k) for k in range(parts - 1, 0, -1)]
    sum_f = jnp.stack([settle(kept_d, last_d)[0], settle(kept_u, last_u)[0]])
    f_x, f_y = links.everywhere(sum_f, (2, 4))
    across, f_x, f_y = after(across, f_x, f_y)
    sum_a = share[0].astype(wide)
    for array in across:
        sum_a = sum_a + array[:rows].astype(wide)
        small = small + array[rows:].astype(wide)
    bit = GROUP
    while bit < dp_size:
        sum_a = sum_a + links.bit(sum_a, bit)
        small = small + links.bit(small, bit)
        bit *= 2
    sum_a = sum_a.astype(low)
    around = links.everywhere(sum_a, (2, 4, 6))
    f_xy = links.plane(jnp.where(is_odd, f_x, f_y), 0)
    held = jnp.stack([sum_f, f_x, f_y])
    *early, mark = finish_ffn(info, held, links.core(held))
    pair = lax.dynamic_index_in_dim(small, 10 + me, 0, keepdims=False)
    grad_b_up = lax.dynamic_index_in_dim(small, 6 + me, 0, keepdims=False)
    around, small, pair, grad_b_up, mark = after(around, small, pair, grad_b_up, mark)
    grad_w_down, grad_w_up = finish_ffn_corner(info, f_xy, links.core(f_xy), mark, *early)
    grad_w_query, grad_w_key, grad_w_value, grad_w_out = finish_attn(info, mates([sum_a] + around))
    grad_w_query, grad_w_key, grad_w_value = grad_w_query.T, grad_w_key.T, grad_w_value.T
    return (
        output,
        grad_tokens,
        grad_w_query,
        pair[:local],
        grad_w_key,
        grad_w_value,
        pair[256 : 256 + local],
        grad_w_out,
        small[0],
        small[1],
        small[2],
        grad_w_up,
        grad_b_up,
        grad_w_down,
        small[3],
        small[4],
        small[5],
    )


def solution(mesh):
    columns, rows, both = P(None, "tensor"), P("tensor", None), P(("dp", "tensor"), None)
    share = P("tensor")
    return jax.shard_map(
        partial(per_device, mesh.shape["dp"], mesh.shape["tensor"]),
        mesh=mesh,
        in_specs=(
            both,
            P("dp"),
            columns,
            share,
            columns,
            columns,
            share,
            rows,
            P(),
            P(),
            P(),
            columns,
            share,
            rows,
            P(),
            P(),
            P(),
            both,
        ),
        out_specs=(
            both,
            both,
            columns,
            share,
            columns,
            columns,
            share,
            rows,
            P(),
            P(),
            P(),
            columns,
            share,
            rows,
            P(),
            P(),
            P(),
        ),
        check_vma=False,
    )
```

```python
from functools import partial

import jax
import jax.numpy as jnp
from jax import lax
from jax.experimental import pallas as pl
from jax.experimental.pallas import tpu as pltpu
from jax.sharding import PartitionSpec as P

HD = 64
SEQ = 512
GROUP = 8
LOG2E = 1.4426950408889634
TAIL_P = 0.39
TAIL = (
    0.23532521908406087,
    0.09138841455460205,
    0.6495593986198918,
    -0.6354002786931026,
    0.8866643698688825,
    -0.22753712513305413,
)

epsilon = 1e-12
masked_score = -1000000000.0
low = jnp.bfloat16
wide = jnp.float32
PEAK = 1.1e15
LIMIT = 16


def mm(left, right, left_dim, right_dim):
    return lax.dot_general(
        left, right, (((left_dim,), (right_dim,)), ((), ())), preferred_element_type=wide
    )


def vmem():
    return pl.BlockSpec(memory_space=pltpu.VMEM)


def smem():
    return pl.BlockSpec(memory_space=pltpu.SMEM)


def hbm():
    return pl.BlockSpec(memory_space=pl.ANY)


def cost(microseconds):
    return pl.CostEstimate(
        flops=int(microseconds * 1e-6 * PEAK), bytes_accessed=1 << 20, transcendentals=0
    )


def params(mebibytes=LIMIT):
    return pltpu.CompilerParams(vmem_limit_bytes=mebibytes << 20)


def shaped(shape, dtype):
    return jax.ShapeDtypeStruct(shape, dtype)


def masked_pad(length, seq):
    row = lax.broadcasted_iota(jnp.int32, (16, seq), 0)
    key = lax.broadcasted_iota(jnp.int32, (16, seq), 1)
    bias = jnp.where((row == 0) & (key >= length), masked_score, 0.0).astype(low)
    ones = jnp.where(row == 0, 1.0, 0.0).astype(low)
    return bias, ones


def as_column(row, ones):
    first = lax.broadcasted_iota(jnp.int32, (16, row.shape[1]), 0) == 0
    return mm(jnp.where(first, row, 0.0).astype(low), ones, 0, 0)


def group_forward(tokens, weights, bias, length, qkv_ref, ctx_ref, lse_ref):
    local = weights[0].shape[0]
    seq = tokens.shape[0]
    scale = HD**-0.5 * LOG2E
    key_pad, ones = masked_pad(length, seq)
    query = (mm(weights[0], tokens, 1, 1) + as_column(bias[:, :local], ones)).astype(low)
    key = mm(weights[1], tokens, 1, 1).astype(low)
    value = mm(weights[2], tokens, 1, 1) + as_column(bias[:, local : 2 * local], ones)
    value = value.astype(low)
    qkv_ref[:local] = query
    qkv_ref[local : 2 * local] = key
    qkv_ref[2 * local :] = value
    for h in range(local // HD):
        part = slice(h * HD, (h + 1) * HD)
        scores = mm(
            jnp.concatenate([key[part], key_pad], 0), jnp.concatenate([query[part], ones], 0), 0, 0
        )
        top = jnp.max(scores, axis=0, keepdims=True)
        probs = jnp.exp2((scores - top) * scale)
        total = jnp.sum(probs, axis=0, keepdims=True)
        context = mm(value[part], probs.astype(low), 1, 0)
        ctx_ref[part] = (context * (1.0 / total)).astype(low)
        lse_ref[h : h + 1] = top * scale + jnp.log2(total)


def gelu_parts(x):
    t = 1.0 / (1.0 + (TAIL_P * 0.5**0.5) * jnp.abs(x))
    poly = TAIL[-1]
    for factor in TAIL[-2::-1]:
        poly = poly * t + factor
    bell = jnp.exp2(x * x * (-0.5 * LOG2E))
    half = 0.5 * poly * t * bell
    cdf = jnp.where(x >= 0, 1.0 - half, half)
    return x * cdf, cdf + x * bell * (0.5 / jnp.pi) ** 0.5


def norm_parts(values):
    centred = values - jnp.mean(values, axis=1, keepdims=True)
    inverse = lax.rsqrt(jnp.mean(centred * centred, axis=1, keepdims=True) + epsilon)
    return centred * inverse, inverse


def norm_back(scaled, normal, inverse):
    return inverse * (
        scaled
        - jnp.mean(scaled, axis=1, keepdims=True)
        - normal * jnp.mean(scaled * normal, axis=1, keepdims=True)
    )


def assemble(info, refs, target, own=None):
    if own is not None:
        target[0] = own[...]
    skip = 1 if own is None else 0
    for s in range(2):
        views = refs[4 * s : 4 * s + 4]
        holder = info[1] ^ s
        order = (1 + holder, 2 - holder, 3)
        for view, move in zip(views, (0,) + order):
            rows = view.shape[1]
            start = pl.multiple_of((holder * 4 + (info[2] ^ move)) * rows, rows)
            for entry, k in enumerate(order):
                target[k - skip, pl.ds(start, rows), :] = view[entry]


def place_pieces(info, scratch, keep_ref, send_ref, entry):
    rows = scratch.shape[0] // GROUP
    for s, target in enumerate((keep_ref, send_ref)):
        half = info[1] ^ s
        for q in range(4):
            move = info[2] ^ q
            x_bit, y_bit = move & 1, move >> 1
            a = jnp.where(half == 0, x_bit, y_bit)
            start = pl.multiple_of((half * 4 + q) * rows, rows)
            target[a, x_bit + y_bit - a, entry] = scratch[pl.ds(start, rows), :]


def attn_own_kernel(info, tokens, w_query, w_key, w_value, bias, qkv, ctx, lse):
    weights = (w_query[...], w_key[...], w_value[...])
    group_forward(tokens[...], weights, bias[0], info[0], qkv.at[0], ctx.at[0], lse.at[0])


def attn_own(info, tokens, weights, bias):
    local, seq = weights[0].shape[0], tokens.shape[0]
    return pl.pallas_call(
        attn_own_kernel,
        in_specs=[smem()] + [vmem()] * 5,
        out_specs=[vmem()] * 3,
        out_shape=[
            shaped((1, 3 * local, seq), low),
            shaped((1, local, seq), low),
            shaped((1, 8, seq), wide),
        ],
        compiler_params=params(),
        cost_estimate=cost(4),
        name="attn_own",
    )(info, tokens, *weights, bias)


def attn_rest_kernel(info, tokens, bias, *refs):
    qkv_out, whole, ctx, lse, out_w, weights, qkv, sems = refs[8:]
    others, local = ctx.shape[:2]
    assemble(info, refs[:8], weights)
    sent = [pltpu.make_async_copy(weights, whole, sems.at[others])]
    sent[0].start()
    out_w[...] = weights[:, 3 * local :]

    def group(k, _):
        joint = tuple(weights[k, i * local : (i + 1) * local] for i in range(3))
        group_forward(
            tokens[...], joint, bias[k + 1], info[0], qkv.at[k], ctx.at[k], lse.at[k]
        )
        pltpu.make_async_copy(qkv.at[k], qkv_out.at[k], sems.at[k]).start()
        return 0

    lax.fori_loop(0, others, group, 0)
    sent += [pltpu.make_async_copy(qkv.at[k], qkv_out.at[k], sems.at[k]) for k in range(others)]
    for copy in sent:
        copy.wait()


def attn_rest(info, tokens, bias, pieces):
    others, rows, cols = pieces[0].shape
    size, seq = rows * GROUP, tokens.shape[0]
    local = size // 4
    joint, whole = (others, 3 * local, seq), (others, size, cols)
    return pl.pallas_call(
        attn_rest_kernel,
        in_specs=[smem()] + [vmem()] * 10,
        out_specs=[pl.BlockSpec(memory_space=pltpu.HBM)] * 2 + [vmem()] * 3,
        out_shape=[
            shaped(joint, low),
            shaped(whole, low),
            shaped((others, local, seq), low),
            shaped((others, 8, seq), wide),
            shaped((others, local, cols), low),
        ],
        scratch_shapes=[
            pltpu.VMEM(whole, low),
            pltpu.VMEM(joint, low),
            pltpu.SemaphoreType.DMA((others + 1,)),
        ],
        compiler_params=params(),
        cost_estimate=cost(8),
        name="attn_rest",
    )(info, tokens, bias, *pieces)


def ffn_in_kernel(tokens, ctx_own, ctx_rest, vec, out_own, out_rest, skip, normed_ref, hat_ref, inv_ref):
    others = ctx_rest.shape[0]
    rows = vec[...]
    b_out, gain_one, bias_one, b_down = (rows[i : i + 1] for i in range(4))
    attended = mm(ctx_own[0], out_own[...], 0, 0)
    for k in range(others):
        attended = attended + mm(ctx_rest[k], out_rest[k], 0, 0)
    hat, inv = norm_parts(tokens[...].astype(wide) + attended + b_out)
    hat_ref[...] = hat
    inv_ref[...] = jnp.broadcast_to(inv, inv_ref.shape)
    normed = hat * gain_one + bias_one
    normed_ref[...] = normed.astype(low)
    skip[...] = normed + b_down


def ffn_in(tokens, ctx_own, ctx_rest, vec, out_own, out_rest):
    seq, width = tokens.shape
    others, local = ctx_rest.shape[:2]
    return pl.pallas_call(
        ffn_in_kernel,
        in_specs=[vmem()] * 6,
        out_specs=[vmem()] * 4,
        out_shape=[
            shaped((seq, width), wide),
            shaped((seq, width), low),
            shaped((seq, width), wide),
            shaped((seq, 128), wide),
        ],
        compiler_params=params(),
        cost_estimate=cost(5),
        name="ffn_in",
    )(tokens, ctx_own, ctx_rest, vec, out_own, out_rest)


def ffn_up_kernel(info, normed, bias, up_own, *refs):
    _, act, slope, up, mark = refs[8:]
    size = up.shape[2]
    first = bias.shape[2] - size
    mark[...] = jnp.zeros(mark.shape, wide)
    assemble(info, refs[:8], up, up_own)

    def forward(k, _):
        preact = mm(normed[...], up[k], 1, 0) + bias[k][:, first:].astype(wide)
        value, derivative = gelu_parts(preact)
        act[k] = value.astype(low)
        slope[k] = derivative.astype(low)
        return 0

    lax.fori_loop(0, act.shape[0], forward, 0)


def ffn_up(info, normed, bias, up_own, pieces, mark):
    seq, width = normed.shape
    others, size = pieces[0].shape[0], up_own.shape[1]
    return pl.pallas_call(
        ffn_up_kernel,
        in_specs=[smem()] + [vmem()] * (3 + 8) + [hbm()],
        out_specs=[vmem()] * 4,
        out_shape=[
            shaped((others + 1, seq, size), low),
            shaped((others + 1, seq, size), low),
            shaped((others + 1, width, size), low),
            shaped((8, 128), wide),
        ],
        compiler_params=params(),
        cost_estimate=cost(11),
        name="ffn_up",
    )(info, normed, bias, up_own, *pieces, mark)


def ffn_down_kernel(info, skip, vec, cot, act, down_own, *refs):
    _, out, grad_ref, branch_ref, small, down = refs[8:]
    parts = act.shape[0]
    assemble(info, refs[:8], down, down_own)
    grad_ref[...] = skip[...]
    total = grad_ref[...]
    for k in range(parts):
        total = total + mm(act[k], down[k], 1, 0)
    gain_two, bias_two = vec[4:5], vec[5:6]
    hat_two, inv_two = norm_parts(total)
    out[...] = (hat_two * gain_two + bias_two).astype(low)
    grad = cot[...].astype(wide)
    grad_branch = norm_back(grad * gain_two, hat_two, inv_two)
    grad_ref[...] = grad_branch
    branch_low = grad_branch.astype(low)
    branch_ref[...] = branch_low
    small[...] = jnp.zeros(small.shape, wide)
    small[3:4] = jnp.sum(grad_branch, axis=0, keepdims=True)
    small[4:5] = jnp.sum(grad * hat_two, axis=0, keepdims=True)
    small[5:6] = jnp.sum(grad, axis=0, keepdims=True)


def down_grad_kernel(first, info, act, branch_low, keep, send, mark, scratch):
    mark[...] = jnp.zeros(mark.shape, wide)

    def weight(i, _):
        scratch[...] = mm(act[first + i], branch_low[...], 0, 0).astype(low)
        place_pieces(info, scratch, keep, send, i)
        return 0

    lax.fori_loop(0, 2, weight, 0)


def down_grad(first, info, act, branch_low, mark):
    size, width = act.shape[2], branch_low.shape[1]
    half = halves_shape(2, size, width)
    return pl.pallas_call(
        partial(down_grad_ordered, first),
        in_specs=[smem()] + [vmem()] * 2 + [hbm()],
        out_specs=[vmem()] * 3,
        out_shape=[shaped(half, low), shaped(half, low), shaped((8, 128), wide)],
        scratch_shapes=[pltpu.VMEM((size, width), low)],
        compiler_params=params(),
        cost_estimate=cost(2),
        name="down_grad",
    )(info, act, branch_low, mark)


def down_grad_ordered(first, info, act, branch_low, _, *refs):
    down_grad_kernel(first, info, act, branch_low, *refs)


def halves_shape(entries, rows, cols):
    return (2, 2, entries, rows // GROUP, cols)


def ffn_down(info, act, skip, vec, cot, down_own, pieces, mark):
    parts, seq, size = act.shape
    width = skip.shape[1]
    return pl.pallas_call(
        ffn_down_kernel,
        in_specs=[smem()] + [vmem()] * (5 + 8) + [hbm()],
        out_specs=[vmem()] * 5,
        out_shape=[
            shaped((seq, width), low),
            shaped((seq, width), wide),
            shaped((seq, width), low),
            shaped((16, width), wide),
            shaped((parts, size, width), low),
        ],
        compiler_params=params(),
        cost_estimate=cost(12),
        name="ffn_down",
    )(info, skip, vec, cot, act, down_own, *pieces, mark)


def ffn_back_kernel(
    info, branch_low, grad_branch, normed_low, hat_ref, inv_ref, vec, small_in, slope, up, down,
    grad_ref, residual_ref, small, keep, send, turned, total, scratch,
):
    parts = slope.shape[0]
    index = lax.broadcasted_iota(jnp.int32, small.shape, 0)
    small[...] = small_in[...]
    total[...] = grad_branch[...]
    turned[...] = normed_low[...].T

    def backward(k, _):
        grad_pre = mm(branch_low[...], down[k], 1, 1) * slope[k].astype(wide)
        grad_pre = grad_pre.astype(low)
        sums = jnp.sum(grad_pre.astype(wide), axis=0, keepdims=True)
        small[...] = jnp.where(index == 6 + (info[3] ^ k), sums, small[...])
        scratch[...] = mm(turned[...], grad_pre, 1, 0).astype(low)
        place_pieces(info, scratch, keep, send, k)
        total[...] += mm(grad_pre, up[k], 1, 1)
        return 0

    lax.fori_loop(0, parts, backward, 0)
    grad_normed = total[...]
    hat = hat_ref[...]
    grad_residual = norm_back(grad_normed * vec[1:2], hat, inv_ref[:, :1])
    grad_ref[...] = grad_residual
    residual_ref[...] = grad_residual.astype(low)
    small[0:1] = jnp.sum(grad_residual, axis=0, keepdims=True)
    small[1:2] = jnp.sum(grad_normed * hat, axis=0, keepdims=True)
    small[2:3] = jnp.sum(grad_normed, axis=0, keepdims=True)


def ffn_back(info, branch_low, grad_branch, slope, normed_low, hat, inv, vec, small, up, down):
    _, width, size = up.shape
    parts, seq = slope.shape[:2]
    half = halves_shape(parts, width, size)
    return pl.pallas_call(
        ffn_back_kernel,
        in_specs=[smem()] + [vmem()] * 10,
        out_specs=[vmem()] * 5,
        out_shape=[
            shaped((seq, width), wide),
            shaped((seq, width), low),
            shaped((16, width), wide),
            shaped(half, low),
            shaped(half, low),
        ],
        scratch_shapes=[
            pltpu.VMEM((width, seq), low),
            pltpu.VMEM((seq, width), wide),
            pltpu.VMEM((width, size), low),
        ],
        compiler_params=params(),
        cost_estimate=cost(11),
        name="ffn_back",
    )(info, branch_low, grad_branch, normed_low, hat, inv, vec, small, slope, up, down)


def attn_back_kernel(first, info, tokens, residual_low, small_in, *refs):
    groups = (refs[:4], refs[4:8])
    small, joint, keep, send, scratch = refs[8:]
    local = groups[0][2].shape[1]
    seq, width = tokens.shape
    scale = HD**-0.5
    index = lax.broadcasted_iota(jnp.int32, small.shape, 0)
    small[...] = small_in[...]
    key_pad, query_pad = masked_pad(info[0], seq)
    ones = jnp.ones((8, seq), low)

    def group(i, out_rows, qkv, ctx, lse):
        grad_ctx = mm(out_rows, residual_low[...], 1, 1).astype(low)
        for h in range(local // HD):
            lo, hi = h * HD, (h + 1) * HD
            query = qkv[lo:hi]
            key = qkv[local + lo : local + hi]
            value = qkv[2 * local + lo : 2 * local + hi]
            grad_head = grad_ctx[lo:hi]
            scores = mm(
                jnp.concatenate([key, key_pad], 0), jnp.concatenate([query, query_pad], 0), 0, 0
            )
            probs = jnp.exp2(scores * (scale * LOG2E) - lse[h : h + 1])
            grad_probs = mm(value, grad_head, 0, 0)
            product = probs * grad_probs
            grad_scores = (product - probs * jnp.sum(product, axis=0, keepdims=True)).astype(low)
            joint[i, lo:hi] = (mm(key, grad_scores, 1, 0) * scale).astype(low)
            joint[i, local + lo : local + hi] = (mm(query, grad_scores, 1, 1) * scale).astype(low)
            joint[i, 2 * local + lo : 2 * local + hi] = mm(
                grad_head, probs.astype(low), 1, 1
            ).astype(low)
        grads = joint[i]
        sums = mm(ones, grads, 1, 1)[:1]
        gap = jnp.zeros((1, 256 - local), wide)
        rest = jnp.zeros((1, width - 512), wide)
        sums = jnp.concatenate([sums[:, :local], gap, sums[:, 2 * local :], gap, rest], 1)
        small[...] = jnp.where(index == 10 + (info[3] ^ (first + i)), sums, small[...])
        scratch[: 3 * local] = mm(grads, tokens[...], 1, 0).astype(low)
        scratch[3 * local :] = mm(ctx[...], residual_low[...], 1, 0).astype(low)
        place_pieces(info, scratch, keep, send, i)

    if first == 0:
        for i, (out_w, qkv_ref, ctx_ref, lse_ref) in enumerate(groups):
            group(i, out_w[...] if i == 0 else out_w[0], qkv_ref.at[0], ctx_ref.at[0], lse_ref.at[0])
        return
    out_w, qkv_ref, ctx_ref, lse_ref = groups[0]

    def step(i, _):
        k = first - 1 + i
        group(i, out_w[k], qkv_ref.at[k], ctx_ref.at[k], lse_ref.at[k])
        return 0

    lax.fori_loop(0, 2, step, 0)


def attn_back(first, info, tokens, residual_low, small, out_own, own, out_rest, rest):
    seq, width = tokens.shape
    local = out_own.shape[0]
    arrays = []
    for k in (first, first + 1):
        arrays += (out_own,) + tuple(own) if k == 0 else (out_rest,) + tuple(rest)
    half = halves_shape(2, 4 * local, width)
    return pl.pallas_call(
        partial(attn_back_kernel, first),
        in_specs=[smem()] + [vmem()] * 11,
        out_specs=[vmem()] * 4,
        out_shape=[
            shaped((16, width), wide),
            shaped((2, 3 * local, seq), low),
            shaped(half, low),
            shaped(half, low),
        ],
        scratch_shapes=[pltpu.VMEM((4 * local, width), low)],
        compiler_params=params(),
        cost_estimate=cost(9),
        name="attn_back",
    )(info, tokens, residual_low, small, *arrays)


def grad_tokens_kernel(grad, joint_a, joint_b, w_query, w_key, w_value, rest_w, out):
    local, rows = w_query.shape[0], joint_a.shape[1]
    total = grad[...]
    for i, weights in enumerate((w_query, w_key, w_value)):
        total = total + mm(joint_a[0, i * local : (i + 1) * local], weights[...], 0, 0)
    for k in range(1, 4):
        joint = joint_a[k] if k < 2 else joint_b[k - 2]
        total = total + mm(joint, rest_w[k - 1, :rows], 0, 0)
    out[...] = total.astype(low)


def grad_tokens_of(grad, joint_a, joint_b, weights, rest_w):
    return pl.pallas_call(
        grad_tokens_kernel,
        in_specs=[vmem()] * 7,
        out_specs=vmem(),
        out_shape=shaped(grad.shape, low),
        compiler_params=params(),
        cost_estimate=cost(4),
        name="grad_tokens",
    )(grad, joint_a, joint_b, *weights, rest_w)


def finish_ffn_kernel(info, held, held_mates, down, up, mark):
    rows = held.shape[2]
    mark[...] = jnp.zeros(mark.shape, wide)
    for s, pieces in enumerate((held, held_mates)):
        holder = info[1] ^ s
        for move in range(3):
            start = pl.multiple_of((holder * 4 + (info[2] ^ move)) * rows, rows)
            down[pl.ds(start, rows), :] = pieces[move, 0].astype(wide)
            up[pl.ds(start, rows), :] = pieces[move, 1].astype(wide)
        start = pl.multiple_of((holder * 4 + (info[2] ^ 3)) * rows, rows)
        down[pl.ds(start, rows), :] = jnp.zeros((rows, down.shape[1]), wide)
        up[pl.ds(start, rows), :] = jnp.zeros((rows, up.shape[1]), wide)


def finish_ffn(info, held, mates):
    _, _, rows, cols = held.shape
    return pl.pallas_call(
        finish_ffn_kernel,
        in_specs=[smem()] + [vmem()] * 2,
        out_specs=[vmem()] * 3,
        out_shape=[shaped((GROUP * rows, cols), wide)] * 2 + [shaped((8, 128), wide)],
        compiler_params=params(),
        cost_estimate=cost(3),
        name="finish_ffn",
    )(info, held, mates)


def finish_ffn_corner_kernel(info, corner, corner_mate, mark, down_in, up_in, down, up, ready, sems):
    rows = corner.shape[1]
    copies = []
    for s, pieces in enumerate((corner, corner_mate)):
        holder = info[1] ^ s
        start = pl.multiple_of((holder * 4 + (info[2] ^ 3)) * rows, rows)
        for i, target in enumerate((down, up)):
            ready[s, i] = pieces[i].astype(wide)
            copies.append(
                pltpu.make_async_copy(ready.at[s, i], target.at[pl.ds(start, rows), :], sems.at[s, i])
            )
            copies[-1].start()
    for copy in copies:
        copy.wait()


def finish_ffn_corner(info, corner, corner_mate, mark, down, up):
    _, rows, cols = corner.shape
    return pl.pallas_call(
        finish_ffn_corner_kernel,
        in_specs=[smem()] + [vmem()] * 2 + [hbm()] * 3,
        out_specs=[hbm()] * 2,
        out_shape=[shaped(down.shape, wide)] * 2,
        scratch_shapes=[pltpu.VMEM((2, 2, rows, cols), wide), pltpu.SemaphoreType.DMA((2, 2))],
        input_output_aliases={4: 0, 5: 1},
        compiler_params=params(),
        cost_estimate=cost(1),
        name="finish_ffn_corner",
    )(info, corner, corner_mate, mark, down, up)


def finish_attn_kernel(info, *refs):
    query, key, value, out, whole = refs[8:]
    for s in range(2):
        holder = info[1] ^ s
        for move in range(4):
            view = refs[4 * s + move]
            rows = view.shape[0]
            start = pl.multiple_of((holder * 4 + (info[2] ^ move)) * rows, rows)
            whole[pl.ds(start, rows), :] = view[...].astype(wide)
    local = whole.shape[0] // 4
    query[...] = whole[:local]
    key[...] = whole[local : 2 * local]
    value[...] = whole[2 * local : 3 * local]
    out[...] = whole[3 * local :]


def finish_attn(info, pieces):
    rows, cols = pieces[0].shape
    size = GROUP * rows
    local = size // 4
    return pl.pallas_call(
        finish_attn_kernel,
        in_specs=[smem()] + [vmem()] * 8,
        out_specs=[vmem()] * 4,
        out_shape=[shaped((local, cols), wide)] * 4,
        scratch_shapes=[pltpu.VMEM((size, cols), wide)],
        compiler_params=params(),
        cost_estimate=cost(2),
        name="finish_attn",
    )(info, *pieces)


class Links:
    def __init__(self, dp_size, parts):
        self.dp_size, self.parts = dp_size, parts

    def move(self, array, partner):
        pairs = []
        for d in range(self.dp_size):
            for t in range(self.parts):
                to_d, to_t = partner(d, t)
                pairs.append((d * self.parts + t, to_d * self.parts + to_t))
        return lax.ppermute(array, ("dp", "tensor"), pairs)

    def bit(self, array, bit):
        return self.move(array, lambda d, t: (d ^ bit, t))

    def core(self, array):
        return self.bit(array, 1)

    def plane(self, array, step):
        return self.move(array, lambda d, t: (d ^ (2 if (d & 1) == step else 4), t))

    def everywhere(self, array, bits):
        return [self.bit(array, bit) for bit in bits]

    def across(self, array, k):
        return self.move(array, lambda d, t: (d, t ^ k))

    def line(self, array, step):
        return self.move(array, lambda d, t: (d, t ^ (1 if (d & 1) == step else 2)))


def add(left, right):
    return (left.astype(wide) + right.astype(wide)).astype(low)


def after(*values):
    return lax.optimization_barrier(values)


def per_device(
    dp_size,
    parts,
    tokens,
    page_lengths,
    w_query,
    b_query,
    w_key,
    w_value,
    b_value,
    w_out,
    b_out,
    ln1_gain,
    ln1_bias,
    w_up,
    b_up,
    w_down,
    b_down,
    ln2_gain,
    ln2_bias,
    cotangent,
):
    links = Links(dp_size, parts)
    me = lax.axis_index("tensor")
    place = lax.axis_index("dp") % GROUP
    core, quarter = place & 1, place >> 1
    is_odd = core == 1
    width = tokens.shape[1]
    local = w_query.shape[1]
    rows = width // GROUP
    length = lax.dynamic_slice_in_dim(page_lengths, me, 1, 0)
    info = jnp.concatenate([length, jnp.stack([core, quarter, me]).astype(jnp.int32)])
    attn_w = (w_query.T, w_key.T, w_value.T, w_out)
    piece = core * 4 + quarter

    def cut(array, index):
        return lax.dynamic_slice_in_dim(array, index * rows, rows, 0)

    def mates(held):
        return held + [links.core(array) for array in held]

    a0 = lax.select_n(piece >> 1, *(cut(array, piece & 1) for array in attn_w))
    bias_own = jnp.concatenate([b_query, b_value, b_up])
    bias_rows = jnp.pad(bias_own, (0, 8 * width - bias_own.size)).reshape(8, width)
    a0, piece_d = after(a0, piece)
    d0 = cut(w_down, piece_d)
    u0 = jnp.concatenate([cut(w_up, piece), bias_rows], axis=0)
    vec = jnp.stack([b_out, ln1_gain, ln1_bias, b_down, ln2_gain, ln2_bias, b_down, b_down])
    vec = vec.astype(wide)
    a1, ax = links.line(a0, 0), links.line(a0, 1)
    d1 = links.line(d0, 0)
    a1, u0, vec, tokens_in = after(a1, u0, vec, tokens)
    ay = links.line(a1, 1)
    u1, ux = links.line(u0, 0), links.line(u0, 1)
    own = list(attn_own(info, tokens_in, attn_w[:3], bias_own.astype(wide)[None, None]))
    ax, ay, u1, d1, own[2] = after(ax, ay, u1, d1, own[2])
    a3 = jnp.stack([a1, ax, ay])
    a4, a5 = links.plane(a3, 0), links.plane(a3, 1)
    uy = links.line(u1, 1)
    dx = links.line(d0, 1)
    a4, ux, uy, d1 = after(a4, ux, uy, d1)
    u3 = jnp.stack([u1, ux, uy])
    bias_rest = u3[:, rows:].reshape(parts - 1, 8 * width)[:, : bias_own.size]
    near, far = bias_rest[0], bias_rest[1]
    bias = jnp.stack(
        [bias_own, jnp.where(is_odd, far, near), jnp.where(is_odd, near, far), bias_rest[2]]
    )
    bias = bias.astype(wide)[:, None]
    u3 = u3[:, :rows]
    a6 = links.plane(a4, 1)
    u4, u5 = links.plane(u3, 0), links.plane(u3, 1)
    dy = links.line(d1, 1)
    a5, a6, u4, dx, dy, bias = after(a5, a6, u4, dx, dy, bias)
    d3 = jnp.stack([d1, dx, dy])
    pieces_a = mates([a3, a4, a5, a6])
    u6 = links.plane(u4, 1)
    d4, d5 = links.plane(d3, 0), links.plane(d3, 1)
    qkv, attn_rest_w, ctx, lse, out_rest = attn_rest(info, tokens, bias, pieces_a)
    skip, normed_low, hat, inv = ffn_in(tokens, own[1], ctx, vec, w_out, out_rest)
    u5, u6, d4, lse, inv = after(u5, u6, d4, lse, inv)
    pieces_u = mates([u3, u4, u5, u6])
    d6 = links.plane(d4, 1)
    act, slope, up, mark = ffn_up(info, normed_low, bias, w_up, pieces_u, inv)
    d5, d6, mark = after(d5, d6, mark)
    pieces_d = mates([d3, d4, d5, d6])
    output, grad_branch, branch_low, small, down = ffn_down(
        info, act, skip, vec, cotangent, w_down, pieces_d, mark
    )
    rest = (qkv, ctx, lse)

    def plane_a(keep, got):
        return links.plane(add(keep[1], got[1]), 0), add(keep[0], got[0])

    def plane_b(kept, got):
        return links.plane(add(kept[1], got[1]), 1), add(kept[0], got[0])

    def line_a(both):
        both = both.reshape(-1, 2, parts // 2, rows, width)
        sent = jnp.where(is_odd, both[:, :, 1], both[:, 1])
        return links.line(sent, 1), jnp.where(is_odd, both[:, :, 0], both[:, 0])

    def line_b(kept, got):
        both = add(kept, got)
        return links.line(both[:, 1], 0), both[:, 0]

    def settle(kept, got):
        total = kept.astype(wide) + got.astype(wide)
        bit = GROUP
        while bit < dp_size:
            total = total + links.bit(total, bit)
            bit *= 2
        return total.astype(low)

    keep_c, send_c, mark = down_grad(0, info, act, branch_low, mark)
    got_c = links.core(send_c)
    keep_d, send_d, mark = down_grad(2, info, act, branch_low, mark)
    got_c, send_d, mark = after(got_c, send_d, mark)
    near_c, kept_c = plane_a(keep_c, got_c)
    got_d = links.core(send_d)
    got_d, small = after(got_d, small)
    near_d, kept_d = plane_a(keep_d, got_d)
    grad_residual, residual_low, small, keep_u, send_u = ffn_back(
        info, branch_low, grad_branch, slope, normed_low, hat, inv, vec, small, up, down
    )
    near_c, near_d, send_u, small = after(near_c, near_d, send_u, small)
    got_u = links.core(send_u)
    far_d = links.plane(jnp.concatenate([add(kept_c[1], near_c[1]), add(kept_d[1], near_d[1])]), 1)
    kept_d = jnp.concatenate([add(kept_c[0], near_c[0]), add(kept_d[0], near_d[0])])
    small, joint_a, keep_a, send_a = attn_back(
        0, info, tokens, residual_low, small, w_out, own, out_rest, rest
    )
    got_u, far_d, send_a, small = after(got_u, far_d, send_a, small)
    near_u, kept_u = plane_a(keep_u, got_u)
    got_a = links.core(send_a)
    line_d, kept_d = line_a(add(kept_d, far_d))
    small, joint_b, keep_b, send_b = attn_back(
        2, info, tokens, residual_low, small, w_out, own, out_rest, rest
    )
    near_u, got_a, line_d, send_b, small, grad_residual = after(
        near_u, got_a, line_d, send_b, small, grad_residual
    )
    got_b = links.core(send_b)
    far_u, kept_u = plane_b(kept_u, near_u)
    last_d, kept_d = line_b(kept_d, line_d)
    grad_tokens = grad_tokens_of(grad_residual, joint_a, joint_b, attn_w[:3], attn_rest_w)
    small_got = links.core(small)
    got_a, got_b, far_u, last_d, grad_tokens, small_got = after(
        got_a, got_b, far_u, last_d, grad_tokens, small_got
    )
    small = small + small_got

    def joined(share, small):
        return jnp.concatenate([share.reshape(-1, width), small.astype(low)], axis=0)

    near_a, kept_a = plane_a(keep_a, got_a)
    near_b = links.plane(joined(add(keep_b[1], got_b[1]), small), 0)
    kept_b = add(keep_b[0], got_b[0])
    line_u, kept_u = line_a(add(kept_u, far_u))
    near_a, near_b, line_u = after(near_a, near_b, line_u)
    size = 4 * rows
    far_a, kept_a = plane_b(kept_a, near_a)
    small = small + near_b[size:].astype(wide)
    near_b = near_b[:size].reshape(kept_b.shape)
    size = 2 * rows
    far_b = links.plane(joined(add(kept_b[1], near_b[1]), small), 1)
    kept_b = add(kept_b[0], near_b[0])
    last_u, kept_u = line_b(kept_u, line_u)
    far_a, far_b = after(far_a, far_b)
    small = small + far_b[size:].astype(wide)
    share = jnp.concatenate([add(kept_a, far_a), add(kept_b, far_b[:size].reshape(kept_b.shape))])
    across = [links.across(joined(share[k], small), k) for k in range(parts - 1, 0, -1)]
    sum_f = jnp.stack([settle(kept_d, last_d)[0], settle(kept_u, last_u)[0]])
    f_x, f_y = links.everywhere(sum_f, (2, 4))
    across, f_y = after(across, f_y)
    sum_a = share[0].astype(wide)
    for array in across:
        sum_a = sum_a + array[:rows].astype(wide)
        small = small + array[rows:].astype(wide)
    bit = GROUP
    while bit < dp_size:
        sum_a = sum_a + links.bit(sum_a, bit)
        small = small + links.bit(small, bit)
        bit *= 2
    sum_a = sum_a.astype(low)
    around = links.everywhere(sum_a, (2, 4, 6))
    f_xy = links.plane(jnp.where(is_odd, f_x, f_y), 0)
    held = jnp.stack([sum_f, f_x, f_y])
    *early, mark = finish_ffn(info, held, links.core(held))
    pair = lax.dynamic_index_in_dim(small, 10 + me, 0, keepdims=False)
    grad_b_up = lax.dynamic_index_in_dim(small, 6 + me, 0, keepdims=False)
    around, small, pair, grad_b_up, mark = after(around, small, pair, grad_b_up, mark)
    grad_w_down, grad_w_up = finish_ffn_corner(info, f_xy, links.core(f_xy), mark, *early)
    grad_w_query, grad_w_key, grad_w_value, grad_w_out = finish_attn(info, mates([sum_a] + around))
    grad_w_query, grad_w_key, grad_w_value = grad_w_query.T, grad_w_key.T, grad_w_value.T
    return (
        output,
        grad_tokens,
        grad_w_query,
        pair[:local],
        grad_w_key,
        grad_w_value,
        pair[256 : 256 + local],
        grad_w_out,
        small[0],
        small[1],
        small[2],
        grad_w_up,
        grad_b_up,
        grad_w_down,
        small[3],
        small[4],
        small[5],
    )


def solution(mesh):
    columns, rows, both = P(None, "tensor"), P("tensor", None), P(("dp", "tensor"), None)
    share = P("tensor")
    return jax.shard_map(
        partial(per_device, mesh.shape["dp"], mesh.shape["tensor"]),
        mesh=mesh,
        in_specs=(
            both,
            P("dp"),
            columns,
            share,
            columns,
            columns,
            share,
            rows,
            P(),
            P(),
            P(),
            columns,
            share,
            rows,
            P(),
            P(),
            P(),
            both,
        ),
        out_specs=(
            both,
            both,
            columns,
            share,
            columns,
            columns,
            share,
            rows,
            P(),
            P(),
            P(),
            columns,
            share,
            rows,
            P(),
            P(),
            P(),
        ),
        check_vma=False,
    )
```
